32 devices in a mesh: gx: 16 (over z, y, core), gy: 2 (over x).
Axes of the slice: x: 2, y: 2, z: 4, core: 2. Of those that a mesh axis runs over, the one named last changes fastest.
Arguments:
- positions: float32 [3, 65536], P(None, ('gx', 'gy')), may hold values from 0 to 6
- features: bfloat16 [64, 65536], P(None, ('gx', 'gy')), may hold values from -6 to 6
- halo_lists: int32 [2, 49152], P(None, ('gx', 'gy')), may hold values from 0 to 2047
- local_pairs: int32 [4, 196608], P(None, ('gx', 'gy')), may hold values from 0 to 2047, as said below
- cross_x: int32 [4, 65536], P(None, ('gx', 'gy')), may hold values from 0 to 2047, as said below
- cross_y: int32 [4, 65536], P(None, ('gx', 'gy')), may hold values from 0 to 2047, as said below
- pair_counts: int32 [32, 3], P(('gx', 'gy')), may hold values from 256 to 6144, as said below
- w_rbf: bfloat16 [8, 256], replicated, may hold values from -2 to 2
- w_src: bfloat16 [64, 256], replicated, may hold values from -0.75 to 0.75
- w_dst: bfloat16 [64, 256], replicated, may hold values from -0.75 to 0.75
- species_src: bfloat16 [4, 256], replicated, may hold values from -3 to 3
- species_dst: bfloat16 [4, 256], replicated, may hold values from -3 to 3
- w_hidden: bfloat16 [256, 256], replicated, may hold values from -0.375 to 0.375
- w_latent: bfloat16 [256, 64], replicated, may hold values from -0.375 to 0.375
- w_energy: float32 [64], replicated, may hold values from -0.75 to 0.75
Outputs:
- energy: float32 [1], replicated
- forces: float32 [3, 65536], P(None, ('gx', 'gy'))
- feature_grads: float32 [64, 65536], P(None, ('gx', 'gy'))
The draws below stay inside these ranges and needn't reach their ends.
Inputs may be any that keep to these rules, and one draw needn't show every extreme that they name: `local_pairs`: rows 0 and 1 are different atoms of the block, below 2048; rows 2 and 3 are species below 4. `cross_x`: row 0 an atom below 2048, row 1 a slot below 1536, rows 2 and 3 species below 4. `cross_y`: row 0 an atom below 2048, row 1 a slot below 1536, rows 2 and 3 species below 4. `pair_counts`: column 0 counts live slots of local_pairs (at most 6144), columns 1 and 2 those of cross_x and cross_y (at most 2048); live slots come first; some device is full in each column.
All inputs are finite; a program needn't handle non-finite values.
Results may differ from the reference program's by a relative error of at most 0.0095.
Values may be sent and summed in bfloat16 or wider, within the bound.
No kernel may reach another device: no remote copies, remote signals or barrier semaphores. Data moves between devices by JAX's collectives and lax.ppermute only.
A program may use at most 64 MiB of HBM per device.

```python
import jax
import jax.numpy as jnp
from jax import lax

NRBF = 8
FEAT = 64
HID = 256
NSPEC = 4
BLOCK = 512
A_DEV = 2048
E_LOC = 6144
E_X = 2048
HALO = 1536
ATOMS = 65536
N_GX = 16
N_GY = 2


def draw_local_pairs(key, part):
    keys = jax.random.split(jax.random.fold_in(key, 3), 4)
    total = E_LOC * N_GX * N_GY
    source = jax.random.randint(keys[0], (total,), 0, A_DEV)
    source = source.at[0].set(A_DEV - 1)
    target = (source + jax.random.randint(keys[1], (total,), 1, A_DEV)) % A_DEV
    kind_one = jax.random.randint(keys[2], (total,), 0, NSPEC)
    kind_two = jax.random.randint(keys[3], (total,), 0, NSPEC)
    return jnp.stack([source, target, kind_one, kind_two]).astype(jnp.int32)


def cross_lists(key, salt):
    keys = jax.random.split(jax.random.fold_in(key, salt), 4)
    total = E_X * N_GX * N_GY
    source = jax.random.randint(keys[0], (total,), 0, A_DEV)
    source = source.at[0].set(A_DEV - 1)
    slots = jax.random.randint(keys[1], (total,), 0, HALO)
    kind_one = jax.random.randint(keys[2], (total,), 0, NSPEC)
    kind_two = jax.random.randint(keys[3], (total,), 0, NSPEC)
    return jnp.stack([source, slots, kind_one, kind_two]).astype(jnp.int32)


def draw_cross_x(key, part):
    return cross_lists(key, 5)


def draw_cross_y(key, part):
    return cross_lists(key, 7)


def draw_pair_counts(key, part):
    keys = jax.random.split(jax.random.fold_in(key, 9), 2)
    devices = N_GX * N_GY
    limits = jnp.array([E_LOC, E_X, E_X], jnp.int32)
    levels = jax.random.randint(keys[0], (devices, 3), 0, 4).astype(jnp.int32)
    counts = jnp.right_shift(limits[None, :], levels)
    fullest = jax.random.randint(keys[1], (3,), 0, devices)
    ranks = jnp.arange(devices, dtype=jnp.int32)[:, None]
    return jnp.where(ranks == fullest[None, :], limits[None, :], counts).astype(jnp.int32)


def set_ends(entries, rng, smallest, largest):
    dims = entries.shape
    spot = [jax.random.randint(jax.random.fold_in(rng, axis), (), 0, dims[axis]) for axis in range(len(dims))]
    entries = entries.at[tuple(spot)].set(smallest)
    longest = dims.index(max(dims))
    spot[longest] = (spot[longest] + 1) % dims[longest]
    return entries.at[tuple(spot)].set(largest)


def steps_of(key, extent, cuts, smallest, top_value):
    gain, own = 1.0, jax.random.fold_in(key, 6)
    for dim, blocks in cuts:
        steps = jnp.exp(jax.random.uniform(jax.random.fold_in(own, dim), (blocks,), jnp.float32, smallest / len(cuts), top_value / len(cuts)))
        gain = gain * jnp.repeat(steps, extent[dim] // blocks).reshape([-1 if axis == dim else 1 for axis in range(len(extent))])
    return gain


def scatter_about(own_key, dims, deviation, bound, cuts=(), kind=jnp.bfloat16):
    values = deviation * jax.random.normal(own_key, dims, jnp.float32)
    if cuts:
        values = values * steps_of(own_key, dims, cuts, -0.22, 0.18)
    return jnp.clip(values, -bound, bound).astype(kind)


def setup_inputs(seed: int = 0) -> dict:
    seeds = jax.random.split(jax.random.key(seed), 16)
    positions = jnp.clip(6.0 * jax.random.uniform(seeds[0], (3, ATOMS), jnp.float32) ** steps_of(seeds[0], (3, ATOMS), ((1, 32),), -0.2, 0.2), 0.0, 6.0)
    features = scatter_about(seeds[1], (FEAT, ATOMS), 1.0, 6.0, ((1, 32),))
    halo_lists = set_ends(jax.random.randint(seeds[2], (2, HALO * N_GX * N_GY), 0, A_DEV), jax.random.fold_in(seeds[2], 1), 0, A_DEV - 1).astype(jnp.int32)
    local_pairs = draw_local_pairs(jax.random.fold_in(seeds[15], 71), 0)
    cross_x = draw_cross_x(jax.random.fold_in(seeds[15], 71), 0)
    cross_y = draw_cross_y(jax.random.fold_in(seeds[15], 71), 0)
    pair_counts = draw_pair_counts(jax.random.fold_in(seeds[15], 71), 0)
    w_rbf = scatter_about(seeds[7], (NRBF, HID), NRBF ** -0.5, 2.0)
    w_src = scatter_about(seeds[8], (FEAT, HID), FEAT ** -0.5, 0.75)
    w_dst = scatter_about(seeds[9], (FEAT, HID), FEAT ** -0.5, 0.75)
    species_src = scatter_about(seeds[10], (NSPEC, HID), 0.5, 3.0)
    species_dst = scatter_about(seeds[11], (NSPEC, HID), 0.5, 3.0)
    w_hidden = scatter_about(seeds[12], (HID, HID), HID ** -0.5, 0.375)
    w_latent = scatter_about(seeds[13], (HID, FEAT), HID ** -0.5, 0.375)
    w_energy = scatter_about(seeds[14], (FEAT,), FEAT ** -0.5, 0.75, (), jnp.float32)
    return {"positions": positions, "features": features, "halo_lists": halo_lists, "local_pairs": local_pairs, "cross_x": cross_x, "cross_y": cross_y, "pair_counts": pair_counts, "w_rbf": w_rbf, "w_src": w_src, "w_dst": w_dst, "species_src": species_src, "species_dst": species_dst, "w_hidden": w_hidden, "w_latent": w_latent, "w_energy": w_energy}


cutoff_radius = 6.0
block_edge = 6.0
softening = 0.1

def pair_energy(src_pos, src_feat, dst_pos, dst_feat, spec_src, spec_dst, live_mask, offset, weights):
    w_rbf, w_src, w_dst, species_src, species_dst, w_hidden, w_latent, w_energy = weights
    displace = dst_pos + offset[:, None] - src_pos
    radius = jnp.sqrt(lax.optimization_barrier(jnp.sum(displace * displace, axis=0)) + softening)
    orders = jnp.arange(1, w_rbf.shape[0] + 1).astype(jnp.float32)[:, None]
    basis = (jnp.sin(orders * (jnp.pi / cutoff_radius) * radius[None, :]) / radius[None, :]).astype(jnp.bfloat16)
    kinds = jnp.arange(species_src.shape[0], dtype=jnp.int32)[:, None]
    onehot_src = (spec_src[None, :] == kinds).astype(jnp.bfloat16)
    onehot_dst = (spec_dst[None, :] == kinds).astype(jnp.bfloat16)
    pre = jnp.dot(w_rbf.T, basis, preferred_element_type=jnp.float32)
    pre = pre + jnp.dot(w_src.T, src_feat.astype(jnp.bfloat16), preferred_element_type=jnp.float32)
    pre = pre + jnp.dot(w_dst.T, dst_feat.astype(jnp.bfloat16), preferred_element_type=jnp.float32)
    pre = pre + jnp.dot(species_src.T, onehot_src, preferred_element_type=jnp.float32)
    pre = pre + jnp.dot(species_dst.T, onehot_dst, preferred_element_type=jnp.float32)
    hidden = jax.nn.silu(pre).astype(jnp.bfloat16)
    second = jax.nn.silu(jnp.dot(w_hidden.T, hidden, preferred_element_type=jnp.float32)).astype(jnp.bfloat16)
    latent = jnp.dot(w_latent.T, second, preferred_element_type=jnp.float32)
    ratio = jnp.minimum(radius / cutoff_radius, 1.0)
    envelope = (1.0 - ratio ** 2) ** 2
    scores = jnp.dot(w_energy, latent, precision=lax.Precision.HIGHEST)
    return jnp.sum(envelope * scores * live_mask)

def block_grads(src_pos, src_feat, dst_pos, dst_feat, spec_src, spec_dst, live_mask, offset, weights):

    def energy_of(pos_one, feat_one, pos_two, feat_two):
        return pair_energy(pos_one, feat_one, pos_two, feat_two, spec_src, spec_dst, live_mask, offset, weights)
    energy, pullback = jax.vjp(energy_of, src_pos, src_feat.astype(jnp.float32), dst_pos, dst_feat.astype(jnp.float32))
    return (energy, pullback(jnp.ones_like(energy)))

def to_blocks(array):
    count = array.shape[-1] // BLOCK
    if array.ndim == 1:
        return array.reshape(count, BLOCK)
    return jnp.moveaxis(array.reshape(array.shape[0], count, BLOCK), 1, 0)

def from_blocks(array):
    return jnp.moveaxis(array, 0, 1).reshape(array.shape[1], -1)

def run_edges(src_pos, src_feat, dst_pos, dst_feat, spec_src, spec_dst, live_mask, offset, weights):
    inputs = tuple((to_blocks(item) for item in (src_pos, src_feat, dst_pos, dst_feat, spec_src, spec_dst, live_mask)))

    def visit(total, blocks):
        energy, grads = block_grads(*blocks, offset, weights)
        return (total + energy, grads)
    total, grads = lax.scan(visit, jnp.zeros((), jnp.float32), inputs)
    return (total, tuple((from_blocks(item) for item in grads)))

def device_work(operands, weights):
    positions, features, local_pairs, cross_x, cross_y, counts, recv_pos_x, recv_feat_x, recv_pos_y, recv_feat_y = operands
    zero_off = jnp.zeros((3,), jnp.float32)
    off_x = jnp.array([block_edge, 0.0, 0.0], jnp.float32)
    off_y = jnp.array([0.0, block_edge, 0.0], jnp.float32)
    slots_loc = jnp.arange(local_pairs.shape[1], dtype=jnp.int32)
    slots_cross = jnp.arange(cross_x.shape[1], dtype=jnp.int32)
    live_loc = (slots_loc < counts[0]).astype(jnp.float32)
    live_x = (slots_cross < counts[1]).astype(jnp.float32)
    live_y = (slots_cross < counts[2]).astype(jnp.float32)
    source, target = (local_pairs[0], local_pairs[1])
    energy_loc, grads = run_edges(positions[:, source], features[:, source], positions[:, target], features[:, target], local_pairs[2], local_pairs[3], live_loc, zero_off, weights)
    grad_pos = jnp.zeros(positions.shape, jnp.float32).at[:, source].add(grads[0]).at[:, target].add(grads[2])
    grad_feat = jnp.zeros(features.shape, jnp.float32).at[:, source].add(grads[1]).at[:, target].add(grads[3])
    halo_size = recv_pos_x.shape[1]
    outputs = []
    energies = energy_loc
    for pairs, recv_pos, recv_feat, live_mask, offset in ((cross_x, recv_pos_x, recv_feat_x, live_x, off_x), (cross_y, recv_pos_y, recv_feat_y, live_y, off_y)):
        source, slots = (pairs[0], pairs[1])
        energy, grads = run_edges(positions[:, source], features[:, source], recv_pos[:, slots], recv_feat[:, slots], pairs[2], pairs[3], live_mask, offset, weights)
        energies = energies + energy
        grad_pos = grad_pos.at[:, source].add(grads[0])
        grad_feat = grad_feat.at[:, source].add(grads[1])
        outputs.append(jnp.zeros((3, halo_size), jnp.float32).at[:, slots].add(grads[2]))
        outputs.append(jnp.zeros((features.shape[0], halo_size), jnp.float32).at[:, slots].add(grads[3]))
    return (energies, grad_pos, grad_feat, outputs[0], outputs[1], outputs[2], outputs[3])

def reference(positions, features, halo_lists, local_pairs, cross_x, cross_y, pair_counts, w_rbf, w_src, w_dst, species_src, species_dst, w_hidden, w_latent, w_energy):
    weights = (w_rbf, w_src, w_dst, species_src, species_dst, w_hidden, w_latent, w_energy)
    devices = N_GX * N_GY

    def per_device(array, width):
        return jnp.moveaxis(array.reshape(array.shape[0], devices, width), 1, 0)

    def grid(array):
        return array.reshape((N_GX, N_GY) + array.shape[1:])

    def flat(array):
        return array.reshape((devices,) + array.shape[2:])
    pick = jax.vmap(lambda table, index: table[:, index])
    scatter = jax.vmap(lambda total, index, extra: total.at[:, index].add(extra))
    pos_dev = per_device(positions, A_DEV)
    feat_dev = per_device(features, A_DEV)
    lists_dev = per_device(halo_lists, HALO)
    local_dev = per_device(local_pairs, E_LOC)
    xdev = per_device(cross_x, E_X)
    ydev = per_device(cross_y, E_X)
    recv_pos_x = flat(jnp.roll(grid(pick(pos_dev, lists_dev[:, 0])), -1, axis=0))
    recv_feat_x = flat(jnp.roll(grid(pick(feat_dev, lists_dev[:, 0])), -1, axis=0))
    recv_pos_y = flat(jnp.roll(grid(pick(pos_dev, lists_dev[:, 1])), -1, axis=1))
    recv_feat_y = flat(jnp.roll(grid(pick(feat_dev, lists_dev[:, 1])), -1, axis=1))
    results = lax.map(lambda operands: device_work(operands, weights), (pos_dev, feat_dev, local_dev, xdev, ydev, pair_counts, recv_pos_x, recv_feat_x, recv_pos_y, recv_feat_y))
    energies, grad_pos, grad_feat, hpos_x, hfeat_x, hpos_y, hfeat_y = results
    grad_pos = scatter(grad_pos, lists_dev[:, 0], flat(jnp.roll(grid(hpos_x), 1, axis=0)))
    grad_feat = scatter(grad_feat, lists_dev[:, 0], flat(jnp.roll(grid(hfeat_x), 1, axis=0)))
    grad_pos = scatter(grad_pos, lists_dev[:, 1], flat(jnp.roll(grid(hpos_y), 1, axis=1)))
    grad_feat = scatter(grad_feat, lists_dev[:, 1], flat(jnp.roll(grid(hfeat_y), 1, axis=1)))
    forces = -jnp.moveaxis(grad_pos, 0, 1).reshape(3, ATOMS)
    feature_grads = jnp.moveaxis(grad_feat, 0, 1).reshape(features.shape[0], ATOMS)
    energy = (jnp.sum(energies) / ATOMS).reshape(1)
    return (energy, forces, feature_grads)
```

```python
import functools
import math

import jax
import jax.numpy as jnp
from jax import lax
from jax.experimental import pallas as pl
from jax.experimental.pallas import tpu as pltpu
from jax.sharding import PartitionSpec as P

BLOCK = 512
GROUPS = 4
FIRST_SHARE = 4

cutoff_radius = 6.0
block_edge = 6.0
softening = 0.1

F32 = jnp.float32
BF16 = jnp.bfloat16


def shifted(array, axis, by):
    length = lax.axis_size(axis)
    return lax.ppermute(array, axis, [(i, (i + by) % length) for i in range(length)])


def sin_cos_pi(x):
    near = jnp.floor(x + 0.5)
    y = (x - near) * math.pi
    odd = near - 2.0 * jnp.floor(near * 0.5)
    sign = 1.0 - 2.0 * odd
    z = y * y
    s = z * (-1.0 / 39916800) + 1.0 / 362880
    s = s * z - 1.0 / 5040
    s = s * z + 1.0 / 120
    s = s * z - 1.0 / 6
    s = s * z + 1.0
    c = z * (1.0 / 479001600) - 1.0 / 3628800
    c = c * z + 1.0 / 40320
    c = c * z - 1.0 / 720
    c = c * z + 1.0 / 24
    c = c * z - 0.5
    c = c * z + 1.0
    return sign * (s * y), sign * c


def group_of(index, size, groups):
    group = jnp.zeros_like(index)
    for g in range(1, groups):
        group = group + (index >= g * size).astype(jnp.int32)
    return group, index - group * size


def pick_group(stack, group, height, groups, base=0):
    out = stack[base + (groups - 1) * height : base + groups * height]
    for g in range(groups - 2, -1, -1):
        out = jnp.where(group == g, stack[base + g * height : base + (g + 1) * height], out)
    return out


def one_hot(row, size):
    spots = lax.broadcasted_iota(jnp.int32, (size, row.shape[1]), 0)
    return jnp.where(spots == row, 1.0, 0.0).astype(BF16)


def fill_table(table, wide, feat, pos):
    width = feat.shape[0]
    size = table.shape[1]
    p = pos[...]
    high = p.astype(BF16).astype(F32)
    low = p - high
    wide[...] = jnp.zeros_like(wide)
    for g in range(GROUPS):
        span = slice(g * size, (g + 1) * size)
        table[g * width : (g + 1) * width, :] = feat[:, span]
        wide[8 * g : 8 * g + 3, :] = high[:, span]
        wide[8 * g + 3 : 8 * g + 6, :] = low[:, span]
    table[GROUPS * width :, :] = wide[...].astype(BF16)


def block_work(
    indices, begin, count, offset, tab_src, tab_dst, weights, scratch, energy, width, nrbf, nspec
):
    fwd_in, fwd_hid, bwd_hid, bwd_in, readout = weights
    hots, grads, inputs = scratch
    src, dst, kind_src, kind_dst = indices
    size = tab_src.shape[1]
    lanes = src.shape[1]
    base = GROUPS * width
    grp_src, row_src = group_of(src, size, GROUPS)
    grp_dst, row_dst = group_of(dst, size, GROUPS)
    hots[:, 0:lanes] = one_hot(row_src, size)
    hots[:, lanes : 2 * lanes] = one_hot(row_dst, size)
    got_src = jnp.dot(tab_src[...], hots[:, 0:lanes], preferred_element_type=F32)
    got_dst = jnp.dot(tab_dst[...], hots[:, lanes : 2 * lanes], preferred_element_type=F32)
    inputs[0:width, :] = pick_group(got_src, grp_src, width, GROUPS).astype(BF16)
    inputs[width : 2 * width, :] = pick_group(got_dst, grp_dst, width, GROUPS).astype(BF16)
    gap = pick_group(got_dst, grp_dst, 8, GROUPS, base) - pick_group(
        got_src, grp_src, 8, GROUPS, base
    )
    sub = lax.broadcasted_iota(jnp.int32, (8, lanes), 0)
    gap = gap + pltpu.roll(gap, 5, 0)
    if offset is not None:
        gap = gap + jnp.where(sub == offset, block_edge, 0.0)
    gap = jnp.where(sub < 3, gap, 0.0)
    radius = jnp.sqrt(jnp.sum(gap * gap, axis=0, keepdims=True) + softening)
    inverse = 1.0 / radius
    ratio = jnp.minimum(radius * (1.0 / cutoff_radius), 1.0)
    inside = 1.0 - ratio * ratio
    slots = begin + lax.broadcasted_iota(jnp.int32, (1, lanes), 1)
    live = jnp.where(slots < count, 1.0, 0.0)
    weight = inside * inside * live
    orders = (sub + 1).astype(F32)
    sines, cosines = sin_cos_pi(orders * ratio)
    basis = sines * inverse
    slope = (orders * (math.pi / cutoff_radius) * cosines - basis) * inverse
    kinds = jnp.where(sub < nspec, kind_src, kind_dst + nspec)
    inputs[2 * width :, :] = jnp.concatenate(
        [basis, jnp.where(sub == kinds, 1.0, 0.0)], axis=0
    ).astype(BF16)

    half = jnp.dot(fwd_in[...], inputs[...], preferred_element_type=F32)
    tan = jnp.tanh(half)
    up = 1.0 + tan
    hidden = half * up
    slope_one = up + hidden * (1.0 - tan)
    half = jnp.dot(fwd_hid[...], hidden.astype(BF16), preferred_element_type=F32)
    tan = jnp.tanh(half)
    up = 1.0 + tan
    second = half * up
    slope_two = up + second * (1.0 - tan)
    read = readout[...]
    score = jnp.concatenate(
        [
            jnp.sum(second[:, c : c + 128] * read, axis=0, keepdims=True)
            for c in range(0, lanes, 128)
        ],
        axis=1,
    )
    energy[...] += weight * score
    back = jnp.dot(bwd_hid[...], slope_two.astype(BF16), preferred_element_type=F32)
    back = (back * slope_one).astype(BF16)
    back = jnp.dot(bwd_in[...], back, preferred_element_type=F32)
    scale = 0.25 * weight
    radial = scale * jnp.sum(back[2 * width : 2 * width + nrbf] * slope, axis=0, keepdims=True)
    radial = radial - (4.0 / cutoff_radius) * (inside * ratio * live) * score
    push = (gap * (radial * inverse)).astype(F32)
    for side, (group, part, move) in enumerate(
        (
            (grp_src, back[0:width] * scale, -push),
            (grp_dst, back[width : 2 * width] * scale, push),
        )
    ):
        span = slice(side * lanes, (side + 1) * lanes)
        part = part.astype(BF16)
        moves = []
        for g in range(GROUPS):
            mask = jnp.where(group == g, 1.0, 0.0)
            grads[g * width : (g + 1) * width, span] = part * mask.astype(BF16)
            moves.append(move * mask)
        grads[base:, span] = jnp.concatenate(moves, axis=0).astype(BF16)


def scatter(total, grads, hots, span):
    total[...] += lax.dot_general(
        grads[:, span], hots[:, span], (((1,), (1,)), ((), ())), preferred_element_type=F32
    )


def rows_of(pairs, begin):
    span = pl.ds(pl.multiple_of(begin, BLOCK), BLOCK)
    return [pairs[k : k + 1, span] for k in range(4)]


def local_kernel(
    first,
    dims,
    counts,
    pairs,
    *refs,
):
    width, nrbf, nspec = dims
    lanes = BLOCK
    if first:
        (feat, pos, w_rbf, w_src, w_dst, sp_src, sp_dst, w_hid, w_lat, w_en) = refs[:10]
        (total, energy, table, fwd_in, fwd_hid, bwd_hid, bwd_in, readout) = refs[10:18]
        hots, grads, inputs, wide, runs = refs[18:]
        fill_table(table, wide, feat, pos)
        full = jnp.concatenate(
            [ref[...].astype(F32) for ref in (w_src, w_dst, w_rbf)]
            + [jnp.concatenate([sp_src[...].astype(F32), sp_dst[...].astype(F32)], axis=0)],
            axis=0,
        )
        bwd_in[...] = full.astype(BF16)
        fwd_in[...] = (0.5 * full.T).astype(BF16)
        hid = w_hid[...].astype(F32)
        fwd_hid[...] = (0.5 * hid.T).astype(BF16)
        column = jnp.sum(w_lat[...].astype(F32) * w_en[...], axis=1, keepdims=True)
        spread = jnp.broadcast_to(column, (column.shape[0], 128))
        readout[...] = spread
        bwd_hid[...] = (hid * spread.T[0:1, :]).astype(BF16)
        total[...] = jnp.zeros_like(total)
        energy_in = None
    else:
        (total_in, energy_in, table, fwd_in, fwd_hid, bwd_hid, bwd_in, readout) = refs[:8]
        total, energy = refs[8:10]
        hots, grads, inputs, runs = refs[10:]
        total[...] = total_in[...]
    runs[...] = jnp.zeros_like(runs)
    count = counts[0, 0]
    filled = (count + BLOCK - 1) // BLOCK
    low = 0 if first else jnp.minimum(filled, FIRST_SHARE)
    high = jnp.minimum(filled, FIRST_SHARE) if first else filled
    weights = (fwd_in, fwd_hid, bwd_hid, bwd_in, readout)

    def visit(index, carry):
        begin = index * BLOCK
        block_work(
            rows_of(pairs, begin),
            begin,
            count,
            None,
            table,
            table,
            weights,
            (hots, grads, inputs),
            runs,
            width,
            nrbf,
            nspec,
        )
        scatter(total, grads, hots, slice(0, 2 * lanes))
        return carry

    lax.fori_loop(low, high, visit, 0)
    fold_energy(energy, runs, energy_in)


def fold_energy(energy, runs, energy_in):
    part = jnp.sum(runs[...], axis=1, keepdims=True)
    part = jnp.broadcast_to(part, energy.shape)
    energy[...] = part if energy_in is None else part + energy_in[...]


def cross_kernel(
    dims,
    counts,
    pairs_x,
    pairs_y,
    feat_x,
    pos_x,
    lists_x,
    feat_y,
    pos_y,
    lists_y,
    total_in,
    energy_in,
    table,
    fwd_in,
    fwd_hid,
    bwd_hid,
    bwd_in,
    readout,
    total,
    energy,
    back_x,
    back_y,
    hots,
    grads,
    inputs,
    wide,
    runs,
    other,
    away,
    lent,
):
    width, nrbf, nspec = dims
    lanes = BLOCK
    size = table.shape[1]
    parts = lists_x.shape[1] // size
    weights = (fwd_in, fwd_hid, bwd_hid, bwd_in, readout)
    total[...] = total_in[...]
    runs[...] = jnp.zeros_like(runs)
    for axis, (pairs, feat, pos, lists, back) in enumerate(
        ((pairs_x, feat_x, pos_x, lists_x, back_x), (pairs_y, feat_y, pos_y, lists_y, back_y))
    ):
        fill_table(other, wide, feat, pos)
        away[...] = jnp.zeros_like(away)
        wide[...] = jnp.zeros_like(wide)
        for g in range(parts):
            ids = lists[axis : axis + 1, g * size : (g + 1) * size]
            wide[2 * g : 2 * g + 1, :] = (ids >> 6).astype(F32)
            wide[2 * g + 1 : 2 * g + 2, :] = (ids & 63).astype(F32)
        lent[...] = wide[0 : lent.shape[0], :].astype(BF16)
        count = counts[0, 1 + axis]

        def visit(index, carry):
            begin = index * BLOCK
            src, slot, kind_src, kind_dst = rows_of(pairs, begin)
            grp, row = group_of(slot, size, parts)
            found = jnp.dot(lent[...], one_hot(row, size), preferred_element_type=F32)
            found = pick_group(found, grp, 2, parts)
            dst = (found[0:1] * 64.0 + found[1:2]).astype(jnp.int32)
            block_work(
                (src, dst, kind_src, kind_dst),
                begin,
                count,
                axis,
                table,
                other,
                weights,
                (hots, grads, inputs),
                runs,
                width,
                nrbf,
                nspec,
            )
            scatter(total, grads, hots, slice(0, lanes))
            scatter(away, grads, hots, slice(lanes, 2 * lanes))
            return carry

        lax.fori_loop(0, (count + BLOCK - 1) // BLOCK, visit, 0)
        back[...] = away[...].astype(BF16)
    fold_energy(energy, runs, energy_in)


def join_kernel(total, back_x, back_y, forces, feature_grads):
    width = feature_grads.shape[0]
    size = total.shape[1]
    base = GROUPS * width
    for g in range(GROUPS):
        span = slice(g * size, (g + 1) * size)
        rows = slice(g * width, (g + 1) * width)
        feature_grads[:, span] = total[rows] + (
            back_x[rows].astype(F32) + back_y[rows].astype(F32)
        )
    moved = total[base:] + (back_x[base:].astype(F32) + back_y[base:].astype(F32))
    for g in range(GROUPS):
        forces[:, g * size : (g + 1) * size] = -moved[8 * g : 8 * g + 3]


def on_device(
    positions,
    features,
    halo_lists,
    local_pairs,
    cross_x,
    cross_y,
    pair_counts,
    w_rbf,
    w_src,
    w_dst,
    species_src,
    species_dst,
    w_hidden,
    w_latent,
    w_energy,
):
    atoms = positions.shape[1]
    width = features.shape[0]
    nrbf, hid = w_rbf.shape
    nspec = species_src.shape[0]
    size = atoms // GROUPS
    tall = GROUPS * (width + 8)
    depth = 2 * width + nrbf + 2 * nspec
    dims = (width, nrbf, nspec)
    got = [
        [shifted(item, axis, -1) for item in (features, positions, halo_lists)]
        for axis in ("gx", "gy")
    ]
    vmem = pl.BlockSpec(memory_space=pltpu.VMEM)
    smem = pl.BlockSpec(memory_space=pltpu.SMEM)
    shape = jax.ShapeDtypeStruct
    scratch = [
        pltpu.VMEM((size, 2 * BLOCK), BF16),
        pltpu.VMEM((tall, 2 * BLOCK), BF16),
        pltpu.VMEM((depth, BLOCK), BF16),
    ]
    wide = pltpu.VMEM((GROUPS * 8, size), F32)
    runs = pltpu.VMEM((1, BLOCK), F32)
    total_like = shape((tall, size), F32)
    energy_like = shape((1, 128), F32)
    params = pltpu.CompilerParams(vmem_limit_bytes=48 * 1024 * 1024)
    prepared = (
        shape((tall, size), BF16),
        shape((hid, depth), BF16),
        shape((hid, hid), BF16),
        shape((hid, hid), BF16),
        shape((depth, hid), BF16),
        shape((hid, 128), F32),
    )
    total, energy, *shared = pl.pallas_call(
        functools.partial(local_kernel, True, dims),
        out_shape=(total_like, energy_like) + prepared,
        in_specs=[smem] + [vmem] * 11,
        out_specs=[vmem] * 8,
        scratch_shapes=scratch + [wide, runs],
        compiler_params=params,
        name="local_first",
    )(
        pair_counts,
        local_pairs,
        features,
        positions,
        w_rbf,
        w_src,
        w_dst,
        species_src,
        species_dst,
        w_hidden,
        w_latent,
        w_energy.reshape(1, -1),
    )
    total, energy, back_x, back_y = pl.pallas_call(
        functools.partial(cross_kernel, dims),
        out_shape=(total_like, energy_like, shape((tall, size), BF16), shape((tall, size), BF16)),
        in_specs=[smem] + [vmem] * 16,
        out_specs=[vmem] * 4,
        scratch_shapes=scratch
        + [
            wide,
            runs,
            pltpu.VMEM((tall, size), BF16),
            pltpu.VMEM((tall, size), F32),
            pltpu.VMEM((16, size), BF16),
        ],
        compiler_params=params,
        name="cross",
    )(pair_counts, cross_x, cross_y, *got[0], *got[1], total, energy, *shared)
    back_x = shifted(back_x, "gx", 1)
    back_y = shifted(back_y, "gy", 1)
    total, energy = pl.pallas_call(
        functools.partial(local_kernel, False, dims),
        out_shape=(total_like, energy_like),
        in_specs=[smem] + [vmem] * 9,
        out_specs=[vmem] * 2,
        scratch_shapes=scratch + [runs],
        compiler_params=params,
        name="local_rest",
    )(pair_counts, local_pairs, total, energy, *shared)
    forces, feature_grads = pl.pallas_call(
        join_kernel,
        out_shape=(shape(positions.shape, F32), shape(features.shape, F32)),
        in_specs=[vmem] * 3,
        out_specs=[vmem] * 2,
        compiler_params=params,
        name="join",
    )(total, back_x, back_y)
    summed = lax.psum(energy[0, 0], ("gx", "gy"))
    atoms_all = atoms * lax.axis_size("gx") * lax.axis_size("gy")
    return ((summed / atoms_all).reshape(1), forces, feature_grads)


def solution(mesh):
    spread = P(None, ("gx", "gy"))
    return jax.shard_map(
        on_device,
        mesh=mesh,
        in_specs=(spread,) * 6 + (P(("gx", "gy"), None),) + (P(),) * 8,
        out_specs=(P(), spread, spread),
        check_vma=False,
    )
```

```python
import functools
import math

import jax
import jax.numpy as jnp
from jax import lax
from jax.experimental import pallas as pl
from jax.experimental.pallas import tpu as pltpu
from jax.sharding import PartitionSpec as P

BLOCK = 512
GROUPS = 4
FIRST_SHARE = 4
LENT_ROWS = 16

cutoff_radius = 6.0
block_edge = 6.0
softening = 0.1

F32 = jnp.float32
BF16 = jnp.bfloat16


def shifted(array, axis, by):
    length = lax.axis_size(axis)
    return lax.ppermute(array, axis, [(i, (i + by) % length) for i in range(length)])


def sin_cos_pi(x):
    near = jnp.floor(x + 0.5)
    y = (x - near) * math.pi
    odd = near - 2.0 * jnp.floor(near * 0.5)
    sign = 1.0 - 2.0 * odd
    z = y * y
    s = z * (-1.0 / 39916800) + 1.0 / 362880
    s = s * z - 1.0 / 5040
    s = s * z + 1.0 / 120
    s = s * z - 1.0 / 6
    s = s * z + 1.0
    c = z * (1.0 / 479001600) - 1.0 / 3628800
    c = c * z + 1.0 / 40320
    c = c * z - 1.0 / 720
    c = c * z + 1.0 / 24
    c = c * z - 0.5
    c = c * z + 1.0
    return sign * (s * y), sign * c


def group_of(index, size, groups):
    group = jnp.zeros_like(index)
    for g in range(1, groups):
        group = group + (index >= g * size).astype(jnp.int32)
    return group, index - group * size


def pick_group(stack, group, height, groups, base=0):
    out = stack[base + (groups - 1) * height : base + groups * height]
    for g in range(groups - 2, -1, -1):
        out = jnp.where(group == g, stack[base + g * height : base + (g + 1) * height], out)
    return out


def one_hot(row, size):
    spots = lax.broadcasted_iota(jnp.int32, (size, row.shape[1]), 0)
    return jnp.where(spots == row, 1.0, 0.0).astype(BF16)


def fetch(sources, targets, sems):
    copies = [
        pltpu.make_async_copy(src, dst, sems.at[k])
        for k, (src, dst) in enumerate(zip(sources, targets))
    ]
    for copy in copies:
        copy.start()
    for copy in copies:
        copy.wait()


def prep_kernel(feat_in, pos_in, lists_in, send_x, send_y, feat, pos, lists, wide, sems):
    fetch((feat_in, pos_in, lists_in), (feat, pos, lists), sems)
    width = feat.shape[0]
    size = send_x.shape[1]
    base = GROUPS * width
    tall = base + 8 * GROUPS
    p = pos[...]
    high = p.astype(BF16).astype(F32)
    low = p - high
    wide[...] = jnp.zeros_like(wide)
    for g in range(GROUPS):
        span = slice(g * size, (g + 1) * size)
        rows = slice(g * width, (g + 1) * width)
        part = feat[:, span]
        send_x[rows, :] = part
        send_y[rows, :] = part
        wide[8 * g : 8 * g + 3, :] = high[:, span]
        wide[8 * g + 3 : 8 * g + 6, :] = low[:, span]
    part = wide[...].astype(BF16)
    send_x[base:tall, :] = part
    send_y[base:tall, :] = part
    for axis, send in enumerate((send_x, send_y)):
        wide[...] = jnp.zeros_like(wide)
        for g in range(lists.shape[1] // size):
            ids = lists[axis : axis + 1, g * size : (g + 1) * size]
            wide[2 * g : 2 * g + 1, :] = (ids >> 6).astype(F32)
            wide[2 * g + 1 : 2 * g + 2, :] = (ids & 63).astype(F32)
        send[tall:, :] = wide[0:LENT_ROWS, :].astype(BF16)


def block_work(
    indices, begin, count, offset, tab_src, tab_dst, weights, scratch, energy, width, nrbf, nspec
):
    fwd_in, fwd_hid, bwd_hid, bwd_in, readout = weights
    hots, grads, inputs = scratch
    src, dst, kind_src, kind_dst = indices
    size = tab_src.shape[1]
    lanes = src.shape[1]
    base = GROUPS * width
    tall = base + 8 * GROUPS
    grp_src, row_src = group_of(src, size, GROUPS)
    grp_dst, row_dst = group_of(dst, size, GROUPS)
    hots[:, 0:lanes] = one_hot(row_src, size)
    hots[:, lanes : 2 * lanes] = one_hot(row_dst, size)
    got_src = jnp.dot(tab_src[0:tall, :], hots[:, 0:lanes], preferred_element_type=F32)
    got_dst = jnp.dot(tab_dst[0:tall, :], hots[:, lanes : 2 * lanes], preferred_element_type=F32)
    inputs[0:width, :] = pick_group(got_src, grp_src, width, GROUPS).astype(BF16)
    inputs[width : 2 * width, :] = pick_group(got_dst, grp_dst, width, GROUPS).astype(BF16)
    gap = pick_group(got_dst, grp_dst, 8, GROUPS, base) - pick_group(
        got_src, grp_src, 8, GROUPS, base
    )
    sub = lax.broadcasted_iota(jnp.int32, (8, lanes), 0)
    gap = gap + pltpu.roll(gap, 5, 0)
    if offset is not None:
        gap = gap + jnp.where(sub == offset, block_edge, 0.0)
    gap = jnp.where(sub < 3, gap, 0.0)
    radius = jnp.sqrt(jnp.sum(gap * gap, axis=0, keepdims=True) + softening)
    inverse = 1.0 / radius
    ratio = jnp.minimum(radius * (1.0 / cutoff_radius), 1.0)
    inside = 1.0 - ratio * ratio
    slots = begin + lax.broadcasted_iota(jnp.int32, (1, lanes), 1)
    live = jnp.where(slots < count, 1.0, 0.0)
    weight = inside * inside * live
    orders = (sub + 1).astype(F32)
    sines, cosines = sin_cos_pi(orders * ratio)
    basis = sines * inverse
    slope = (orders * (math.pi / cutoff_radius) * cosines - basis) * inverse
    kinds = jnp.where(sub < nspec, kind_src, kind_dst + nspec)
    inputs[2 * width :, :] = jnp.concatenate(
        [basis, jnp.where(sub == kinds, 1.0, 0.0)], axis=0
    ).astype(BF16)

    half = jnp.dot(fwd_in[...], inputs[...], preferred_element_type=F32)
    tan = jnp.tanh(half)
    up = 1.0 + tan
    hidden = half * up
    slope_one = up + hidden * (1.0 - tan)
    half = jnp.dot(fwd_hid[...], hidden.astype(BF16), preferred_element_type=F32)
    tan = jnp.tanh(half)
    up = 1.0 + tan
    second = half * up
    slope_two = up + second * (1.0 - tan)
    read = readout[...]
    score = jnp.concatenate(
        [
            jnp.sum(second[:, c : c + 128] * read, axis=0, keepdims=True)
            for c in range(0, lanes, 128)
        ],
        axis=1,
    )
    energy[...] += weight * score
    back = jnp.dot(bwd_hid[...], slope_two.astype(BF16), preferred_element_type=F32)
    back = (back * slope_one).astype(BF16)
    back = jnp.dot(bwd_in[...], back, preferred_element_type=F32)
    scale = 0.25 * weight
    radial = scale * jnp.sum(back[2 * width : 2 * width + nrbf] * slope, axis=0, keepdims=True)
    radial = radial - (4.0 / cutoff_radius) * (inside * ratio * live) * score
    push = (gap * (radial * inverse)).astype(F32)
    for side, (group, part, move) in enumerate(
        (
            (grp_src, back[0:width] * scale, -push),
            (grp_dst, back[width : 2 * width] * scale, push),
        )
    ):
        span = slice(side * lanes, (side + 1) * lanes)
        part = part.astype(BF16)
        moves = []
        for g in range(GROUPS):
            mask = jnp.where(group == g, 1.0, 0.0)
            grads[g * width : (g + 1) * width, span] = part * mask.astype(BF16)
            moves.append(move * mask)
        grads[base:, span] = jnp.concatenate(moves, axis=0).astype(BF16)


def scatter(total, grads, hots, span):
    total[...] += lax.dot_general(
        grads[:, span], hots[:, span], (((1,), (1,)), ((), ())), preferred_element_type=F32
    )


def rows_of(pairs, begin):
    span = pl.ds(pl.multiple_of(begin, BLOCK), BLOCK)
    return [pairs[k : k + 1, span] for k in range(4)]


def local_kernel(first, dims, counts, pairs_in, table, *refs):
    width, nrbf, nspec = dims
    lanes = BLOCK
    if first:
        sources = refs[:8]
        (total, energy, fwd_in, fwd_hid, bwd_hid, bwd_in, readout, pairs) = refs[8:16]
        targets = refs[16:24]
        hots, grads, inputs, runs, sems = refs[24:]
        fetch((pairs_in,) + tuple(sources), (pairs,) + tuple(targets), sems)
        w_rbf, w_src, w_dst, sp_src, sp_dst, w_hid, w_lat, w_en = targets
        full = jnp.concatenate(
            [ref[...].astype(F32) for ref in (w_src, w_dst, w_rbf)]
            + [jnp.concatenate([sp_src[...].astype(F32), sp_dst[...].astype(F32)], axis=0)],
            axis=0,
        )
        bwd_in[...] = full.astype(BF16)
        fwd_in[...] = (0.5 * full.T).astype(BF16)
        hid = w_hid[...].astype(F32)
        fwd_hid[...] = (0.5 * hid.T).astype(BF16)
        column = jnp.sum(w_lat[...].astype(F32) * w_en[...], axis=1, keepdims=True)
        spread = jnp.broadcast_to(column, (column.shape[0], 128))
        readout[...] = spread
        bwd_hid[...] = (hid * spread.T[0:1, :]).astype(BF16)
        total[...] = jnp.zeros_like(total)
        energy_in = None
    else:
        (_, energy_in, fwd_in, fwd_hid, bwd_hid, bwd_in, readout) = refs[:7]
        total, energy = refs[7:9]
        hots, grads, inputs, runs = refs[9:]
        pairs = pairs_in
    runs[...] = jnp.zeros_like(runs)
    count = counts[0, 0]
    filled = (count + BLOCK - 1) // BLOCK
    low = 0 if first else jnp.minimum(filled, FIRST_SHARE)
    high = jnp.minimum(filled, FIRST_SHARE) if first else filled
    weights = (fwd_in, fwd_hid, bwd_hid, bwd_in, readout)

    def visit(index, carry):
        begin = index * BLOCK
        block_work(
            rows_of(pairs, begin),
            begin,
            count,
            None,
            table,
            table,
            weights,
            (hots, grads, inputs),
            runs,
            width,
            nrbf,
            nspec,
        )
        scatter(total, grads, hots, slice(0, 2 * lanes))
        return carry

    lax.fori_loop(low, high, visit, 0)
    fold_energy(energy, runs, energy_in)


def fold_energy(energy, runs, energy_in):
    part = jnp.sum(runs[...], axis=1, keepdims=True)
    part = jnp.broadcast_to(part, energy.shape[-2:])
    if energy_in is not None:
        part = part + energy_in[...]
    energy[...] = jnp.broadcast_to(part, energy.shape)


def cross_kernel(
    dims,
    counts,
    pairs_x,
    pairs_y,
    got_x,
    got_y,
    total_in,
    energy_in,
    table,
    fwd_in,
    fwd_hid,
    bwd_hid,
    bwd_in,
    readout,
    total,
    energy,
    back_x,
    back_y,
    hots,
    grads,
    inputs,
    runs,
    away,
):
    width, nrbf, nspec = dims
    lanes = BLOCK
    size = table.shape[1]
    tall = GROUPS * (width + 8)
    weights = (fwd_in, fwd_hid, bwd_hid, bwd_in, readout)
    runs[...] = jnp.zeros_like(runs)
    for axis, (pairs, other, back) in enumerate(
        ((pairs_x, got_x, back_x), (pairs_y, got_y, back_y))
    ):
        away[...] = jnp.zeros_like(away)
        count = counts[0, 1 + axis]

        def visit(index, carry):
            begin = index * BLOCK
            src, slot, kind_src, kind_dst = rows_of(pairs, begin)
            grp, row = group_of(slot, size, LENT_ROWS // 2)
            found = jnp.dot(other[tall:, :], one_hot(row, size), preferred_element_type=F32)
            found = pick_group(found, grp, 2, LENT_ROWS // 2)
            dst = (found[0:1] * 64.0 + found[1:2]).astype(jnp.int32)
            block_work(
                (src, dst, kind_src, kind_dst),
                begin,
                count,
                axis,
                table,
                other,
                weights,
                (hots, grads, inputs),
                runs,
                width,
                nrbf,
                nspec,
            )
            scatter(total, grads, hots, slice(0, lanes))
            scatter(away, grads, hots, slice(lanes, 2 * lanes))
            return carry

        lax.fori_loop(0, (count + BLOCK - 1) // BLOCK, visit, 0)
        back[...] = away[...].astype(BF16)
    fold_energy(energy, runs, energy_in)


def join_kernel(total, back_x, back_y, forces, feature_grads):
    width = feature_grads.shape[0]
    size = total.shape[1]
    base = GROUPS * width
    for g in range(GROUPS):
        span = slice(g * size, (g + 1) * size)
        rows = slice(g * width, (g + 1) * width)
        feature_grads[:, span] = total[rows] + (
            back_x[rows].astype(F32) + back_y[rows].astype(F32)
        )
    moved = total[base:] + (back_x[base:].astype(F32) + back_y[base:].astype(F32))
    for g in range(GROUPS):
        forces[:, g * size : (g + 1) * size] = -moved[8 * g : 8 * g + 3]


def on_device(
    positions,
    features,
    halo_lists,
    local_pairs,
    cross_x,
    cross_y,
    pair_counts,
    w_rbf,
    w_src,
    w_dst,
    species_src,
    species_dst,
    w_hidden,
    w_latent,
    w_energy,
):
    atoms = positions.shape[1]
    width = features.shape[0]
    nrbf, hid = w_rbf.shape
    nspec = species_src.shape[0]
    size = atoms // GROUPS
    tall = GROUPS * (width + 8)
    depth = 2 * width + nrbf + 2 * nspec
    dims = (width, nrbf, nspec)
    devices = lax.axis_size("gx") * lax.axis_size("gy")
    vmem = pl.BlockSpec(memory_space=pltpu.VMEM)
    smem = pl.BlockSpec(memory_space=pltpu.SMEM)
    hbm = pl.BlockSpec(memory_space=pl.ANY)
    shape = jax.ShapeDtypeStruct

    def like(*arrays):
        return [pltpu.VMEM(item.shape, item.dtype) for item in arrays]

    params = pltpu.CompilerParams(vmem_limit_bytes=48 * 1024 * 1024)
    packed = shape((tall + LENT_ROWS, size), BF16)
    send_x, send_y = pl.pallas_call(
        prep_kernel,
        out_shape=(packed, packed),
        in_specs=[hbm] * 3,
        out_specs=[vmem] * 2,
        scratch_shapes=like(features, positions, halo_lists)
        + [pltpu.VMEM((GROUPS * 8, size), F32), pltpu.SemaphoreType.DMA((3,))],
        compiler_params=params,
        name="prep",
    )(features, positions, halo_lists)
    got_x = shifted(send_x, "gx", -1)
    got_y = shifted(send_y, "gy", -1)
    scratch = [
        pltpu.VMEM((size, 2 * BLOCK), BF16),
        pltpu.VMEM((tall, 2 * BLOCK), BF16),
        pltpu.VMEM((depth, BLOCK), BF16),
        pltpu.VMEM((1, BLOCK), F32),
    ]
    total_like = shape((tall, size), F32)
    energy_like = shape((1, 128), F32)
    prepared = (
        shape((hid, depth), BF16),
        shape((hid, hid), BF16),
        shape((hid, hid), BF16),
        shape((depth, hid), BF16),
        shape((hid, 128), F32),
    )
    params_of = (
        w_rbf,
        w_src,
        w_dst,
        species_src,
        species_dst,
        w_hidden,
        w_latent,
        w_energy.reshape(1, -1),
    )
    total, energy, *shared, pairs = pl.pallas_call(
        functools.partial(local_kernel, True, dims),
        out_shape=(total_like, energy_like)
        + prepared
        + (shape(local_pairs.shape, local_pairs.dtype),),
        in_specs=[smem, hbm, vmem] + [hbm] * 8,
        out_specs=[vmem] * 8,
        scratch_shapes=like(*params_of) + scratch + [pltpu.SemaphoreType.DMA((9,))],
        compiler_params=params,
        name="local_first",
    )(pair_counts, local_pairs, send_x, *params_of)
    back_like = shape((tall, size), BF16)
    total, energy, back_x, back_y = pl.pallas_call(
        functools.partial(cross_kernel, dims),
        out_shape=(total_like, energy_like, back_like, back_like),
        in_specs=[smem] + [vmem] * 12,
        out_specs=[vmem] * 4,
        scratch_shapes=scratch + [pltpu.VMEM((tall, size), F32)],
        input_output_aliases={5: 0},
        compiler_params=params,
        name="cross",
    )(pair_counts, cross_x, cross_y, got_x, got_y, total, energy, send_x, *shared)
    back_x = shifted(back_x, "gx", 1)
    back_y = shifted(back_y, "gy", 1)
    total, energy = pl.pallas_call(
        functools.partial(local_kernel, False, dims),
        out_shape=(total_like, shape((devices, 1, 128), F32)),
        in_specs=[smem] + [vmem] * 9,
        out_specs=[vmem] * 2,
        scratch_shapes=scratch,
        input_output_aliases={3: 0},
        compiler_params=params,
        name="local_rest",
    )(pair_counts, pairs, send_x, total, energy, *shared)
    forces, feature_grads = pl.pallas_call(
        join_kernel,
        out_shape=(shape(positions.shape, F32), shape(features.shape, F32)),
        in_specs=[vmem] * 3,
        out_specs=[vmem] * 2,
        compiler_params=params,
        name="join",
    )(total, back_x, back_y)
    parts = lax.all_to_all(energy, ("gx", "gy"), 0, 0)
    summed = jnp.sum(parts[:, 0, 0])
    return ((summed / (atoms * devices)).reshape(1), forces, feature_grads)


def solution(mesh):
    spread = P(None, ("gx", "gy"))
    return jax.shard_map(
        on_device,
        mesh=mesh,
        in_specs=(spread,) * 6 + (P(("gx", "gy"), None),) + (P(),) * 8,
        out_specs=(P(), spread, spread),
        check_vma=False,
    )
```

```python
import functools
import math

import jax
import jax.numpy as jnp
from jax import lax
from jax.experimental import pallas as pl
from jax.experimental.pallas import tpu as pltpu
from jax.sharding import PartitionSpec as P

BLOCK = 1024
GROUPS = 4
FIRST_SHARE = 2
LENT_ROWS = 16

cutoff_radius = 6.0
block_edge = 6.0
softening = 0.1

F32 = jnp.float32
BF16 = jnp.bfloat16


def shifted(array, axis, by):
    length = lax.axis_size(axis)
    return lax.ppermute(array, axis, [(i, (i + by) % length) for i in range(length)])


def sin_cos_pi(x):
    near = jnp.floor(x + 0.5)
    y = (x - near) * math.pi
    odd = near - 2.0 * jnp.floor(near * 0.5)
    sign = 1.0 - 2.0 * odd
    z = y * y
    s = z * (-1.0 / 39916800) + 1.0 / 362880
    s = s * z - 1.0 / 5040
    s = s * z + 1.0 / 120
    s = s * z - 1.0 / 6
    s = s * z + 1.0
    c = z * (1.0 / 479001600) - 1.0 / 3628800
    c = c * z + 1.0 / 40320
    c = c * z - 1.0 / 720
    c = c * z + 1.0 / 24
    c = c * z - 0.5
    c = c * z + 1.0
    return sign * (s * y), sign * c


def group_of(index, size, groups):
    group = jnp.zeros_like(index)
    for g in range(1, groups):
        group = group + (index >= g * size).astype(jnp.int32)
    return group, index - group * size


def pick_group(stack, group, height, groups, base=0):
    out = stack[base + (groups - 1) * height : base + groups * height]
    for g in range(groups - 2, -1, -1):
        out = jnp.where(group == g, stack[base + g * height : base + (g + 1) * height], out)
    return out


def one_hot(row, size):
    spots = lax.broadcasted_iota(jnp.int16, (size, row.shape[1]), 0)
    hit = spots == row.astype(jnp.int16)
    return jnp.where(hit, jnp.ones((), BF16), jnp.zeros((), BF16))


def fetch(sources, targets, sems):
    copies = [
        pltpu.make_async_copy(src, dst, sems.at[k])
        for k, (src, dst) in enumerate(zip(sources, targets))
    ]
    for copy in copies:
        copy.start()
    for copy in copies:
        copy.wait()


def prep_kernel(feat_in, pos_in, lists_in, send_x, send_y, feat, pos, lists, wide, sems):
    fetch((feat_in, pos_in, lists_in), (feat, pos, lists), sems)
    width = feat.shape[0]
    size = send_x.shape[1]
    base = GROUPS * width
    tall = base + 8 * GROUPS
    p = pos[...]
    high = p.astype(BF16).astype(F32)
    low = p - high
    wide[...] = jnp.zeros_like(wide)
    for g in range(GROUPS):
        span = slice(g * size, (g + 1) * size)
        rows = slice(g * width, (g + 1) * width)
        part = feat[:, span]
        send_x[rows, :] = part
        send_y[rows, :] = part
        wide[8 * g : 8 * g + 3, :] = high[:, span]
        wide[8 * g + 3 : 8 * g + 6, :] = low[:, span]
    part = wide[...].astype(BF16)
    send_x[base:tall, :] = part
    send_y[base:tall, :] = part
    for axis, send in enumerate((send_x, send_y)):
        wide[...] = jnp.zeros_like(wide)
        for g in range(lists.shape[1] // size):
            ids = lists[axis : axis + 1, g * size : (g + 1) * size]
            wide[2 * g : 2 * g + 1, :] = (ids >> 6).astype(F32)
            wide[2 * g + 1 : 2 * g + 2, :] = (ids & 63).astype(F32)
        send[tall:, :] = wide[0:LENT_ROWS, :].astype(BF16)


def half_block(
    indices, begin, count, offset, tab_src, tab_dst, weights, scratch, energy, dims, totals, lookup
):
    width, nrbf, nspec = dims
    fwd_in, fwd_hid, bwd_hid, bwd_in, readout = weights
    hots, grads, inputs = scratch
    src, dst, kind_src, kind_dst = indices
    size = tab_src.shape[1]
    lanes = src.shape[1]
    base = GROUPS * width
    tall = base + 8 * GROUPS
    if lookup:
        groups = LENT_ROWS // 2
        grp, row = group_of(dst, size, groups)
        found = jnp.dot(tab_dst[tall:, :], one_hot(row, size), preferred_element_type=F32)
        found = pick_group(found, grp, 2, groups)
        dst = (found[0:1] * 64.0 + found[1:2]).astype(jnp.int32)
    grp_src, row_src = group_of(src, size, GROUPS)
    grp_dst, row_dst = group_of(dst, size, GROUPS)
    hots[:, 0:lanes] = one_hot(row_src, size)
    hots[:, lanes : 2 * lanes] = one_hot(row_dst, size)
    yield
    got_src = jnp.dot(tab_src[0:tall, :], hots[:, 0:lanes], preferred_element_type=F32)
    got_dst = jnp.dot(tab_dst[0:tall, :], hots[:, lanes : 2 * lanes], preferred_element_type=F32)
    inputs[0:width, :] = pick_group(got_src, grp_src, width, GROUPS).astype(BF16)
    inputs[width : 2 * width, :] = pick_group(got_dst, grp_dst, width, GROUPS).astype(BF16)
    gap = pick_group(got_dst, grp_dst, 8, GROUPS, base) - pick_group(
        got_src, grp_src, 8, GROUPS, base
    )
    sub = lax.broadcasted_iota(jnp.int32, (8, lanes), 0)
    gap = gap + pltpu.roll(gap, 5, 0)
    if offset is not None:
        gap = gap + jnp.where(sub == offset, block_edge, 0.0)
    gap = jnp.where(sub < 3, gap, 0.0)
    radius = jnp.sqrt(jnp.sum(gap * gap, axis=0, keepdims=True) + softening)
    inverse = 1.0 / radius
    ratio = jnp.minimum(radius * (1.0 / cutoff_radius), 1.0)
    inside = 1.0 - ratio * ratio
    slots = begin + lax.broadcasted_iota(jnp.int32, (1, lanes), 1)
    live = jnp.where(slots < count, 1.0, 0.0)
    weight = inside * inside * live
    orders = (sub + 1).astype(F32)
    sines, cosines = sin_cos_pi(orders * ratio)
    basis = sines * inverse
    slope = (orders * (math.pi / cutoff_radius) * cosines - basis) * inverse
    kinds = jnp.where(sub < nspec, kind_src, kind_dst + nspec)
    inputs[2 * width :, :] = jnp.concatenate(
        [basis, jnp.where(sub == kinds, 1.0, 0.0)], axis=0
    ).astype(BF16)
    yield
    half = jnp.dot(fwd_in[...], inputs[...], preferred_element_type=F32)
    tan = jnp.tanh(half)
    up = 1.0 + tan
    hidden = half * up
    slope_one = up + hidden * (1.0 - tan)
    hidden = hidden.astype(BF16)
    yield
    half = jnp.dot(fwd_hid[...], hidden, preferred_element_type=F32)
    tan = jnp.tanh(half)
    up = 1.0 + tan
    second = half * up
    slope_two = (up + second * (1.0 - tan)).astype(BF16)
    second = second.astype(BF16)
    yield
    score = jnp.dot(readout[...], second, preferred_element_type=F32)
    score = score[0:1] + score[1:2]
    energy[...] += weight * score
    back = jnp.dot(bwd_hid[...], slope_two, preferred_element_type=F32)
    back = (back * slope_one).astype(BF16)
    yield
    back = jnp.dot(bwd_in[...], back, preferred_element_type=F32)
    scale = 0.25 * weight
    radial = scale * jnp.sum(back[2 * width : 2 * width + nrbf] * slope, axis=0, keepdims=True)
    radial = radial - (4.0 / cutoff_radius) * (inside * ratio * live) * score
    push = gap * (radial * inverse)
    for side, (group, part, move) in enumerate(
        (
            (grp_src, back[0:width] * scale, -push),
            (grp_dst, back[width : 2 * width] * scale, push),
        )
    ):
        span = slice(side * lanes, (side + 1) * lanes)
        part = part.astype(BF16)
        moves = []
        for g in range(GROUPS):
            mask = jnp.where(group == g, 1.0, 0.0)
            grads[g * width : (g + 1) * width, span] = part * mask.astype(BF16)
            moves.append(move * mask)
        grads[base:, span] = jnp.concatenate(moves, axis=0).astype(BF16)
    yield
    scatter(totals, scratch)
    yield


def scatter(totals, scratch):
    hots, grads, _ = scratch
    total_src, total_dst = totals
    lanes = hots.shape[1] // 2
    spans = [(total_src, slice(0, 2 * lanes))]
    if total_dst is not total_src:
        spans = [(total_src, slice(0, lanes)), (total_dst, slice(lanes, 2 * lanes))]
    for total, span in spans:
        total[...] += lax.dot_general(
            grads[:, span], hots[:, span], (((1,), (1,)), ((), ())), preferred_element_type=F32
        )


def pair_loop(low, high, pairs, count, offset, tables, weights, scratch, energy, dims, totals, lookup):
    sets = (scratch[0:3], scratch[3:6])
    lanes = BLOCK // 2

    def visit(index, carry):
        halves = []
        for k in range(2):
            begin = index * BLOCK + k * lanes
            halves.append(
                half_block(
                    rows_of(pairs, begin, lanes),
                    begin,
                    count,
                    offset,
                    *tables,
                    weights,
                    sets[k],
                    energy,
                    dims,
                    totals,
                    lookup,
                )
            )
        for _ in zip(*halves):
            pass
        return carry

    lax.fori_loop(low, high, visit, 0)


def rows_of(pairs, begin, lanes):
    span = pl.ds(pl.multiple_of(begin, lanes), lanes)
    return [pairs[k : k + 1, span] for k in range(4)]


def units(count):
    return (count + BLOCK - 1) // BLOCK


def spare_units(counts, slots):
    return 2 * pl.cdiv(slots, BLOCK) - units(counts[0, 1]) - units(counts[0, 2])


def local_kernel(first, dims, cross_slots, counts, pairs_in, table, *refs):
    if first:
        sources = refs[:8]
        (total, energy, fwd_in, fwd_hid, bwd_hid, bwd_in, readout, pairs) = refs[8:16]
        targets = refs[16:24]
        *scratch, runs, sems = refs[24:]
        fetch((pairs_in,) + tuple(sources), (pairs,) + tuple(targets), sems)
        w_rbf, w_src, w_dst, sp_src, sp_dst, w_hid, w_lat, w_en = targets
        full = jnp.concatenate(
            [ref[...].astype(F32) for ref in (w_src, w_dst, w_rbf)]
            + [jnp.concatenate([sp_src[...].astype(F32), sp_dst[...].astype(F32)], axis=0)],
            axis=0,
        )
        bwd_in[...] = full.astype(BF16)
        fwd_in[...] = (0.5 * full.T).astype(BF16)
        hid = w_hid[...].astype(F32)
        fwd_hid[...] = (0.5 * hid.T).astype(BF16)
        column = jnp.sum(w_lat[...].astype(F32) * w_en[...], axis=1, keepdims=True)
        spread = jnp.broadcast_to(column, (column.shape[0], 128))
        line = spread.T[0:8, :]
        high = line.astype(BF16).astype(F32)
        first_row = lax.broadcasted_iota(jnp.int32, line.shape, 0) == 0
        both = jnp.where(first_row, high, line - high)
        readout[...] = jnp.concatenate([both, jnp.zeros_like(both)], axis=0).astype(BF16)
        bwd_hid[...] = (hid * line[0:1, :]).astype(BF16)
        total[...] = jnp.zeros_like(total)
        energy_in = None
    else:
        (_, energy_in, fwd_in, fwd_hid, bwd_hid, bwd_in, readout) = refs[:7]
        total, energy = refs[7:9]
        *scratch, runs = refs[9:]
        pairs = pairs_in
    runs[...] = jnp.zeros_like(runs)
    count = counts[0, 0]
    filled = units(count)
    early = jnp.minimum(filled, FIRST_SHARE)
    low = 0 if first else jnp.minimum(filled, FIRST_SHARE + spare_units(counts, cross_slots))
    high = early if first else filled
    weights = (fwd_in, fwd_hid, bwd_hid, bwd_in, readout)

    pair_loop(
        low,
        high,
        pairs,
        count,
        None,
        (table, table),
        weights,
        scratch,
        runs,
        dims,
        (total, total),
        False,
    )
    fold_energy(energy, runs, energy_in)


def fold_energy(energy, runs, energy_in):
    part = jnp.sum(runs[...], axis=1, keepdims=True)
    part = jnp.broadcast_to(part, energy.shape[-2:])
    if energy_in is not None:
        part = part + energy_in[...]
    energy[...] = jnp.broadcast_to(part, energy.shape)


def cross_kernel(
    dims,
    counts,
    pairs_x,
    pairs_y,
    pairs_own,
    got_x,
    got_y,
    total_in,
    energy_in,
    table,
    fwd_in,
    fwd_hid,
    bwd_hid,
    bwd_in,
    readout,
    total,
    energy,
    back_x,
    back_y,
    *scratch,
):
    *scratch, runs, away = scratch
    weights = (fwd_in, fwd_hid, bwd_hid, bwd_in, readout)
    runs[...] = jnp.zeros_like(runs)
    for axis, (pairs, other, back) in enumerate(
        ((pairs_x, got_x, back_x), (pairs_y, got_y, back_y))
    ):
        away[...] = jnp.zeros_like(away)
        count = counts[0, 1 + axis]
        pair_loop(
            0,
            units(count),
            pairs,
            count,
            axis,
            (table, other),
            weights,
            scratch,
            runs,
            dims,
            (total, away),
            True,
        )
        back[...] = away[...].astype(BF16)
    count = counts[0, 0]
    filled = units(count)
    pair_loop(
        jnp.minimum(filled, FIRST_SHARE),
        jnp.minimum(filled, FIRST_SHARE + spare_units(counts, pairs_x.shape[1])),
        pairs_own,
        count,
        None,
        (table, table),
        weights,
        scratch,
        runs,
        dims,
        (total, total),
        False,
    )
    fold_energy(energy, runs, energy_in)


def join_kernel(total, back_x, back_y, forces, feature_grads):
    width = feature_grads.shape[0]
    size = total.shape[1]
    base = GROUPS * width
    for g in range(GROUPS):
        span = slice(g * size, (g + 1) * size)
        rows = slice(g * width, (g + 1) * width)
        feature_grads[:, span] = total[rows] + (
            back_x[rows].astype(F32) + back_y[rows].astype(F32)
        )
    moved = total[base:] + (back_x[base:].astype(F32) + back_y[base:].astype(F32))
    for g in range(GROUPS):
        forces[:, g * size : (g + 1) * size] = -moved[8 * g : 8 * g + 3]


vmem = pl.BlockSpec(memory_space=pltpu.VMEM)
smem = pl.BlockSpec(memory_space=pltpu.SMEM)
hbm = pl.BlockSpec(memory_space=pltpu.MemorySpace.HBM)
shape = jax.ShapeDtypeStruct
params = pltpu.CompilerParams(vmem_limit_bytes=48 * 1024 * 1024)


def like(*arrays):
    return [pltpu.VMEM(item.shape, item.dtype) for item in arrays]


def scratch_of(table, depth):
    tall, size = table.shape
    tall = tall - LENT_ROWS
    lanes = BLOCK // 2
    one = [
        pltpu.VMEM((size, 2 * lanes), BF16),
        pltpu.VMEM((tall, 2 * lanes), BF16),
        pltpu.VMEM((depth, lanes), BF16),
    ]
    return one + one + [pltpu.VMEM((1, lanes), F32)]


def prep_call(features, positions, halo_lists):
    size = features.shape[1] // GROUPS
    tall = GROUPS * (features.shape[0] + 8)
    packed = shape((tall + LENT_ROWS, size), BF16)
    return pl.pallas_call(
        prep_kernel,
        out_shape=(packed, packed),
        in_specs=[hbm] * 3,
        out_specs=[vmem] * 2,
        scratch_shapes=like(features, positions, halo_lists)
        + [pltpu.VMEM((GROUPS * 8, size), F32), pltpu.SemaphoreType.DMA((3,))],
        compiler_params=params,
        name="prep",
    )(features, positions, halo_lists)


def first_call(counts, local_pairs, table, *weights):
    w_rbf, w_src, _, sp_src = weights[:4]
    nrbf, hid = w_rbf.shape
    width = w_src.shape[0]
    nspec = sp_src.shape[0]
    depth = 2 * width + nrbf + 2 * nspec
    tall, size = table.shape
    tall = tall - LENT_ROWS
    return pl.pallas_call(
        functools.partial(local_kernel, True, (width, nrbf, nspec), None),
        out_shape=(
            shape((tall, size), F32),
            shape((1, 128), F32),
            shape((hid, depth), BF16),
            shape((hid, hid), BF16),
            shape((hid, hid), BF16),
            shape((depth, hid), BF16),
            shape((16, hid), BF16),
            shape(local_pairs.shape, local_pairs.dtype),
        ),
        in_specs=[smem, hbm, vmem] + [hbm] * 8,
        out_specs=[vmem] * 8,
        scratch_shapes=like(*weights) + scratch_of(table, depth) + [pltpu.SemaphoreType.DMA((9,))],
        compiler_params=params,
        name="local_first",
    )(counts, local_pairs, table, *weights)


def on_device(
    positions,
    features,
    halo_lists,
    local_pairs,
    cross_x,
    cross_y,
    pair_counts,
    w_rbf,
    w_src,
    w_dst,
    species_src,
    species_dst,
    w_hidden,
    w_latent,
    w_energy,
):
    atoms = positions.shape[1]
    width = features.shape[0]
    nrbf, hid = w_rbf.shape
    nspec = species_src.shape[0]
    size = atoms // GROUPS
    tall = GROUPS * (width + 8)
    depth = 2 * width + nrbf + 2 * nspec
    dims = (width, nrbf, nspec)
    devices = lax.axis_size("gx") * lax.axis_size("gy")
    send_x, send_y = prep_call(features, positions, halo_lists)
    got_x = shifted(send_x, "gx", -1)
    got_y = shifted(send_y, "gy", -1)
    total, energy, *shared, pairs = first_call(
        pair_counts,
        local_pairs,
        send_x,
        w_rbf,
        w_src,
        w_dst,
        species_src,
        species_dst,
        w_hidden,
        w_latent,
        w_energy.reshape(1, -1),
    )
    scratch = scratch_of(send_x, depth)
    total_like = shape((tall, size), F32)
    back_like = shape((tall, size), BF16)
    total, energy, back_x, back_y = pl.pallas_call(
        functools.partial(cross_kernel, dims),
        out_shape=(total_like, shape((1, 128), F32), back_like, back_like),
        in_specs=[smem] + [vmem] * 13,
        out_specs=[vmem] * 4,
        scratch_shapes=scratch + [pltpu.VMEM((tall, size), F32)],
        input_output_aliases={6: 0},
        compiler_params=params,
        name="cross",
    )(pair_counts, cross_x, cross_y, pairs, got_x, got_y, total, energy, send_x, *shared)
    back_x = shifted(back_x, "gx", 1)
    back_y = shifted(back_y, "gy", 1)
    total, energy = pl.pallas_call(
        functools.partial(local_kernel, False, dims, cross_x.shape[1]),
        out_shape=(total_like, shape((devices, 1, 128), F32)),
        in_specs=[smem] + [vmem] * 9,
        out_specs=[vmem] * 2,
        scratch_shapes=scratch,
        input_output_aliases={3: 0},
        compiler_params=params,
        name="local_rest",
    )(pair_counts, pairs, send_x, total, energy, *shared)
    forces, feature_grads = pl.pallas_call(
        join_kernel,
        out_shape=(shape(positions.shape, F32), shape(features.shape, F32)),
        in_specs=[vmem] * 3,
        out_specs=[vmem] * 2,
        compiler_params=params,
        name="join",
    )(total, back_x, back_y)
    parts = lax.all_to_all(energy, ("gx", "gy"), 0, 0)
    summed = jnp.sum(parts[:, 0, 0])
    return ((summed / (atoms * devices)).reshape(1), forces, feature_grads)


def solution(mesh):
    spread = P(None, ("gx", "gy"))
    return jax.shard_map(
        on_device,
        mesh=mesh,
        in_specs=(spread,) * 6 + (P(("gx", "gy"), None),) + (P(),) * 8,
        out_specs=(P(), spread, spread),
        check_vma=False,
    )
```

```python
import functools
import math

import jax
import jax.numpy as jnp
from jax import lax
from jax.experimental import pallas as pl
from jax.experimental.pallas import tpu as pltpu
from jax.sharding import PartitionSpec as P

BLOCK = 1024
STREAMS = 4
OFFSETS = (0, 0, 0, 0)
GROUPS = 4
FIRST_SHARE = 3
LENT_ROWS = 16

cutoff_radius = 6.0
block_edge = 6.0
softening = 0.1

F32 = jnp.float32
BF16 = jnp.bfloat16


def shifted(array, axis, by):
    length = lax.axis_size(axis)
    return lax.ppermute(array, axis, [(i, (i + by) % length) for i in range(length)])


def sin_cos_pi(x):
    near = jnp.floor(x + 0.5)
    y = (x - near) * math.pi
    odd = near - 2.0 * jnp.floor(near * 0.5)
    sign = 1.0 - 2.0 * odd
    z = y * y
    s = z * (-1.0 / 39916800) + 1.0 / 362880
    s = s * z - 1.0 / 5040
    s = s * z + 1.0 / 120
    s = s * z - 1.0 / 6
    s = s * z + 1.0
    c = z * (1.0 / 479001600) - 1.0 / 3628800
    c = c * z + 1.0 / 40320
    c = c * z - 1.0 / 720
    c = c * z + 1.0 / 24
    c = c * z - 0.5
    c = c * z + 1.0
    return sign * (s * y), sign * c


def group_of(index, size, groups):
    group = jnp.zeros_like(index)
    for g in range(1, groups):
        group = group + (index >= g * size).astype(jnp.int32)
    return group, index - group * size


def pick_group(stack, group, height, groups, base=0):
    out = stack[base + (groups - 1) * height : base + groups * height]
    for g in range(groups - 2, -1, -1):
        out = jnp.where(group == g, stack[base + g * height : base + (g + 1) * height], out)
    return out


def one_hot(row, size):
    spots = lax.broadcasted_iota(jnp.int16, (size, row.shape[1]), 0)
    hit = spots == row.astype(jnp.int16)
    return jnp.where(hit, jnp.ones((), BF16), jnp.zeros((), BF16))


def fetch(sources, targets, sems):
    copies = [
        pltpu.make_async_copy(src, dst, sems.at[k])
        for k, (src, dst) in enumerate(zip(sources, targets))
    ]
    for copy in copies:
        copy.start()
    for copy in copies:
        copy.wait()


def prep_kernel(feat_in, pos_in, lists_in, send_x, send_y, feat, pos, lists, wide, sems):
    fetch((feat_in, pos_in, lists_in), (feat, pos, lists), sems)
    width = feat.shape[0]
    size = send_x.shape[1]
    base = GROUPS * width
    tall = base + 8 * GROUPS
    p = pos[...]
    high = p.astype(BF16).astype(F32)
    low = p - high
    wide[...] = jnp.zeros_like(wide)
    for g in range(GROUPS):
        span = slice(g * size, (g + 1) * size)
        rows = slice(g * width, (g + 1) * width)
        part = feat[:, span]
        send_x[rows, :] = part
        send_y[rows, :] = part
        wide[8 * g : 8 * g + 3, :] = high[:, span]
        wide[8 * g + 3 : 8 * g + 6, :] = low[:, span]
    part = wide[...].astype(BF16)
    send_x[base:tall, :] = part
    send_y[base:tall, :] = part
    for axis, send in enumerate((send_x, send_y)):
        wide[...] = jnp.zeros_like(wide)
        for g in range(lists.shape[1] // size):
            ids = lists[axis : axis + 1, g * size : (g + 1) * size]
            wide[2 * g : 2 * g + 1, :] = (ids >> 6).astype(F32)
            wide[2 * g + 1 : 2 * g + 2, :] = (ids & 63).astype(F32)
        send[tall:, :] = wide[0:LENT_ROWS, :].astype(BF16)


def half_block(
    indices, begin, count, offset, tab_src, tab_dst, weights, scratch, energy, dims, lookup
):
    width, nrbf, nspec = dims
    fwd_in, fwd_hid, bwd_hid, bwd_in, readout = weights
    hots, grads, inputs, place = scratch
    src, dst, kind_src, kind_dst = indices
    size = tab_src.shape[1]
    lanes = src.shape[1]
    here = slice(place * lanes, (place + 1) * lanes)
    there = slice(BLOCK + place * lanes, BLOCK + (place + 1) * lanes)
    base = GROUPS * width
    tall = base + 8 * GROUPS
    if lookup:
        groups = LENT_ROWS // 2
        grp, row = group_of(dst, size, groups)
        found = jnp.dot(tab_dst[tall:, :], one_hot(row, size), preferred_element_type=F32)
        found = pick_group(found, grp, 2, groups)
        dst = (found[0:1] * 64.0 + found[1:2]).astype(jnp.int32)
    grp_src, row_src = group_of(src, size, GROUPS)
    grp_dst, row_dst = group_of(dst, size, GROUPS)
    hots[:, here] = one_hot(row_src, size)
    hots[:, there] = one_hot(row_dst, size)
    yield
    got_src = jnp.dot(tab_src[0:tall, :], hots[:, here], preferred_element_type=F32)
    got_dst = jnp.dot(tab_dst[0:tall, :], hots[:, there], preferred_element_type=F32)
    inputs[0:width, :] = pick_group(got_src, grp_src, width, GROUPS).astype(BF16)
    inputs[width : 2 * width, :] = pick_group(got_dst, grp_dst, width, GROUPS).astype(BF16)
    gap = pick_group(got_dst, grp_dst, 8, GROUPS, base) - pick_group(
        got_src, grp_src, 8, GROUPS, base
    )
    sub = lax.broadcasted_iota(jnp.int32, (8, lanes), 0)
    gap = gap + pltpu.roll(gap, 5, 0)
    if offset is not None:
        gap = gap + jnp.where(sub == offset, block_edge, 0.0)
    gap = jnp.where(sub < 3, gap, 0.0)
    radius = jnp.sqrt(jnp.sum(gap * gap, axis=0, keepdims=True) + softening)
    inverse = 1.0 / radius
    ratio = jnp.minimum(radius * (1.0 / cutoff_radius), 1.0)
    inside = 1.0 - ratio * ratio
    slots = begin + lax.broadcasted_iota(jnp.int32, (1, lanes), 1)
    live = jnp.where(slots < count, 1.0, 0.0)
    weight = inside * inside * live
    orders = (sub + 1).astype(F32)
    sines, cosines = sin_cos_pi(orders * ratio)
    basis = sines * inverse
    slope = (orders * (math.pi / cutoff_radius) * cosines - basis) * inverse
    kinds = jnp.where(sub < nspec, kind_src, kind_dst + nspec)
    inputs[2 * width :, :] = jnp.concatenate(
        [basis, jnp.where(sub == kinds, 1.0, 0.0)], axis=0
    ).astype(BF16)
    yield
    half = jnp.dot(fwd_in[...], inputs[...], preferred_element_type=F32)
    tan = jnp.tanh(half)
    up = 1.0 + tan
    hidden = half * up
    slope_one = up + hidden * (1.0 - tan)
    hidden = hidden.astype(BF16)
    yield
    half = jnp.dot(fwd_hid[...], hidden, preferred_element_type=F32)
    tan = jnp.tanh(half)
    up = 1.0 + tan
    second = half * up
    slope_two = (up + second * (1.0 - tan)).astype(BF16)
    second = second.astype(BF16)
    yield
    score = jnp.dot(readout[...], second, preferred_element_type=F32)
    score = score[0:1] + score[1:2]
    energy[...] += weight * score
    back = jnp.dot(bwd_hid[...], slope_two, preferred_element_type=F32)
    back = (back * slope_one).astype(BF16)
    yield
    back = jnp.dot(bwd_in[...], back, preferred_element_type=F32)
    scale = 0.25 * weight
    radial = scale * jnp.sum(back[2 * width : 2 * width + nrbf] * slope, axis=0, keepdims=True)
    radial = radial - (4.0 / cutoff_radius) * (inside * ratio * live) * score
    push = gap * (radial * inverse)
    for span, group, part, move in (
        (here, grp_src, back[0:width] * scale, -push),
        (there, grp_dst, back[width : 2 * width] * scale, push),
    ):
        part = part.astype(BF16)
        moves = []
        for g in range(GROUPS):
            mask = jnp.where(group == g, 1.0, 0.0)
            grads[g * width : (g + 1) * width, span] = part * mask.astype(BF16)
            moves.append(move * mask)
        grads[base:, span] = jnp.concatenate(moves, axis=0).astype(BF16)
    yield


def scatter(totals, scratch):
    hots, grads = scratch
    total_src, total_dst = totals
    spans = [(total_src, slice(0, 2 * BLOCK))]
    if total_dst is not total_src:
        spans = [(total_src, slice(0, BLOCK)), (total_dst, slice(BLOCK, 2 * BLOCK))]
    for total, span in spans:
        total[...] += lax.dot_general(
            grads[:, span], hots[:, span], (((1,), (1,)), ((), ())), preferred_element_type=F32
        )


def pair_loop(low, high, pairs, count, offset, tables, weights, scratch, energy, dims, totals, lookup):
    hots, grads, *inputs = scratch
    lanes = BLOCK // STREAMS

    def visit(index, carry):
        halves = []
        for k in range(STREAMS):
            begin = index * BLOCK + k * lanes
            halves.append(
                half_block(
                    rows_of(pairs, begin, lanes),
                    begin,
                    count,
                    offset,
                    *tables,
                    weights,
                    (hots, grads, inputs[k], k),
                    energy,
                    dims,
                    lookup,
                )
            )
        for tick in range(6 + max(OFFSETS)):
            for half, late in zip(halves, OFFSETS):
                if 0 <= tick - late < 6:
                    next(half)
        scatter(totals, (hots, grads))
        return carry

    lax.fori_loop(low, high, visit, 0)


def rows_of(pairs, begin, lanes):
    span = pl.ds(pl.multiple_of(begin, lanes), lanes)
    return [pairs[k : k + 1, span] for k in range(4)]


def units(count):
    return (count + BLOCK - 1) // BLOCK


def spare_units(counts, slots):
    return 2 * pl.cdiv(slots, BLOCK) - units(counts[0, 1]) - units(counts[0, 2])


def local_kernel(first, dims, cross_slots, counts, pairs_in, table, *refs):
    if first:
        sources = refs[:8]
        (total, energy, fwd_in, fwd_hid, bwd_hid, bwd_in, readout, pairs) = refs[8:16]
        targets = refs[16:24]
        *scratch, runs, sems = refs[24:]
        fetch((pairs_in,) + tuple(sources), (pairs,) + tuple(targets), sems)
        w_rbf, w_src, w_dst, sp_src, sp_dst, w_hid, w_lat, w_en = targets
        full = jnp.concatenate(
            [ref[...].astype(F32) for ref in (w_src, w_dst, w_rbf)]
            + [jnp.concatenate([sp_src[...].astype(F32), sp_dst[...].astype(F32)], axis=0)],
            axis=0,
        )
        bwd_in[...] = full.astype(BF16)
        fwd_in[...] = (0.5 * full.T).astype(BF16)
        hid = w_hid[...].astype(F32)
        fwd_hid[...] = (0.5 * hid.T).astype(BF16)
        column = jnp.sum(w_lat[...].astype(F32) * w_en[...], axis=1, keepdims=True)
        spread = jnp.broadcast_to(column, (column.shape[0], 128))
        line = spread.T[0:8, :]
        high = line.astype(BF16).astype(F32)
        first_row = lax.broadcasted_iota(jnp.int32, line.shape, 0) == 0
        both = jnp.where(first_row, high, line - high)
        readout[...] = jnp.concatenate([both, jnp.zeros_like(both)], axis=0).astype(BF16)
        bwd_hid[...] = (hid * line[0:1, :]).astype(BF16)
        total[...] = jnp.zeros_like(total)
        energy_in = None
    else:
        (_, energy_in, fwd_in, fwd_hid, bwd_hid, bwd_in, readout) = refs[:7]
        total, energy = refs[7:9]
        *scratch, runs = refs[9:]
        pairs = pairs_in
    runs[...] = jnp.zeros_like(runs)
    count = counts[0, 0]
    filled = units(count)
    early = jnp.minimum(filled, FIRST_SHARE)
    low = 0 if first else jnp.minimum(filled, FIRST_SHARE + spare_units(counts, cross_slots))
    high = early if first else filled
    weights = (fwd_in, fwd_hid, bwd_hid, bwd_in, readout)

    pair_loop(
        low,
        high,
        pairs,
        count,
        None,
        (table, table),
        weights,
        scratch,
        runs,
        dims,
        (total, total),
        False,
    )
    fold_energy(energy, runs, energy_in)


def fold_energy(energy, runs, energy_in):
    part = jnp.sum(runs[...], axis=1, keepdims=True)
    part = jnp.broadcast_to(part, energy.shape[-2:])
    if energy_in is not None:
        part = part + energy_in[...]
    energy[...] = jnp.broadcast_to(part, energy.shape)


def cross_kernel(
    dims,
    counts,
    pairs_x,
    pairs_y,
    pairs_own,
    got_x,
    got_y,
    total_in,
    energy_in,
    table,
    fwd_in,
    fwd_hid,
    bwd_hid,
    bwd_in,
    readout,
    total,
    energy,
    back_x,
    back_y,
    *scratch,
):
    *scratch, runs, away = scratch
    weights = (fwd_in, fwd_hid, bwd_hid, bwd_in, readout)
    runs[...] = jnp.zeros_like(runs)
    for axis, (pairs, other, back) in enumerate(
        ((pairs_x, got_x, back_x), (pairs_y, got_y, back_y))
    ):
        away[...] = jnp.zeros_like(away)
        count = counts[0, 1 + axis]
        pair_loop(
            0,
            units(count),
            pairs,
            count,
            axis,
            (table, other),
            weights,
            scratch,
            runs,
            dims,
            (total, away),
            True,
        )
        back[...] = away[...].astype(BF16)
    count = counts[0, 0]
    filled = units(count)
    pair_loop(
        jnp.minimum(filled, FIRST_SHARE),
        jnp.minimum(filled, FIRST_SHARE + spare_units(counts, pairs_x.shape[1])),
        pairs_own,
        count,
        None,
        (table, table),
        weights,
        scratch,
        runs,
        dims,
        (total, total),
        False,
    )
    fold_energy(energy, runs, energy_in)


def join_kernel(atoms, total, back_x, back_y, parts, energy, forces, feature_grads):
    energy[0] = jnp.sum(parts[:, 0:1, 0:1]) / atoms
    width = feature_grads.shape[0]
    size = total.shape[1]
    base = GROUPS * width
    for g in range(GROUPS):
        span = slice(g * size, (g + 1) * size)
        rows = slice(g * width, (g + 1) * width)
        feature_grads[:, span] = total[rows] + (
            back_x[rows].astype(F32) + back_y[rows].astype(F32)
        )
    moved = total[base:] + (back_x[base:].astype(F32) + back_y[base:].astype(F32))
    for g in range(GROUPS):
        forces[:, g * size : (g + 1) * size] = -moved[8 * g : 8 * g + 3]


vmem = pl.BlockSpec(memory_space=pltpu.VMEM)
smem = pl.BlockSpec(memory_space=pltpu.SMEM)
hbm = pl.BlockSpec(memory_space=pltpu.MemorySpace.HBM)
shape = jax.ShapeDtypeStruct
params = pltpu.CompilerParams(vmem_limit_bytes=48 * 1024 * 1024)


def in_hbm(array):
    return pltpu.with_memory_space_constraint(array, pltpu.MemorySpace.HBM)


def like(*arrays):
    return [pltpu.VMEM(item.shape, item.dtype) for item in arrays]


def scratch_of(table, depth):
    tall, size = table.shape
    tall = tall - LENT_ROWS
    lanes = BLOCK // STREAMS
    return (
        [pltpu.VMEM((size, 2 * BLOCK), BF16), pltpu.VMEM((tall, 2 * BLOCK), BF16)]
        + [pltpu.VMEM((depth, lanes), BF16)] * STREAMS
        + [pltpu.VMEM((1, lanes), F32)]
    )


def prep_call(features, positions, halo_lists):
    size = features.shape[1] // GROUPS
    tall = GROUPS * (features.shape[0] + 8)
    packed = shape((tall + LENT_ROWS, size), BF16)
    return pl.pallas_call(
        prep_kernel,
        out_shape=(packed, packed),
        in_specs=[hbm] * 3,
        out_specs=[vmem] * 2,
        scratch_shapes=like(features, positions, halo_lists)
        + [pltpu.VMEM((GROUPS * 8, size), F32), pltpu.SemaphoreType.DMA((3,))],
        compiler_params=params,
        name="prep",
    )(*[in_hbm(item) for item in (features, positions, halo_lists)])


def first_call(counts, local_pairs, table, *weights):
    w_rbf, w_src, _, sp_src = weights[:4]
    nrbf, hid = w_rbf.shape
    width = w_src.shape[0]
    nspec = sp_src.shape[0]
    depth = 2 * width + nrbf + 2 * nspec
    tall, size = table.shape
    tall = tall - LENT_ROWS
    return pl.pallas_call(
        functools.partial(local_kernel, True, (width, nrbf, nspec), None),
        out_shape=(
            shape((tall, size), F32),
            shape((1, 128), F32),
            shape((hid, depth), BF16),
            shape((hid, hid), BF16),
            shape((hid, hid), BF16),
            shape((depth, hid), BF16),
            shape((16, hid), BF16),
            shape(local_pairs.shape, local_pairs.dtype),
        ),
        in_specs=[smem, hbm, vmem] + [hbm] * 8,
        out_specs=[vmem] * 8,
        scratch_shapes=like(*weights) + scratch_of(table, depth) + [pltpu.SemaphoreType.DMA((9,))],
        compiler_params=params,
        name="local_first",
    )(counts, local_pairs, table, *weights)


def on_device(
    positions,
    features,
    halo_lists,
    local_pairs,
    cross_x,
    cross_y,
    pair_counts,
    w_rbf,
    w_src,
    w_dst,
    species_src,
    species_dst,
    w_hidden,
    w_latent,
    w_energy,
):
    atoms = positions.shape[1]
    width = features.shape[0]
    nrbf, hid = w_rbf.shape
    nspec = species_src.shape[0]
    size = atoms // GROUPS
    tall = GROUPS * (width + 8)
    depth = 2 * width + nrbf + 2 * nspec
    dims = (width, nrbf, nspec)
    devices = lax.axis_size("gx") * lax.axis_size("gy")
    send_x, send_y = prep_call(features, positions, halo_lists)
    got_x = shifted(send_x, "gx", -1)
    got_y = shifted(send_y, "gy", -1)
    total, energy, *shared, pairs = first_call(
        pair_counts,
        local_pairs,
        send_x,
        w_rbf,
        w_src,
        w_dst,
        species_src,
        species_dst,
        w_hidden,
        w_latent,
        w_energy.reshape(1, -1),
    )
    scratch = scratch_of(send_x, depth)
    total_like = shape((tall, size), F32)
    back_like = shape((tall, size), BF16)
    total, energy, back_x, back_y = pl.pallas_call(
        functools.partial(cross_kernel, dims),
        out_shape=(total_like, shape((1, 128), F32), back_like, back_like),
        in_specs=[smem] + [vmem] * 13,
        out_specs=[vmem] * 4,
        scratch_shapes=scratch + [pltpu.VMEM((tall, size), F32)],
        input_output_aliases={6: 0},
        compiler_params=params,
        name="cross",
    )(pair_counts, cross_x, cross_y, pairs, got_x, got_y, total, energy, send_x, *shared)
    back_x = shifted(back_x, "gx", 1)
    back_y = shifted(back_y, "gy", 1)
    total, energy = pl.pallas_call(
        functools.partial(local_kernel, False, dims, cross_x.shape[1]),
        out_shape=(total_like, shape((devices, 1, 128), F32)),
        in_specs=[smem] + [vmem] * 9,
        out_specs=[vmem] * 2,
        scratch_shapes=scratch,
        input_output_aliases={3: 0},
        compiler_params=params,
        name="local_rest",
    )(pair_counts, pairs, send_x, total, energy, *shared)
    parts = lax.all_to_all(energy, ("gx", "gy"), 0, 0)
    return pl.pallas_call(
        functools.partial(join_kernel, atoms * devices),
        out_shape=(shape((1,), F32), shape(positions.shape, F32), shape(features.shape, F32)),
        in_specs=[vmem] * 4,
        out_specs=[smem, vmem, vmem],
        compiler_params=params,
        name="join",
    )(total, back_x, back_y, parts)


def solution(mesh):
    spread = P(None, ("gx", "gy"))
    return jax.shard_map(
        on_device,
        mesh=mesh,
        in_specs=(spread,) * 6 + (P(("gx", "gy"), None),) + (P(),) * 8,
        out_specs=(P(), spread, spread),
        check_vma=False,
    )
```

```python
import functools
import math

import jax
import jax.numpy as jnp
from jax import lax
from jax.experimental import pallas as pl
from jax.experimental.pallas import tpu as pltpu
from jax.sharding import PartitionSpec as P

BLOCK = 1024
STREAMS = 4
OFFSETS = (0, 0, 0, 0)
GROUPS = 4
FIRST_SHARE = 3
LENT_ROWS = 16

cutoff_radius = 6.0
block_edge = 6.0
softening = 0.1

F32 = jnp.float32
BF16 = jnp.bfloat16


def shifted(array, axis, by):
    length = lax.axis_size(axis)
    return lax.ppermute(array, axis, [(i, (i + by) % length) for i in range(length)])


def sin_cos_pi(x):
    near = jnp.floor(x + 0.5)
    y = (x - near) * math.pi
    odd = near - 2.0 * jnp.floor(near * 0.5)
    sign = 1.0 - 2.0 * odd
    z = y * y
    s = z * (-1.0 / 39916800) + 1.0 / 362880
    s = s * z - 1.0 / 5040
    s = s * z + 1.0 / 120
    s = s * z - 1.0 / 6
    s = s * z + 1.0
    c = z * (1.0 / 479001600) - 1.0 / 3628800
    c = c * z + 1.0 / 40320
    c = c * z - 1.0 / 720
    c = c * z + 1.0 / 24
    c = c * z - 0.5
    c = c * z + 1.0
    return sign * (s * y), sign * c


def group_of(index, size, groups):
    group = jnp.zeros_like(index)
    for g in range(1, groups):
        group = group + (index >= g * size).astype(jnp.int32)
    return group, index - group * size


def pick_group(stack, group, height, groups, base=0):
    out = stack[base + (groups - 1) * height : base + groups * height]
    for g in range(groups - 2, -1, -1):
        out = jnp.where(group == g, stack[base + g * height : base + (g + 1) * height], out)
    return out


def pick_lanes(table, index):
    out = []
    for c in range(0, index.shape[1], 128):
        spots = jnp.broadcast_to(index[:, c : c + 128], (8, 128))
        chunk = spots >> 7
        lane = spots & 127
        best = jnp.zeros((8, 128), F32)
        for j in range(table.shape[1] // 128):
            found = jnp.take_along_axis(
                table[:, j * 128 : (j + 1) * 128], lane, axis=1, mode="promise_in_bounds"
            )
            best = jnp.where(chunk == j, found, best)
        out.append(best)
    return jnp.concatenate(out, axis=1)


def one_hot(row, size):
    spots = lax.broadcasted_iota(jnp.int16, (size, row.shape[1]), 0)
    hit = spots == row.astype(jnp.int16)
    return jnp.where(hit, jnp.ones((), BF16), jnp.zeros((), BF16))


def prep_kernel(*refs):
    sources, refs = refs[:12], refs[12:]
    (send_x, send_y, places, fwd_in, fwd_hid, bwd_hid, bwd_in, readout, pairs), refs = (
        refs[:9],
        refs[9:],
    )
    targets, (wide, sems) = refs[:11], refs[11:]
    copies = [
        pltpu.make_async_copy(src, dst, sems.at[k])
        for k, (src, dst) in enumerate(zip(sources, targets + (pairs,)))
    ]
    for copy in copies:
        copy.start()
    for copy in copies[:3]:
        copy.wait()
    feat, pos, lists, w_rbf, w_src, w_dst, sp_src, sp_dst, w_hid, w_lat, w_en = targets
    width = feat.shape[0]
    size = send_x.shape[1]
    base = GROUPS * width
    tall = base + 8 * GROUPS
    p = pos[...]
    high = p.astype(BF16).astype(F32)
    low = p - high
    places[...] = jnp.zeros_like(places)
    places[0:3, :] = p
    wide[...] = jnp.zeros_like(wide)
    for g in range(GROUPS):
        span = slice(g * size, (g + 1) * size)
        rows = slice(g * width, (g + 1) * width)
        part = feat[:, span]
        send_x[rows, :] = part
        send_y[rows, :] = part
        wide[8 * g : 8 * g + 3, :] = high[:, span]
        wide[8 * g + 3 : 8 * g + 6, :] = low[:, span]
    part = wide[...].astype(BF16)
    send_x[base:tall, :] = part
    send_y[base:tall, :] = part
    for axis, send in enumerate((send_x, send_y)):
        wide[...] = jnp.zeros_like(wide)
        for g in range(lists.shape[1] // size):
            ids = lists[axis : axis + 1, g * size : (g + 1) * size]
            wide[2 * g : 2 * g + 1, :] = (ids >> 6).astype(F32)
            wide[2 * g + 1 : 2 * g + 2, :] = (ids & 63).astype(F32)
        send[tall:, :] = wide[0:LENT_ROWS, :].astype(BF16)
    for copy in copies[3:]:
        copy.wait()
    full = jnp.concatenate(
        [ref[...].astype(F32) for ref in (w_src, w_dst, w_rbf)]
        + [jnp.concatenate([sp_src[...].astype(F32), sp_dst[...].astype(F32)], axis=0)],
        axis=0,
    )
    bwd_in[...] = full.astype(BF16)
    fwd_in[...] = (0.5 * full.T).astype(BF16)
    hid = w_hid[...].astype(F32)
    fwd_hid[...] = (0.5 * hid.T).astype(BF16)
    column = jnp.sum(w_lat[...].astype(F32) * w_en[...], axis=1, keepdims=True)
    line = jnp.broadcast_to(column, (column.shape[0], 128)).T[0:8, :]
    high = line.astype(BF16).astype(F32)
    first_row = lax.broadcasted_iota(jnp.int32, line.shape, 0) == 0
    both = jnp.where(first_row, high, line - high)
    readout[...] = jnp.concatenate([both, jnp.zeros_like(both)], axis=0).astype(BF16)
    bwd_hid[...] = (hid * line[0:1, :]).astype(BF16)


def half_block(
    indices, begin, count, offset, tables, weights, scratch, energy, dims, lookup
):
    width, nrbf, nspec = dims
    fwd_in, fwd_hid, bwd_hid, bwd_in, readout = weights
    hots, grads, inputs, place = scratch
    src, dst, kind_src, kind_dst = indices
    tab_src, tab_dst, pos_src, pos_dst = tables
    size = tab_src.shape[1]
    lanes = src.shape[1]
    here = slice(place * lanes, (place + 1) * lanes)
    there = slice(BLOCK + place * lanes, BLOCK + (place + 1) * lanes)
    base = GROUPS * width
    if lookup is not None:
        dst = pick_lanes(lookup, dst)[0:1].astype(jnp.int32)
    grp_src, row_src = group_of(src, size, GROUPS)
    grp_dst, row_dst = group_of(dst, size, GROUPS)
    hots[:, here] = one_hot(row_src, size)
    hots[:, there] = one_hot(row_dst, size)
    yield
    got_src = jnp.dot(tab_src[0:base, :], hots[:, here], preferred_element_type=F32)
    got_dst = jnp.dot(tab_dst[0:base, :], hots[:, there], preferred_element_type=F32)
    inputs[0:width, :] = pick_group(got_src, grp_src, width, GROUPS).astype(BF16)
    inputs[width : 2 * width, :] = pick_group(got_dst, grp_dst, width, GROUPS).astype(BF16)
    sub = lax.broadcasted_iota(jnp.int32, (8, lanes), 0)
    gap = pick_lanes(pos_dst, dst) - pick_lanes(pos_src, src)
    if offset is not None:
        gap = gap + jnp.where(sub == offset, block_edge, 0.0)
    radius = jnp.sqrt(jnp.sum(gap * gap, axis=0, keepdims=True) + softening)
    inverse = 1.0 / radius
    ratio = jnp.minimum(radius * (1.0 / cutoff_radius), 1.0)
    inside = 1.0 - ratio * ratio
    slots = begin + lax.broadcasted_iota(jnp.int32, (1, lanes), 1)
    live = jnp.where(slots < count, 1.0, 0.0)
    weight = inside * inside * live
    orders = (sub + 1).astype(F32)
    sines, cosines = sin_cos_pi(orders * ratio)
    basis = sines * inverse
    slope = (orders * (math.pi / cutoff_radius) * cosines - basis) * inverse
    kinds = jnp.where(sub < nspec, kind_src, kind_dst + nspec)
    inputs[2 * width :, :] = jnp.concatenate(
        [basis, jnp.where(sub == kinds, 1.0, 0.0)], axis=0
    ).astype(BF16)
    yield
    half = jnp.dot(fwd_in[...], inputs[...], preferred_element_type=F32)
    tan = jnp.tanh(half)
    up = 1.0 + tan
    hidden = half * up
    slope_one = up + hidden * (1.0 - tan)
    hidden = hidden.astype(BF16)
    yield
    half = jnp.dot(fwd_hid[...], hidden, preferred_element_type=F32)
    tan = jnp.tanh(half)
    up = 1.0 + tan
    second = half * up
    slope_two = (up + second * (1.0 - tan)).astype(BF16)
    second = second.astype(BF16)
    yield
    score = jnp.dot(readout[...], second, preferred_element_type=F32)
    score = score[0:1] + score[1:2]
    energy[...] += weight * score
    back = jnp.dot(bwd_hid[...], slope_two, preferred_element_type=F32)
    back = (back * slope_one).astype(BF16)
    yield
    back = jnp.dot(bwd_in[...], back, preferred_element_type=F32)
    scale = 0.25 * weight
    radial = scale * jnp.sum(back[2 * width : 2 * width + nrbf] * slope, axis=0, keepdims=True)
    radial = radial - (4.0 / cutoff_radius) * (inside * ratio * live) * score
    push = gap * (radial * inverse)
    for span, group, part, move in (
        (here, grp_src, back[0:width] * scale, -push),
        (there, grp_dst, back[width : 2 * width] * scale, push),
    ):
        part = part.astype(BF16)
        masks = [jnp.where(group == g, 1.0, 0.0) for g in range(GROUPS)]
        for g, mask in enumerate(masks):
            grads[g * width : (g + 1) * width, span] = part * mask.astype(BF16)
        other = pltpu.roll(move, 4, 0)
        grads[base:, span] = jnp.concatenate(
            [move * masks[g] + other * masks[g + 1] for g in range(0, GROUPS, 2)], axis=0
        ).astype(BF16)
    yield


def scatter(totals, scratch):
    hots, grads = scratch
    total_src, total_dst = totals
    spans = [(total_src, slice(0, 2 * BLOCK))]
    if total_dst is not total_src:
        spans = [(total_src, slice(0, BLOCK)), (total_dst, slice(BLOCK, 2 * BLOCK))]
    for total, span in spans:
        total[...] += lax.dot_general(
            grads[:, span], hots[:, span], (((1,), (1,)), ((), ())), preferred_element_type=F32
        )


def pair_loop(low, high, pairs, count, offset, tables, weights, scratch, energy, dims, totals, lookup):
    hots, grads, *inputs = scratch
    lanes = BLOCK // STREAMS

    def visit(index, carry):
        halves = []
        for k in range(STREAMS):
            begin = index * BLOCK + k * lanes
            halves.append(
                half_block(
                    rows_of(pairs, begin, lanes),
                    begin,
                    count,
                    offset,
                    tables,
                    weights,
                    (hots, grads, inputs[k], k),
                    energy,
                    dims,
                    lookup,
                )
            )
        for tick in range(6 + max(OFFSETS)):
            for half, late in zip(halves, OFFSETS):
                if 0 <= tick - late < 6:
                    next(half)
        scatter(totals, (hots, grads))
        return carry

    lax.fori_loop(low, high, visit, 0)


def rows_of(pairs, begin, lanes):
    span = pl.ds(pl.multiple_of(begin, lanes), lanes)
    return [pairs[k : k + 1, span] for k in range(4)]


def units(count):
    return (count + BLOCK - 1) // BLOCK


def spare_units(counts, slots):
    return 2 * pl.cdiv(slots, BLOCK) - units(counts[0, 1]) - units(counts[0, 2])


def local_kernel(first, dims, cross_slots, counts, *refs):
    if not first:
        _, energy_in, *refs = refs
    pairs, table, places, *weights = refs[:8]
    total, energy, *scratch, runs = refs[8:]
    if first:
        total[...] = jnp.zeros_like(total)
        energy_in = None
    runs[...] = jnp.zeros_like(runs)
    count = counts[0, 0]
    filled = units(count)
    early = jnp.minimum(filled, FIRST_SHARE)
    low = 0 if first else jnp.minimum(filled, FIRST_SHARE + spare_units(counts, cross_slots))
    high = early if first else filled
    pair_loop(
        low,
        high,
        pairs,
        count,
        None,
        (table, table, places, places),
        weights,
        scratch,
        runs,
        dims,
        (total, total),
        None,
    )
    fold_energy(energy, runs, energy_in)


def fold_energy(energy, runs, energy_in):
    part = jnp.sum(runs[...], axis=1, keepdims=True)
    part = jnp.broadcast_to(part, energy.shape[-2:])
    if energy_in is not None:
        part = part + energy_in[...]
    energy[...] = jnp.broadcast_to(part, energy.shape)


def cross_kernel(
    dims, counts, _, energy_in, pairs_x, pairs_y, got_x, got_y, pairs_own, table, places, *refs
):
    weights = refs[:5]
    total, energy, back_x, back_y = refs[5:9]
    *scratch, runs, away, far, lent = refs[9:]
    base = GROUPS * dims[0]
    size = table.shape[1]
    runs[...] = jnp.zeros_like(runs)
    far[...] = jnp.zeros_like(far)
    for axis, (pairs, other, back) in enumerate(
        ((pairs_x, got_x, back_x), (pairs_y, got_y, back_y))
    ):
        away[...] = jnp.zeros_like(away)
        extra = other[base:, :].astype(F32)
        for g in range(GROUPS):
            span = slice(g * size, (g + 1) * size)
            far[0:3, span] = extra[8 * g : 8 * g + 3] + extra[8 * g + 3 : 8 * g + 6]
        extra = extra[8 * GROUPS :]
        for g in range(lent.shape[1] // size):
            ids = extra[2 * g : 2 * g + 1] * 64.0 + extra[2 * g + 1 : 2 * g + 2]
            lent[:, g * size : (g + 1) * size] = jnp.broadcast_to(ids, (8, size))
        count = counts[0, 1 + axis]
        pair_loop(
            0,
            units(count),
            pairs,
            count,
            axis,
            (table, other, places, far),
            weights,
            scratch,
            runs,
            dims,
            (total, away),
            lent,
        )
        back[...] = away[...].astype(BF16)
    count = counts[0, 0]
    filled = units(count)
    pair_loop(
        jnp.minimum(filled, FIRST_SHARE),
        jnp.minimum(filled, FIRST_SHARE + spare_units(counts, pairs_x.shape[1])),
        pairs_own,
        count,
        None,
        (table, table, places, places),
        weights,
        scratch,
        runs,
        dims,
        (total, total),
        None,
    )
    fold_energy(energy, runs, energy_in)


def join_kernel(atoms, total, back_x, back_y, parts, energy, forces, feature_grads):
    energy[0] = jnp.sum(parts[:, 0:1, 0:1]) / atoms
    width = feature_grads.shape[0]
    size = total.shape[1]
    base = GROUPS * width
    for g in range(GROUPS):
        span = slice(g * size, (g + 1) * size)
        rows = slice(g * width, (g + 1) * width)
        feature_grads[:, span] = total[rows] + (
            back_x[rows].astype(F32) + back_y[rows].astype(F32)
        )
    moved = total[base:] + (back_x[base:].astype(F32) + back_y[base:].astype(F32))
    for g in range(GROUPS):
        forces[:, g * size : (g + 1) * size] = -moved[4 * g : 4 * g + 3]


vmem = pl.BlockSpec(memory_space=pltpu.VMEM)
smem = pl.BlockSpec(memory_space=pltpu.SMEM)
hbm = pl.BlockSpec(memory_space=pltpu.MemorySpace.HBM)
shape = jax.ShapeDtypeStruct
params = pltpu.CompilerParams(vmem_limit_bytes=48 * 1024 * 1024)


def in_hbm(array):
    return pltpu.with_memory_space_constraint(array, pltpu.MemorySpace.HBM)


def like(*arrays):
    return [pltpu.VMEM(item.shape, item.dtype) for item in arrays]


def scratch_of(total, depth):
    tall, size = total.shape
    lanes = BLOCK // STREAMS
    return (
        [pltpu.VMEM((size, 2 * BLOCK), BF16), pltpu.VMEM((tall, 2 * BLOCK), BF16)]
        + [pltpu.VMEM((depth, lanes), BF16)] * STREAMS
        + [pltpu.VMEM((1, lanes), F32)]
    )


def prep_call(features, positions, halo_lists, local_pairs, *weights):
    width, atoms = features.shape
    size = atoms // GROUPS
    nrbf, hid = weights[0].shape
    depth = 2 * width + nrbf + 2 * weights[3].shape[0]
    packed = shape((GROUPS * (width + 8) + LENT_ROWS, size), BF16)
    inputs = (features, positions, halo_lists) + weights
    return pl.pallas_call(
        prep_kernel,
        out_shape=(
            packed,
            packed,
            shape((8, atoms), F32),
            shape((hid, depth), BF16),
            shape((hid, hid), BF16),
            shape((hid, hid), BF16),
            shape((depth, hid), BF16),
            shape((16, hid), BF16),
            shape(local_pairs.shape, local_pairs.dtype),
        ),
        in_specs=[hbm] * 12,
        out_specs=[vmem] * 9,
        scratch_shapes=like(*inputs)
        + [pltpu.VMEM((GROUPS * 8, size), F32), pltpu.SemaphoreType.DMA((12,))],
        compiler_params=params,
        name="prep",
    )(*[in_hbm(item) for item in inputs + (local_pairs,)])


def first_call(dims, counts, pairs, table, places, *weights):
    depth, _ = weights[3].shape
    total_like = shape((GROUPS * (dims[0] + 4), table.shape[1]), F32)
    return pl.pallas_call(
        functools.partial(local_kernel, True, dims, None),
        out_shape=(total_like, shape((1, 128), F32)),
        in_specs=[smem] + [vmem] * 8,
        out_specs=[vmem] * 2,
        scratch_shapes=scratch_of(total_like, depth),
        compiler_params=params,
        name="local_first",
    )(counts, pairs, table, places, *weights)


def on_device(
    positions,
    features,
    halo_lists,
    local_pairs,
    cross_x,
    cross_y,
    pair_counts,
    w_rbf,
    w_src,
    w_dst,
    species_src,
    species_dst,
    w_hidden,
    w_latent,
    w_energy,
):
    atoms = positions.shape[1]
    width = features.shape[0]
    nrbf, hid = w_rbf.shape
    nspec = species_src.shape[0]
    size = atoms // GROUPS
    tall = GROUPS * (width + 4)
    depth = 2 * width + nrbf + 2 * nspec
    dims = (width, nrbf, nspec)
    devices = lax.axis_size("gx") * lax.axis_size("gy")
    send_x, send_y, *shared, pairs = prep_call(
        features,
        positions,
        halo_lists,
        local_pairs,
        w_rbf,
        w_src,
        w_dst,
        species_src,
        species_dst,
        w_hidden,
        w_latent,
        w_energy.reshape(1, -1),
    )
    got_x = shifted(send_x, "gx", -1)
    got_y = shifted(send_y, "gy", -1)
    own = (pairs, send_x, *shared)
    total, energy = first_call(dims, pair_counts, *own)
    total_like = shape(total.shape, F32)
    back_like = shape(total.shape, BF16)
    scratch = scratch_of(total, depth)
    total, energy, back_x, back_y = pl.pallas_call(
        functools.partial(cross_kernel, dims),
        out_shape=(total_like, shape((1, 128), F32), back_like, back_like),
        in_specs=[smem] + [vmem] * 14,
        out_specs=[vmem] * 4,
        scratch_shapes=scratch
        + [
            pltpu.VMEM((tall, size), F32),
            pltpu.VMEM((8, atoms), F32),
            pltpu.VMEM((8, halo_lists.shape[1]), F32),
        ],
        input_output_aliases={1: 0},
        compiler_params=params,
        name="cross",
    )(pair_counts, total, energy, cross_x, cross_y, got_x, got_y, *own)
    back_x = shifted(back_x, "gx", 1)
    back_y = shifted(back_y, "gy", 1)
    total, energy = pl.pallas_call(
        functools.partial(local_kernel, False, dims, cross_x.shape[1]),
        out_shape=(total_like, shape((devices, 1, 128), F32)),
        in_specs=[smem] + [vmem] * 10,
        out_specs=[vmem] * 2,
        scratch_shapes=scratch,
        input_output_aliases={1: 0},
        compiler_params=params,
        name="local_rest",
    )(pair_counts, total, energy, *own)
    parts = lax.all_to_all(energy, ("gx", "gy"), 0, 0)
    return pl.pallas_call(
        functools.partial(join_kernel, atoms * devices),
        out_shape=(shape((1,), F32), shape(positions.shape, F32), shape(features.shape, F32)),
        in_specs=[vmem] * 4,
        out_specs=[smem, vmem, vmem],
        compiler_params=params,
        name="join",
    )(total, back_x, back_y, parts)


def solution(mesh):
    spread = P(None, ("gx", "gy"))
    return jax.shard_map(
        on_device,
        mesh=mesh,
        in_specs=(spread,) * 6 + (P(("gx", "gy"), None),) + (P(),) * 8,
        out_specs=(P(), spread, spread),
        check_vma=False,
    )
```

```python
import functools
import math

import jax
import jax.numpy as jnp
from jax import lax
from jax.experimental import pallas as pl
from jax.experimental.pallas import tpu as pltpu
from jax.sharding import PartitionSpec as P

BLOCK = 1024
STREAMS = 4
OFFSETS = (0, 0, 0, 0)
GROUPS = 4
FIRST_SHARE = 3
LENT_ROWS = 16

cutoff_radius = 6.0
block_edge = 6.0
softening = 0.1

F32 = jnp.float32
BF16 = jnp.bfloat16


def shifted(array, axis, by):
    length = lax.axis_size(axis)
    return lax.ppermute(array, axis, [(i, (i + by) % length) for i in range(length)])


def sin_cos_pi(x):
    near = jnp.floor(x + 0.5)
    y = (x - near) * math.pi
    odd = near - 2.0 * jnp.floor(near * 0.5)
    sign = 1.0 - 2.0 * odd
    z = y * y
    s = z * (-1.0 / 39916800) + 1.0 / 362880
    s = s * z - 1.0 / 5040
    s = s * z + 1.0 / 120
    s = s * z - 1.0 / 6
    s = s * z + 1.0
    c = z * (1.0 / 479001600) - 1.0 / 3628800
    c = c * z + 1.0 / 40320
    c = c * z - 1.0 / 720
    c = c * z + 1.0 / 24
    c = c * z - 0.5
    c = c * z + 1.0
    return sign * (s * y), sign * c


def group_of(index, size, groups):
    group = jnp.zeros_like(index)
    for g in range(1, groups):
        group = group + (index >= g * size).astype(jnp.int32)
    return group, index - group * size


def pick_group(stack, group, height, groups, base=0):
    out = stack[base + (groups - 1) * height : base + groups * height]
    for g in range(groups - 2, -1, -1):
        out = jnp.where(group == g, stack[base + g * height : base + (g + 1) * height], out)
    return out


def pick_lanes(table, index, other):
    out = []
    upper = lax.broadcasted_iota(jnp.int32, (8, 128), 0) >= 4
    for c in range(0, index.shape[1], 128):
        spots = jnp.where(upper, other[:, c : c + 128], index[:, c : c + 128])
        chunk = spots >> 7
        lane = spots & 127
        best = jnp.zeros((8, 128), F32)
        for j in range(table.shape[1] // 128):
            found = jnp.take_along_axis(
                table[:, j * 128 : (j + 1) * 128], lane, axis=1, mode="promise_in_bounds"
            )
            best = jnp.where(chunk == j, found, best)
        out.append(best)
    return jnp.concatenate(out, axis=1)


def one_hot(row, size):
    spots = lax.broadcasted_iota(jnp.int16, (size, row.shape[1]), 0)
    hit = spots == row.astype(jnp.int16)
    return jnp.where(hit, jnp.ones((), BF16), jnp.zeros((), BF16))


def prep_kernel(*refs):
    sources, refs = refs[:13], refs[13:]
    (send_x, send_y, places, fwd_in, fwd_hid, bwd_hid, bwd_in, readout, pairs, counts), refs = (
        refs[:10],
        refs[10:],
    )
    targets, (wide, sems) = refs[:11], refs[11:]
    copies = [
        pltpu.make_async_copy(src, dst, sems.at[k])
        for k, (src, dst) in enumerate(zip(sources, targets + (pairs, counts)))
    ]
    for copy in copies:
        copy.start()
    for copy in copies[:3]:
        copy.wait()
    feat, pos, lists, w_rbf, w_src, w_dst, sp_src, sp_dst, w_hid, w_lat, w_en = targets
    width = feat.shape[0]
    size = send_x.shape[1]
    base = GROUPS * width
    tall = base + 8 * GROUPS
    p = pos[...]
    high = p.astype(BF16).astype(F32)
    low = p - high
    places[...] = jnp.zeros_like(places)
    places[0:3, :] = p
    places[4:7, :] = p
    wide[...] = jnp.zeros_like(wide)
    for g in range(GROUPS):
        span = slice(g * size, (g + 1) * size)
        rows = slice(g * width, (g + 1) * width)
        part = feat[:, span]
        send_x[rows, :] = part
        send_y[rows, :] = part
        wide[8 * g : 8 * g + 3, :] = high[:, span]
        wide[8 * g + 3 : 8 * g + 6, :] = low[:, span]
    part = wide[...].astype(BF16)
    send_x[base:tall, :] = part
    send_y[base:tall, :] = part
    for axis, send in enumerate((send_x, send_y)):
        wide[...] = jnp.zeros_like(wide)
        for g in range(lists.shape[1] // size):
            ids = lists[axis : axis + 1, g * size : (g + 1) * size]
            wide[2 * g : 2 * g + 1, :] = (ids >> 6).astype(F32)
            wide[2 * g + 1 : 2 * g + 2, :] = (ids & 63).astype(F32)
        send[tall:, :] = wide[0:LENT_ROWS, :].astype(BF16)
    for copy in copies[3:]:
        copy.wait()
    full = jnp.concatenate(
        [ref[...].astype(F32) for ref in (w_src, w_dst, w_rbf)]
        + [jnp.concatenate([sp_src[...].astype(F32), sp_dst[...].astype(F32)], axis=0)],
        axis=0,
    )
    bwd_in[...] = full.astype(BF16)
    fwd_in[...] = (0.5 * full.T).astype(BF16)
    hid = w_hid[...].astype(F32)
    fwd_hid[...] = (0.5 * hid.T).astype(BF16)
    column = jnp.sum(w_lat[...].astype(F32).T * w_en[...].reshape(1, -1), axis=1, keepdims=True)
    line = jnp.broadcast_to(column, (column.shape[0], 128)).T[0:8, :]
    high = line.astype(BF16).astype(F32)
    first_row = lax.broadcasted_iota(jnp.int32, line.shape, 0) == 0
    both = jnp.where(first_row, high, line - high)
    readout[...] = jnp.concatenate([both, jnp.zeros_like(both)], axis=0).astype(BF16)
    bwd_hid[...] = (hid * line[0:1, :]).astype(BF16)


def half_block(
    indices, begin, count, offset, tables, weights, scratch, energy, dims, lookup
):
    width, nrbf, nspec = dims
    fwd_in, fwd_hid, bwd_hid, bwd_in, readout = weights
    hots, grads, inputs, place = scratch
    src, dst, kind_src, kind_dst = indices
    tab_src, tab_dst, places = tables
    size = tab_src.shape[1]
    lanes = src.shape[1]
    here = slice(place * lanes, (place + 1) * lanes)
    there = slice(BLOCK + place * lanes, BLOCK + (place + 1) * lanes)
    base = GROUPS * width
    if lookup is not None:
        dst = pick_lanes(lookup, dst, dst)[0:1].astype(jnp.int32)
    grp_src, row_src = group_of(src, size, GROUPS)
    grp_dst, row_dst = group_of(dst, size, GROUPS)
    hots[:, here] = one_hot(row_src, size)
    hots[:, there] = one_hot(row_dst, size)
    yield
    got_src = jnp.dot(tab_src[0:base, :], hots[:, here], preferred_element_type=F32)
    got_dst = jnp.dot(tab_dst[0:base, :], hots[:, there], preferred_element_type=F32)
    inputs[0:width, :] = pick_group(got_src, grp_src, width, GROUPS).astype(BF16)
    inputs[width : 2 * width, :] = pick_group(got_dst, grp_dst, width, GROUPS).astype(BF16)
    sub = lax.broadcasted_iota(jnp.int32, (8, lanes), 0)
    gap = pick_lanes(places, src, dst)
    gap = pltpu.roll(gap, 4, 0) - gap
    if offset is not None:
        gap = gap + jnp.where(sub == offset, block_edge, 0.0)
    gap = jnp.where(sub < 3, gap, 0.0)
    radius = jnp.sqrt(jnp.sum(gap * gap, axis=0, keepdims=True) + softening)
    inverse = 1.0 / radius
    ratio = jnp.minimum(radius * (1.0 / cutoff_radius), 1.0)
    inside = 1.0 - ratio * ratio
    slots = begin + lax.broadcasted_iota(jnp.int32, (1, lanes), 1)
    live = jnp.where(slots < count, 1.0, 0.0)
    weight = inside * inside * live
    orders = (sub + 1).astype(F32)
    sines, cosines = sin_cos_pi(orders * ratio)
    basis = sines * inverse
    slope = (orders * (math.pi / cutoff_radius) * cosines - basis) * inverse
    kinds = jnp.where(sub < nspec, kind_src, kind_dst + nspec)
    inputs[2 * width :, :] = jnp.concatenate(
        [basis, jnp.where(sub == kinds, 1.0, 0.0)], axis=0
    ).astype(BF16)
    yield
    half = jnp.dot(fwd_in[...], inputs[...], preferred_element_type=F32)
    tan = jnp.tanh(half)
    up = 1.0 + tan
    hidden = half * up
    slope_one = up + hidden * (1.0 - tan)
    hidden = hidden.astype(BF16)
    yield
    half = jnp.dot(fwd_hid[...], hidden, preferred_element_type=F32)
    up = (1.0 + jnp.tanh(half)).astype(BF16)
    second = half.astype(BF16) * up
    slope_two = up + second * (2.0 - up)
    yield
    score = jnp.dot(readout[...], second, preferred_element_type=F32)
    score = score[0:1] + score[1:2]
    energy[...] += weight * score
    back = jnp.dot(bwd_hid[...], slope_two, preferred_element_type=F32)
    back = (back * slope_one).astype(BF16)
    yield
    back = jnp.dot(bwd_in[...], back, preferred_element_type=F32)
    scale = 0.25 * weight
    radial = scale * jnp.sum(back[2 * width : 2 * width + nrbf] * slope, axis=0, keepdims=True)
    radial = radial - (4.0 / cutoff_radius) * (inside * ratio * live) * score
    push = gap * (radial * inverse)
    for span, group, part, move in (
        (here, grp_src, back[0:width] * scale, -push),
        (there, grp_dst, back[width : 2 * width] * scale, push),
    ):
        part = part.astype(BF16)
        masks = [jnp.where(group == g, 1.0, 0.0) for g in range(GROUPS)]
        for g, mask in enumerate(masks):
            grads[g * width : (g + 1) * width, span] = part * mask.astype(BF16)
        other = pltpu.roll(move, 4, 0)
        grads[base:, span] = jnp.concatenate(
            [move * masks[g] + other * masks[g + 1] for g in range(0, GROUPS, 2)], axis=0
        ).astype(BF16)
    yield


def scatter(totals, scratch):
    hots, grads = scratch
    total_src, total_dst = totals
    spans = [(total_src, slice(0, 2 * BLOCK))]
    if total_dst is not total_src:
        spans = [(total_src, slice(0, BLOCK)), (total_dst, slice(BLOCK, 2 * BLOCK))]
    for total, span in spans:
        total[...] += lax.dot_general(
            grads[:, span], hots[:, span], (((1,), (1,)), ((), ())), preferred_element_type=F32
        )


def pair_loop(low, high, pairs, count, offset, tables, weights, scratch, energy, dims, totals, lookup):
    hots, grads, *inputs = scratch
    lanes = BLOCK // STREAMS

    def visit(index, carry):
        halves = []
        for k in range(STREAMS):
            begin = index * BLOCK + k * lanes
            halves.append(
                half_block(
                    rows_of(pairs, begin, lanes),
                    begin,
                    count,
                    offset,
                    tables,
                    weights,
                    (hots, grads, inputs[k], k),
                    energy,
                    dims,
                    lookup,
                )
            )
        for tick in range(6 + max(OFFSETS)):
            for half, late in zip(halves, OFFSETS):
                if 0 <= tick - late < 6:
                    next(half)
        scatter(totals, (hots, grads))
        return carry

    lax.fori_loop(low, high, visit, 0)


def rows_of(pairs, begin, lanes):
    span = pl.ds(pl.multiple_of(begin, lanes), lanes)
    return [pairs[k : k + 1, span] for k in range(4)]


def units(count):
    return (count + BLOCK - 1) // BLOCK


def spare_units(counts, slots):
    return 2 * pl.cdiv(slots, BLOCK) - units(counts[0, 1]) - units(counts[0, 2])


def local_kernel(first, dims, cross_slots, counts, *refs):
    if not first:
        _, energy_in, *refs = refs
    pairs, table, places, *weights = refs[:8]
    total, energy, *scratch, runs = refs[8:]
    if first:
        total[...] = jnp.zeros_like(total)
        energy_in = None
    runs[...] = jnp.zeros_like(runs)
    count = counts[0, 0]
    filled = units(count)
    early = jnp.minimum(filled, FIRST_SHARE)
    low = 0 if first else jnp.minimum(filled, FIRST_SHARE + spare_units(counts, cross_slots))
    high = early if first else filled
    pair_loop(
        low,
        high,
        pairs,
        count,
        None,
        (table, table, places),
        weights,
        scratch,
        runs,
        dims,
        (total, total),
        None,
    )
    fold_energy(energy, runs, energy_in)


def fold_energy(energy, runs, energy_in):
    part = jnp.sum(runs[...], axis=1, keepdims=True)
    part = jnp.broadcast_to(part, energy.shape[-2:])
    if energy_in is not None:
        part = part + energy_in[...]
    energy[...] = jnp.broadcast_to(part, energy.shape)


def cross_kernel(
    dims, counts, _, energy_in, pairs_x, pairs_y, got_x, got_y, pairs_own, table, places, *refs
):
    weights = refs[:5]
    total, energy, back_x, back_y = refs[5:9]
    *scratch, runs, away, far, lent = refs[9:]
    base = GROUPS * dims[0]
    size = table.shape[1]
    runs[...] = jnp.zeros_like(runs)
    far[...] = places[...]
    for axis, (pairs, other, back) in enumerate(
        ((pairs_x, got_x, back_x), (pairs_y, got_y, back_y))
    ):
        away[...] = jnp.zeros_like(away)
        extra = other[base:, :].astype(F32)
        for g in range(GROUPS):
            span = slice(g * size, (g + 1) * size)
            far[4:7, span] = extra[8 * g : 8 * g + 3] + extra[8 * g + 3 : 8 * g + 6]
        extra = extra[8 * GROUPS :]
        for g in range(lent.shape[1] // size):
            ids = extra[2 * g : 2 * g + 1] * 64.0 + extra[2 * g + 1 : 2 * g + 2]
            lent[:, g * size : (g + 1) * size] = jnp.broadcast_to(ids, (8, size))
        count = counts[0, 1 + axis]
        pair_loop(
            0,
            units(count),
            pairs,
            count,
            axis,
            (table, other, far),
            weights,
            scratch,
            runs,
            dims,
            (total, away),
            lent,
        )
        back[...] = away[...].astype(BF16)
    count = counts[0, 0]
    filled = units(count)
    pair_loop(
        jnp.minimum(filled, FIRST_SHARE),
        jnp.minimum(filled, FIRST_SHARE + spare_units(counts, pairs_x.shape[1])),
        pairs_own,
        count,
        None,
        (table, table, places),
        weights,
        scratch,
        runs,
        dims,
        (total, total),
        None,
    )
    fold_energy(energy, runs, energy_in)


def join_kernel(atoms, total, back_x, back_y, parts, energy, forces, feature_grads):
    energy[0] = jnp.sum(parts[:, 0:1, 0:1]) / atoms
    width = feature_grads.shape[0]
    size = total.shape[1]
    base = GROUPS * width
    for g in range(GROUPS):
        span = slice(g * size, (g + 1) * size)
        rows = slice(g * width, (g + 1) * width)
        feature_grads[:, span] = total[rows] + (
            back_x[rows].astype(F32) + back_y[rows].astype(F32)
        )
    moved = total[base:] + (back_x[base:].astype(F32) + back_y[base:].astype(F32))
    for g in range(GROUPS):
        forces[:, g * size : (g + 1) * size] = -moved[4 * g : 4 * g + 3]


vmem = pl.BlockSpec(memory_space=pltpu.VMEM)
smem = pl.BlockSpec(memory_space=pltpu.SMEM)
hbm = pl.BlockSpec(memory_space=pltpu.MemorySpace.HBM)
shape = jax.ShapeDtypeStruct
params = pltpu.CompilerParams(vmem_limit_bytes=48 * 1024 * 1024)


def in_hbm(array):
    return pltpu.with_memory_space_constraint(array, pltpu.MemorySpace.HBM)


def like(*arrays):
    return [pltpu.VMEM(item.shape, item.dtype) for item in arrays]


def scratch_of(total, depth):
    tall, size = total.shape
    lanes = BLOCK // STREAMS
    return (
        [pltpu.VMEM((size, 2 * BLOCK), BF16), pltpu.VMEM((tall, 2 * BLOCK), BF16)]
        + [pltpu.VMEM((depth, lanes), BF16)] * STREAMS
        + [pltpu.VMEM((1, lanes), F32)]
    )


def prep_call(features, positions, halo_lists, local_pairs, counts, *weights):
    width, atoms = features.shape
    size = atoms // GROUPS
    nrbf, hid = weights[0].shape
    depth = 2 * width + nrbf + 2 * weights[3].shape[0]
    packed = shape((GROUPS * (width + 8) + LENT_ROWS, size), BF16)
    *front, w_latent, w_energy = weights
    inputs = (features, positions, halo_lists, *front, w_latent.T, w_energy)
    return pl.pallas_call(
        prep_kernel,
        out_shape=(
            packed,
            packed,
            shape((8, atoms), F32),
            shape((hid, depth), BF16),
            shape((hid, hid), BF16),
            shape((hid, hid), BF16),
            shape((depth, hid), BF16),
            shape((16, hid), BF16),
            shape(local_pairs.shape, local_pairs.dtype),
            shape(counts.shape, counts.dtype),
        ),
        in_specs=[hbm] * 13,
        out_specs=[vmem] * 9 + [smem],
        scratch_shapes=like(*inputs)
        + [pltpu.VMEM((GROUPS * 8, size), F32), pltpu.SemaphoreType.DMA((13,))],
        compiler_params=params,
        name="prep",
    )(*[in_hbm(item) for item in inputs + (local_pairs, counts)])


def first_call(dims, counts, pairs, table, places, *weights):
    depth, _ = weights[3].shape
    total_like = shape((GROUPS * (dims[0] + 4), table.shape[1]), F32)
    return pl.pallas_call(
        functools.partial(local_kernel, True, dims, None),
        out_shape=(total_like, shape((1, 128), F32)),
        in_specs=[smem] + [vmem] * 8,
        out_specs=[vmem] * 2,
        scratch_shapes=scratch_of(total_like, depth),
        compiler_params=params,
        name="local_first",
    )(counts, pairs, table, places, *weights)


def on_device(
    positions,
    features,
    halo_lists,
    local_pairs,
    cross_x,
    cross_y,
    pair_counts,
    w_rbf,
    w_src,
    w_dst,
    species_src,
    species_dst,
    w_hidden,
    w_latent,
    w_energy,
):
    atoms = positions.shape[1]
    width = features.shape[0]
    nrbf, hid = w_rbf.shape
    nspec = species_src.shape[0]
    size = atoms // GROUPS
    tall = GROUPS * (width + 4)
    depth = 2 * width + nrbf + 2 * nspec
    dims = (width, nrbf, nspec)
    devices = lax.axis_size("gx") * lax.axis_size("gy")
    send_x, send_y, *shared, pairs, counts = prep_call(
        features,
        positions,
        halo_lists,
        local_pairs,
        pair_counts,
        w_rbf,
        w_src,
        w_dst,
        species_src,
        species_dst,
        w_hidden,
        w_latent,
        w_energy,
    )
    got_x = shifted(send_x, "gx", -1)
    got_y = shifted(send_y, "gy", -1)
    own = (pairs, send_x, *shared)
    total, energy = first_call(dims, counts, *own)
    total_like = shape(total.shape, F32)
    back_like = shape(total.shape, BF16)
    scratch = scratch_of(total, depth)
    total, energy, back_x, back_y = pl.pallas_call(
        functools.partial(cross_kernel, dims),
        out_shape=(total_like, shape((1, 128), F32), back_like, back_like),
        in_specs=[smem] + [vmem] * 14,
        out_specs=[vmem] * 4,
        scratch_shapes=scratch
        + [
            pltpu.VMEM((tall, size), F32),
            pltpu.VMEM((8, atoms), F32),
            pltpu.VMEM((8, halo_lists.shape[1]), F32),
        ],
        input_output_aliases={1: 0},
        compiler_params=params,
        name="cross",
    )(counts, total, energy, cross_x, cross_y, got_x, got_y, *own)
    back_x = shifted(back_x, "gx", 1)
    back_y = shifted(back_y, "gy", 1)
    total, energy = pl.pallas_call(
        functools.partial(local_kernel, False, dims, cross_x.shape[1]),
        out_shape=(total_like, shape((devices, 1, 128), F32)),
        in_specs=[smem] + [vmem] * 10,
        out_specs=[vmem] * 2,
        scratch_shapes=scratch,
        input_output_aliases={1: 0},
        compiler_params=params,
        name="local_rest",
    )(counts, total, energy, *own)
    parts = lax.all_to_all(energy, ("gx", "gy"), 0, 0)
    return pl.pallas_call(
        functools.partial(join_kernel, atoms * devices),
        out_shape=(shape((1,), F32), shape(positions.shape, F32), shape(features.shape, F32)),
        in_specs=[vmem] * 4,
        out_specs=[smem, vmem, vmem],
        compiler_params=params,
        name="join",
    )(total, back_x, back_y, parts)


def solution(mesh):
    spread = P(None, ("gx", "gy"))
    return jax.shard_map(
        on_device,
        mesh=mesh,
        in_specs=(spread,) * 6 + (P(("gx", "gy"), None),) + (P(),) * 8,
        out_specs=(P(), spread, spread),
        check_vma=False,
    )
```

```python
import functools
import math

import jax
import jax.numpy as jnp
from jax import lax
from jax.experimental import pallas as pl
from jax.experimental.pallas import tpu as pltpu
from jax.sharding import PartitionSpec as P

BLOCK = 1024
STREAMS = 4
OFFSETS = (0, 0, 0, 0)
GROUPS = 4
LENT_ROWS = 16

cutoff_radius = 6.0
block_edge = 6.0
softening = 0.1

F32 = jnp.float32
BF16 = jnp.bfloat16


def shifted(array, axis, by):
    length = lax.axis_size(axis)
    return lax.ppermute(array, axis, [(i, (i + by) % length) for i in range(length)])


def sin_cos_pi(x):
    near = jnp.floor(x + 0.5)
    y = (x - near) * math.pi
    odd = near - 2.0 * jnp.floor(near * 0.5)
    sign = 1.0 - 2.0 * odd
    z = y * y
    s = z * (-1.0 / 39916800) + 1.0 / 362880
    s = s * z - 1.0 / 5040
    s = s * z + 1.0 / 120
    s = s * z - 1.0 / 6
    s = s * z + 1.0
    c = z * (1.0 / 479001600) - 1.0 / 3628800
    c = c * z + 1.0 / 40320
    c = c * z - 1.0 / 720
    c = c * z + 1.0 / 24
    c = c * z - 0.5
    c = c * z + 1.0
    return sign * (s * y), sign * c


def group_of(index, size, groups):
    group = jnp.zeros_like(index)
    for g in range(1, groups):
        group = group + (index >= g * size).astype(jnp.int32)
    return group, index - group * size


def pick_group(stack, group, height, groups, base=0):
    out = stack[base + (groups - 1) * height : base + groups * height]
    for g in range(groups - 2, -1, -1):
        out = jnp.where(group == g, stack[base + g * height : base + (g + 1) * height], out)
    return out


def pick_lanes(table, index, other):
    out = []
    upper = lax.broadcasted_iota(jnp.int32, (8, 128), 0) >= 4
    for c in range(0, index.shape[1], 128):
        spots = jnp.where(upper, other[:, c : c + 128], index[:, c : c + 128])
        chunk = spots >> 7
        lane = spots & 127
        best = jnp.zeros((8, 128), F32)
        for j in range(table.shape[1] // 128):
            found = jnp.take_along_axis(
                table[:, j * 128 : (j + 1) * 128], lane, axis=1, mode="promise_in_bounds"
            )
            best = jnp.where(chunk == j, found, best)
        out.append(best)
    return jnp.concatenate(out, axis=1)


def one_hot(row, size):
    spots = lax.broadcasted_iota(jnp.int16, (size, row.shape[1]), 0)
    hit = spots == row.astype(jnp.int16)
    return jnp.where(hit, jnp.ones((), BF16), jnp.zeros((), BF16))


def prep_kernel(*refs):
    sources, refs = refs[:13], refs[13:]
    (send_x, send_y, places, fwd_in, fwd_hid, bwd_hid, bwd_in, readout, pairs, counts), refs = (
        refs[:10],
        refs[10:],
    )
    targets, (wide, sems) = refs[:11], refs[11:]
    copies = [
        pltpu.make_async_copy(src, dst, sems.at[k])
        for k, (src, dst) in enumerate(zip(sources, targets + (pairs, counts)))
    ]
    for copy in copies:
        copy.start()
    for copy in copies[:3]:
        copy.wait()
    feat, pos, lists, w_rbf, w_src, w_dst, sp_src, sp_dst, w_hid, w_lat, w_en = targets
    width = feat.shape[0]
    size = send_x.shape[1]
    base = GROUPS * width
    tall = base + 8 * GROUPS
    p = pos[...]
    high = p.astype(BF16).astype(F32)
    low = p - high
    places[...] = jnp.zeros_like(places)
    places[0:3, :] = p
    places[4:7, :] = p
    wide[...] = jnp.zeros_like(wide)
    for g in range(GROUPS):
        span = slice(g * size, (g + 1) * size)
        rows = slice(g * width, (g + 1) * width)
        part = feat[:, span]
        send_x[rows, :] = part
        send_y[rows, :] = part
        wide[8 * g : 8 * g + 3, :] = high[:, span]
        wide[8 * g + 3 : 8 * g + 6, :] = low[:, span]
    part = wide[...].astype(BF16)
    send_x[base:tall, :] = part
    send_y[base:tall, :] = part
    for axis, send in enumerate((send_x, send_y)):
        wide[...] = jnp.zeros_like(wide)
        for g in range(lists.shape[1] // size):
            ids = lists[axis : axis + 1, g * size : (g + 1) * size]
            wide[2 * g : 2 * g + 1, :] = (ids >> 6).astype(F32)
            wide[2 * g + 1 : 2 * g + 2, :] = (ids & 63).astype(F32)
        send[tall:, :] = wide[0:LENT_ROWS, :].astype(BF16)
    for copy in copies[3:]:
        copy.wait()
    full = jnp.concatenate(
        [ref[...].astype(F32) for ref in (w_src, w_dst, w_rbf)]
        + [jnp.concatenate([sp_src[...].astype(F32), sp_dst[...].astype(F32)], axis=0)],
        axis=0,
    )
    bwd_in[...] = full.astype(BF16)
    fwd_in[...] = (0.5 * full.T).astype(BF16)
    hid = w_hid[...].astype(F32)
    fwd_hid[...] = (0.5 * hid.T).astype(BF16)
    column = jnp.sum(w_lat[...].astype(F32).T * w_en[...].reshape(1, -1), axis=1, keepdims=True)
    line = jnp.broadcast_to(column, (column.shape[0], 128)).T[0:8, :]
    high = line.astype(BF16).astype(F32)
    first_row = lax.broadcasted_iota(jnp.int32, line.shape, 0) == 0
    both = jnp.where(first_row, high, line - high)
    readout[...] = jnp.concatenate([both, jnp.zeros_like(both)], axis=0).astype(BF16)
    bwd_hid[...] = (hid * line[0:1, :]).astype(BF16)


def half_block(
    indices, begin, count, offset, tables, weights, scratch, energy, dims, lookup
):
    width, nrbf, nspec = dims
    fwd_in, fwd_hid, bwd_hid, bwd_in, readout = weights
    hots, grads, inputs, place = scratch
    src, dst, kind_src, kind_dst = indices
    tab_src, tab_dst, places = tables
    size = tab_src.shape[1]
    lanes = src.shape[1]
    here = slice(place * lanes, (place + 1) * lanes)
    there = slice(BLOCK + place * lanes, BLOCK + (place + 1) * lanes)
    base = GROUPS * width
    if lookup is not None:
        dst = pick_lanes(lookup, dst, dst)[0:1].astype(jnp.int32)
    grp_src, row_src = group_of(src, size, GROUPS)
    grp_dst, row_dst = group_of(dst, size, GROUPS)
    hots[:, here] = one_hot(row_src, size)
    hots[:, there] = one_hot(row_dst, size)
    yield
    got_src = jnp.dot(tab_src[0:base, :], hots[:, here], preferred_element_type=F32)
    got_dst = jnp.dot(tab_dst[0:base, :], hots[:, there], preferred_element_type=F32)
    inputs[0:width, :] = pick_group(got_src, grp_src, width, GROUPS).astype(BF16)
    inputs[width : 2 * width, :] = pick_group(got_dst, grp_dst, width, GROUPS).astype(BF16)
    sub = lax.broadcasted_iota(jnp.int32, (8, lanes), 0)
    gap = pick_lanes(places, src, dst)
    gap = pltpu.roll(gap, 4, 0) - gap
    if offset is not None:
        gap = gap + jnp.where(sub == offset, block_edge, 0.0)
    gap = jnp.where(sub < 3, gap, 0.0)
    radius = jnp.sqrt(jnp.sum(gap * gap, axis=0, keepdims=True) + softening)
    inverse = 1.0 / radius
    ratio = jnp.minimum(radius * (1.0 / cutoff_radius), 1.0)
    inside = 1.0 - ratio * ratio
    slots = begin + lax.broadcasted_iota(jnp.int32, (1, lanes), 1)
    live = jnp.where(slots < count, 1.0, 0.0)
    weight = inside * inside * live
    orders = (sub + 1).astype(F32)
    sines, cosines = sin_cos_pi(orders * ratio)
    basis = sines * inverse
    slope = (orders * (math.pi / cutoff_radius) * cosines - basis) * inverse
    kinds = jnp.where(sub < nspec, kind_src, kind_dst + nspec)
    inputs[2 * width :, :] = jnp.concatenate(
        [basis, jnp.where(sub == kinds, 1.0, 0.0)], axis=0
    ).astype(BF16)
    yield
    half = jnp.dot(fwd_in[...], inputs[...], preferred_element_type=F32)
    tan = jnp.tanh(half)
    up = 1.0 + tan
    hidden = half * up
    slope_one = up + hidden * (1.0 - tan)
    hidden = hidden.astype(BF16)
    yield
    half = jnp.dot(fwd_hid[...], hidden, preferred_element_type=F32)
    up = (1.0 + jnp.tanh(half)).astype(BF16)
    second = half.astype(BF16) * up
    slope_two = up + second * (2.0 - up)
    yield
    score = jnp.dot(readout[...], second, preferred_element_type=F32)
    score = score[0:1] + score[1:2]
    energy[...] += weight * score
    back = jnp.dot(bwd_hid[...], slope_two, preferred_element_type=F32)
    back = (back * slope_one).astype(BF16)
    yield
    back = jnp.dot(bwd_in[...], back, preferred_element_type=F32)
    scale = 0.25 * weight
    radial = scale * jnp.sum(back[2 * width : 2 * width + nrbf] * slope, axis=0, keepdims=True)
    radial = radial - (4.0 / cutoff_radius) * (inside * ratio * live) * score
    push = gap * (radial * inverse)
    for span, group, part, move in (
        (here, grp_src, back[0:width] * scale, -push),
        (there, grp_dst, back[width : 2 * width] * scale, push),
    ):
        part = part.astype(BF16)
        masks = [jnp.where(group == g, 1.0, 0.0) for g in range(GROUPS)]
        for g, mask in enumerate(masks):
            grads[g * width : (g + 1) * width, span] = part * mask.astype(BF16)
        other = pltpu.roll(move, 4, 0)
        grads[base:, span] = jnp.concatenate(
            [move * masks[g] + other * masks[g + 1] for g in range(0, GROUPS, 2)], axis=0
        ).astype(BF16)
    yield


def scatter(totals, scratch):
    hots, grads = scratch
    total_src, total_dst = totals
    spans = [(total_src, slice(0, 2 * BLOCK))]
    if total_dst is not total_src:
        spans = [(total_src, slice(0, BLOCK)), (total_dst, slice(BLOCK, 2 * BLOCK))]
    for total, span in spans:
        total[...] += lax.dot_general(
            grads[:, span], hots[:, span], (((1,), (1,)), ((), ())), preferred_element_type=F32
        )


def pair_loop(filled, pairs, count, offset, tables, weights, scratch, energy, dims, totals, lookup):
    hots, grads, *inputs = scratch
    lanes = BLOCK // STREAMS

    def visit(index, carry):
        halves = []
        for k in range(STREAMS):
            begin = index * BLOCK + k * lanes
            halves.append(
                half_block(
                    rows_of(pairs, begin, lanes),
                    begin,
                    count,
                    offset,
                    tables,
                    weights,
                    (hots, grads, inputs[k], k),
                    energy,
                    dims,
                    lookup,
                )
            )
        for tick in range(6 + max(OFFSETS)):
            for half, late in zip(halves, OFFSETS):
                if 0 <= tick - late < 6:
                    next(half)
        scatter(totals, (hots, grads))
        return carry

    lax.fori_loop(0, filled, visit, 0)


def rows_of(pairs, begin, lanes):
    span = pl.ds(pl.multiple_of(begin, lanes), lanes)
    return [pairs[k : k + 1, span] for k in range(4)]


def units(count):
    return (count + BLOCK - 1) // BLOCK


def local_kernel(dims, counts, pairs, table, places, *refs):
    weights = refs[:5]
    total, energy, *scratch, runs = refs[5:]
    total[...] = jnp.zeros_like(total)
    runs[...] = jnp.zeros_like(runs)
    count = counts[0, 0]
    pair_loop(
        units(count),
        pairs,
        count,
        None,
        (table, table, places),
        weights,
        scratch,
        runs,
        dims,
        (total, total),
        None,
    )
    fold_energy(energy, runs, None)


def fold_energy(energy, runs, energy_in):
    part = jnp.sum(runs[...], axis=1, keepdims=True)
    part = jnp.broadcast_to(part, energy.shape[-2:])
    if energy_in is not None:
        part = part + energy_in[...]
    energy[...] = jnp.broadcast_to(part, energy.shape)


def cross_kernel(
    dims, counts, _, energy_in, pairs_x, pairs_y, got_x, got_y, table, places, *refs
):
    weights = refs[:5]
    total, energy, back_x, back_y = refs[5:9]
    *scratch, runs, away, far, lent = refs[9:]
    base = GROUPS * dims[0]
    size = table.shape[1]
    runs[...] = jnp.zeros_like(runs)
    far[...] = places[...]
    for axis, (pairs, other, back) in enumerate(
        ((pairs_x, got_x, back_x), (pairs_y, got_y, back_y))
    ):
        away[...] = jnp.zeros_like(away)
        extra = other[base:, :].astype(F32)
        for g in range(GROUPS):
            span = slice(g * size, (g + 1) * size)
            far[4:7, span] = extra[8 * g : 8 * g + 3] + extra[8 * g + 3 : 8 * g + 6]
        extra = extra[8 * GROUPS :]
        for g in range(lent.shape[1] // size):
            ids = extra[2 * g : 2 * g + 1] * 64.0 + extra[2 * g + 1 : 2 * g + 2]
            lent[:, g * size : (g + 1) * size] = jnp.broadcast_to(ids, (8, size))
        count = counts[0, 1 + axis]
        pair_loop(
            units(count),
            pairs,
            count,
            axis,
            (table, other, far),
            weights,
            scratch,
            runs,
            dims,
            (total, away),
            lent,
        )
        back[...] = away[...].astype(BF16)
    fold_energy(energy, runs, energy_in)


def join_kernel(atoms, total, back_x, back_y, parts, energy, forces, feature_grads):
    energy[0] = jnp.sum(parts[:, 0:1, 0:1]) / atoms
    width = feature_grads.shape[0]
    size = total.shape[1]
    base = GROUPS * width
    for g in range(GROUPS):
        span = slice(g * size, (g + 1) * size)
        rows = slice(g * width, (g + 1) * width)
        feature_grads[:, span] = total[rows] + (
            back_x[rows].astype(F32) + back_y[rows].astype(F32)
        )
    moved = total[base:] + (back_x[base:].astype(F32) + back_y[base:].astype(F32))
    for g in range(GROUPS):
        forces[:, g * size : (g + 1) * size] = -moved[4 * g : 4 * g + 3]


vmem = pl.BlockSpec(memory_space=pltpu.VMEM)
smem = pl.BlockSpec(memory_space=pltpu.SMEM)
hbm = pl.BlockSpec(memory_space=pltpu.MemorySpace.HBM)
shape = jax.ShapeDtypeStruct
params = pltpu.CompilerParams(vmem_limit_bytes=48 * 1024 * 1024)


def in_hbm(array):
    return pltpu.with_memory_space_constraint(array, pltpu.MemorySpace.HBM)


def like(*arrays):
    return [pltpu.VMEM(item.shape, item.dtype) for item in arrays]


def scratch_of(total, depth):
    tall, size = total.shape
    lanes = BLOCK // STREAMS
    return (
        [pltpu.VMEM((size, 2 * BLOCK), BF16), pltpu.VMEM((tall, 2 * BLOCK), BF16)]
        + [pltpu.VMEM((depth, lanes), BF16)] * STREAMS
        + [pltpu.VMEM((1, lanes), F32)]
    )


def prep_call(features, positions, halo_lists, local_pairs, counts, *weights):
    width, atoms = features.shape
    size = atoms // GROUPS
    nrbf, hid = weights[0].shape
    depth = 2 * width + nrbf + 2 * weights[3].shape[0]
    packed = shape((GROUPS * (width + 8) + LENT_ROWS, size), BF16)
    *front, w_latent, w_energy = weights
    inputs = (features, positions, halo_lists, *front, w_latent.T, w_energy)
    return pl.pallas_call(
        prep_kernel,
        out_shape=(
            packed,
            packed,
            shape((8, atoms), F32),
            shape((hid, depth), BF16),
            shape((hid, hid), BF16),
            shape((hid, hid), BF16),
            shape((depth, hid), BF16),
            shape((16, hid), BF16),
            shape(local_pairs.shape, local_pairs.dtype),
            shape(counts.shape, counts.dtype),
        ),
        in_specs=[hbm] * 13,
        out_specs=[vmem] * 9 + [smem],
        scratch_shapes=like(*inputs)
        + [pltpu.VMEM((GROUPS * 8, size), F32), pltpu.SemaphoreType.DMA((13,))],
        compiler_params=params,
        name="prep",
    )(*[in_hbm(item) for item in inputs + (local_pairs, counts)])


def local_call(dims, counts, pairs, table, places, *weights):
    depth, _ = weights[3].shape
    total_like = shape((GROUPS * (dims[0] + 4), table.shape[1]), F32)
    return pl.pallas_call(
        functools.partial(local_kernel, dims),
        out_shape=(total_like, shape((1, 128), F32)),
        in_specs=[smem] + [vmem] * 8,
        out_specs=[vmem] * 2,
        scratch_shapes=scratch_of(total_like, depth),
        compiler_params=params,
        name="local",
    )(counts, pairs, table, places, *weights)


def on_device(
    positions,
    features,
    halo_lists,
    local_pairs,
    cross_x,
    cross_y,
    pair_counts,
    w_rbf,
    w_src,
    w_dst,
    species_src,
    species_dst,
    w_hidden,
    w_latent,
    w_energy,
):
    atoms = positions.shape[1]
    width = features.shape[0]
    nrbf, hid = w_rbf.shape
    nspec = species_src.shape[0]
    size = atoms // GROUPS
    tall = GROUPS * (width + 4)
    depth = 2 * width + nrbf + 2 * nspec
    dims = (width, nrbf, nspec)
    devices = lax.axis_size("gx") * lax.axis_size("gy")
    send_x, send_y, *shared, pairs, counts = prep_call(
        features,
        positions,
        halo_lists,
        local_pairs,
        pair_counts,
        w_rbf,
        w_src,
        w_dst,
        species_src,
        species_dst,
        w_hidden,
        w_latent,
        w_energy,
    )
    got_x = shifted(send_x, "gx", -1)
    got_y = shifted(send_y, "gy", -1)
    total, energy = local_call(dims, counts, pairs, send_x, *shared)
    total_like = shape(total.shape, F32)
    back_like = shape(total.shape, BF16)
    scratch = scratch_of(total, depth)
    total, energy, back_x, back_y = pl.pallas_call(
        functools.partial(cross_kernel, dims),
        out_shape=(total_like, shape((devices, 1, 128), F32), back_like, back_like),
        in_specs=[smem] + [vmem] * 13,
        out_specs=[vmem] * 4,
        scratch_shapes=scratch
        + [
            pltpu.VMEM((tall, size), F32),
            pltpu.VMEM((8, atoms), F32),
            pltpu.VMEM((8, halo_lists.shape[1]), F32),
        ],
        input_output_aliases={1: 0},
        compiler_params=params,
        name="cross",
    )(counts, total, energy, cross_x, cross_y, got_x, got_y, send_x, *shared)
    back_x = shifted(back_x, "gx", 1)
    back_y = shifted(back_y, "gy", 1)
    parts = lax.all_to_all(energy, ("gx", "gy"), 0, 0)
    return pl.pallas_call(
        functools.partial(join_kernel, atoms * devices),
        out_shape=(shape((1,), F32), shape(positions.shape, F32), shape(features.shape, F32)),
        in_specs=[vmem] * 4,
        out_specs=[smem, vmem, vmem],
        compiler_params=params,
        name="join",
    )(total, back_x, back_y, parts)


def solution(mesh):
    spread = P(None, ("gx", "gy"))
    return jax.shard_map(
        on_device,
        mesh=mesh,
        in_specs=(spread,) * 6 + (P(("gx", "gy"), None),) + (P(),) * 8,
        out_specs=(P(), spread, spread),
        check_vma=False,
    )
```

```python
import functools
import math

import jax
import jax.numpy as jnp
from jax import lax
from jax.experimental import pallas as pl
from jax.experimental.pallas import tpu as pltpu
from jax.sharding import PartitionSpec as P

BLOCK = 1024
STREAMS = 4
OFFSETS = (0, 0, 0, 0)
GROUPS = 4
LENT_ROWS = 16

cutoff_radius = 6.0
block_edge = 6.0
softening = 0.1

F32 = jnp.float32
BF16 = jnp.bfloat16


def shifted(array, axis, by):
    length = lax.axis_size(axis)
    return lax.ppermute(array, axis, [(i, (i + by) % length) for i in range(length)])


def sin_cos_pi(x):
    near = jnp.floor(x + 0.5)
    y = (x - near) * math.pi
    odd = near - 2.0 * jnp.floor(near * 0.5)
    sign = 1.0 - 2.0 * odd
    z = y * y
    s = z * (-1.0 / 39916800) + 1.0 / 362880
    s = s * z - 1.0 / 5040
    s = s * z + 1.0 / 120
    s = s * z - 1.0 / 6
    s = s * z + 1.0
    c = z * (1.0 / 479001600) - 1.0 / 3628800
    c = c * z + 1.0 / 40320
    c = c * z - 1.0 / 720
    c = c * z + 1.0 / 24
    c = c * z - 0.5
    c = c * z + 1.0
    return sign * (s * y), sign * c


def group_of(index, size, groups):
    group = jnp.zeros_like(index)
    for g in range(1, groups):
        group = group + (index >= g * size).astype(jnp.int32)
    return group, index - group * size


def pick_group(stack, group, height, groups, base=0):
    out = stack[base + (groups - 1) * height : base + groups * height]
    for g in range(groups - 2, -1, -1):
        out = jnp.where(group == g, stack[base + g * height : base + (g + 1) * height], out)
    return out


def pick_lanes(table, index, other):
    out = []
    upper = lax.broadcasted_iota(jnp.int32, (8, 128), 0) >= 4
    for c in range(0, index.shape[1], 128):
        spots = jnp.where(upper, other[:, c : c + 128], index[:, c : c + 128])
        chunk = spots >> 7
        lane = spots & 127
        best = jnp.zeros((8, 128), F32)
        for j in range(table.shape[1] // 128):
            found = jnp.take_along_axis(
                table[:, j * 128 : (j + 1) * 128], lane, axis=1, mode="promise_in_bounds"
            )
            best = jnp.where(chunk == j, found, best)
        out.append(best)
    return jnp.concatenate(out, axis=1)


def one_hot(row, size):
    spots = lax.broadcasted_iota(jnp.int16, (size, row.shape[1]), 0)
    hit = spots == row.astype(jnp.int16)
    return jnp.where(hit, jnp.ones((), BF16), jnp.zeros((), BF16))


def prep_kernel(*refs):
    sources, refs = refs[:13], refs[13:]
    (send_x, send_y, places, fwd_in, fwd_hid, bwd_hid, bwd_in, readout, pairs, counts), refs = (
        refs[:10],
        refs[10:],
    )
    targets, (wide, sems) = refs[:11], refs[11:]
    copies = [
        pltpu.make_async_copy(src, dst, sems.at[k])
        for k, (src, dst) in enumerate(zip(sources, targets + (pairs, counts)))
    ]
    for copy in copies:
        copy.start()
    for copy in copies[:3]:
        copy.wait()
    feat, pos, lists, w_rbf, w_src, w_dst, sp_src, sp_dst, w_hid, w_lat, w_en = targets
    width = feat.shape[0]
    size = send_x.shape[1]
    base = GROUPS * width
    tall = base + 8 * GROUPS
    p = pos[...]
    high = p.astype(BF16).astype(F32)
    low = p - high
    places[...] = jnp.zeros_like(places)
    places[0:3, :] = p
    places[4:7, :] = p
    wide[...] = jnp.zeros_like(wide)
    for g in range(GROUPS):
        span = slice(g * size, (g + 1) * size)
        rows = slice(g * width, (g + 1) * width)
        part = feat[:, span]
        send_x[rows, :] = part
        send_y[rows, :] = part
        wide[8 * g : 8 * g + 3, :] = high[:, span]
        wide[8 * g + 3 : 8 * g + 6, :] = low[:, span]
    part = wide[...].astype(BF16)
    send_x[base:tall, :] = part
    send_y[base:tall, :] = part
    for axis, send in enumerate((send_x, send_y)):
        wide[...] = jnp.zeros_like(wide)
        for g in range(lists.shape[1] // size):
            ids = lists[axis : axis + 1, g * size : (g + 1) * size]
            wide[2 * g : 2 * g + 1, :] = (ids >> 6).astype(F32)
            wide[2 * g + 1 : 2 * g + 2, :] = (ids & 63).astype(F32)
        send[tall:, :] = wide[0:LENT_ROWS, :].astype(BF16)
    for copy in copies[3:]:
        copy.wait()
    full = jnp.concatenate(
        [ref[...].astype(F32) for ref in (w_src, w_dst, w_rbf)]
        + [jnp.concatenate([sp_src[...].astype(F32), sp_dst[...].astype(F32)], axis=0)],
        axis=0,
    )
    bwd_in[...] = full.astype(BF16)
    fwd_in[...] = (0.5 * full.T).astype(BF16)
    hid = w_hid[...].astype(F32)
    fwd_hid[...] = (0.5 * hid.T).astype(BF16)
    column = jnp.sum(w_lat[...].astype(F32).T * w_en[...].reshape(1, -1), axis=1, keepdims=True)
    line = jnp.broadcast_to(column, (column.shape[0], 128)).T[0:8, :]
    high = line.astype(BF16).astype(F32)
    first_row = lax.broadcasted_iota(jnp.int32, line.shape, 0) == 0
    both = jnp.where(first_row, high, line - high)
    readout[...] = jnp.concatenate([both, jnp.zeros_like(both)], axis=0).astype(BF16)
    bwd_hid[...] = (hid * line[0:1, :]).astype(BF16)


def half_block(
    indices, begin, count, offset, tables, weights, scratch, energy, dims, lookup
):
    width, nrbf, nspec = dims
    fwd_in, fwd_hid, bwd_hid, bwd_in, readout = weights
    hots, grads, inputs, place = scratch
    src, dst, kind_src, kind_dst = indices
    tab_src, tab_dst, places = tables
    size = tab_src.shape[1]
    lanes = src.shape[1]
    here = slice(place * lanes, (place + 1) * lanes)
    there = slice(BLOCK + place * lanes, BLOCK + (place + 1) * lanes)
    base = GROUPS * width
    if lookup is not None:
        dst = pick_lanes(lookup, dst, dst)[0:1].astype(jnp.int32)
    grp_src, row_src = group_of(src, size, GROUPS)
    grp_dst, row_dst = group_of(dst, size, GROUPS)
    hots[:, here] = one_hot(row_src, size)
    hots[:, there] = one_hot(row_dst, size)
    yield
    got_src = jnp.dot(tab_src[0:base, :], hots[:, here], preferred_element_type=F32)
    got_dst = jnp.dot(tab_dst[0:base, :], hots[:, there], preferred_element_type=F32)
    inputs[0:width, :] = pick_group(got_src, grp_src, width, GROUPS).astype(BF16)
    inputs[width : 2 * width, :] = pick_group(got_dst, grp_dst, width, GROUPS).astype(BF16)
    sub = lax.broadcasted_iota(jnp.int32, (8, lanes), 0)
    gap = pick_lanes(places, src, dst)
    gap = pltpu.roll(gap, 4, 0) - gap
    if offset is not None:
        gap = gap + jnp.where(sub == offset, block_edge, 0.0)
    gap = jnp.where(sub < 3, gap, 0.0)
    radius = jnp.sqrt(jnp.sum(gap * gap, axis=0, keepdims=True) + softening)
    inverse = 1.0 / radius
    ratio = jnp.minimum(radius * (1.0 / cutoff_radius), 1.0)
    inside = 1.0 - ratio * ratio
    slots = begin + lax.broadcasted_iota(jnp.int32, (1, lanes), 1)
    live = jnp.where(slots < count, 1.0, 0.0)
    weight = inside * inside * live
    orders = (sub + 1).astype(F32)
    sines, cosines = sin_cos_pi(orders * ratio)
    basis = sines * inverse
    slope = (orders * (math.pi / cutoff_radius) * cosines - basis) * inverse
    kinds = jnp.where(sub < nspec, kind_src, kind_dst + nspec)
    inputs[2 * width :, :] = jnp.concatenate(
        [basis, jnp.where(sub == kinds, 1.0, 0.0)], axis=0
    ).astype(BF16)
    yield
    half = jnp.dot(fwd_in[...], inputs[...], preferred_element_type=F32)
    tan = jnp.tanh(half)
    up = 1.0 + tan
    hidden = half * up
    slope_one = up + hidden * (1.0 - tan)
    hidden = hidden.astype(BF16)
    yield
    half = jnp.dot(fwd_hid[...], hidden, preferred_element_type=F32)
    up = (1.0 + jnp.tanh(half)).astype(BF16)
    second = half.astype(BF16) * up
    slope_two = up + second * (2.0 - up)
    yield
    score = jnp.dot(readout[...], second, preferred_element_type=F32)
    score = score[0:1] + score[1:2]
    energy[...] += weight * score
    back = jnp.dot(bwd_hid[...], slope_two, preferred_element_type=F32)
    back = (back * slope_one).astype(BF16)
    yield
    back = jnp.dot(bwd_in[...], back, preferred_element_type=F32)
    scale = 0.25 * weight
    radial = scale * jnp.sum(back[2 * width : 2 * width + nrbf] * slope, axis=0, keepdims=True)
    radial = radial - (4.0 / cutoff_radius) * (inside * ratio * live) * score
    push = gap * (radial * inverse)
    for span, group, part, move in (
        (here, grp_src, back[0:width] * scale, -push),
        (there, grp_dst, back[width : 2 * width] * scale, push),
    ):
        part = part.astype(BF16)
        masks = [jnp.where(group == g, 1.0, 0.0) for g in range(GROUPS)]
        for g, mask in enumerate(masks):
            grads[g * width : (g + 1) * width, span] = part * mask.astype(BF16)
        other = pltpu.roll(move, 4, 0)
        grads[base:, span] = jnp.concatenate(
            [move * masks[g] + other * masks[g + 1] for g in range(0, GROUPS, 2)], axis=0
        ).astype(BF16)
    yield


def scatter(totals, scratch):
    hots, grads = scratch
    total_src, total_dst = totals
    spans = [(total_src, slice(0, 2 * BLOCK))]
    if total_dst is not total_src:
        spans = [(total_src, slice(0, BLOCK)), (total_dst, slice(BLOCK, 2 * BLOCK))]
    for total, span in spans:
        total[...] += lax.dot_general(
            grads[:, span], hots[:, span], (((1,), (1,)), ((), ())), preferred_element_type=F32
        )


def pair_loop(filled, pairs, count, offset, tables, weights, scratch, energy, dims, totals, lookup):
    hots, grads, *inputs = scratch
    lanes = BLOCK // STREAMS

    def visit(index, carry):
        halves = []
        for k in range(STREAMS):
            begin = index * BLOCK + k * lanes
            halves.append(
                half_block(
                    rows_of(pairs, begin, lanes),
                    begin,
                    count,
                    offset,
                    tables,
                    weights,
                    (hots, grads, inputs[k], k),
                    energy,
                    dims,
                    lookup,
                )
            )
        for tick in range(6 + max(OFFSETS)):
            for half, late in zip(halves, OFFSETS):
                if 0 <= tick - late < 6:
                    next(half)
        scatter(totals, (hots, grads))
        return carry

    lax.fori_loop(0, filled, visit, 0)


def rows_of(pairs, begin, lanes):
    span = pl.ds(pl.multiple_of(begin, lanes), lanes)
    return [pairs[k : k + 1, span] for k in range(4)]


def units(count):
    return (count + BLOCK - 1) // BLOCK


def local_kernel(dims, counts, pairs, table, places, *refs):
    weights = refs[:5]
    total, energy, *scratch, runs = refs[5:]
    total[...] = jnp.zeros_like(total)
    runs[...] = jnp.zeros_like(runs)
    count = counts[0, 0]
    pair_loop(
        units(count),
        pairs,
        count,
        None,
        (table, table, places),
        weights,
        scratch,
        runs,
        dims,
        (total, total),
        None,
    )
    fold_energy(energy, runs, None)


def fold_energy(energy, runs, energy_in):
    part = jnp.sum(runs[...], axis=1, keepdims=True)
    part = jnp.broadcast_to(part, energy.shape[-2:])
    if energy_in is not None:
        part = part + energy_in[...]
    energy[...] = jnp.broadcast_to(part, energy.shape)


def cross_kernel(
    dims, counts, _, energy_in, pairs_x, pairs_y, got_x, got_y, table, places, *refs
):
    weights = refs[:5]
    total, energy, back_x, back_y = refs[5:9]
    *scratch, runs, away, far, lent, other, pairs = refs[9:]
    base = GROUPS * dims[0]
    size = table.shape[1]
    runs[...] = jnp.zeros_like(runs)
    far[...] = places[...]

    def visit(axis, carry):
        for k, (got, listed) in enumerate(((got_x, pairs_x), (got_y, pairs_y))):

            @pl.when(axis == k)
            def _():
                other[...] = got[...]
                pairs[...] = listed[...]

        away[...] = jnp.zeros_like(away)
        extra = other[base:, :].astype(F32)
        for g in range(GROUPS):
            span = slice(g * size, (g + 1) * size)
            far[4:7, span] = extra[8 * g : 8 * g + 3] + extra[8 * g + 3 : 8 * g + 6]
        extra = extra[8 * GROUPS :]
        for g in range(lent.shape[1] // size):
            ids = extra[2 * g : 2 * g + 1] * 64.0 + extra[2 * g + 1 : 2 * g + 2]
            lent[:, g * size : (g + 1) * size] = jnp.broadcast_to(ids, (8, size))
        count = counts[0, 1 + axis]
        pair_loop(
            units(count),
            pairs,
            count,
            axis,
            (table, other, far),
            weights,
            scratch,
            runs,
            dims,
            (total, away),
            lent,
        )
        for k, back in enumerate((back_x, back_y)):

            @pl.when(axis == k)
            def _():
                back[...] = away[...].astype(BF16)

        return carry

    lax.fori_loop(0, 2, visit, 0)
    fold_energy(energy, runs, energy_in)


def join_kernel(atoms, total, back_x, back_y, parts, energy, forces, feature_grads):
    energy[0] = jnp.sum(parts[:, 0:1, 0:1]) / atoms
    width = feature_grads.shape[0]
    size = total.shape[1]
    base = GROUPS * width
    for g in range(GROUPS):
        span = slice(g * size, (g + 1) * size)
        rows = slice(g * width, (g + 1) * width)
        feature_grads[:, span] = total[rows] + (
            back_x[rows].astype(F32) + back_y[rows].astype(F32)
        )
    moved = total[base:] + (back_x[base:].astype(F32) + back_y[base:].astype(F32))
    for g in range(GROUPS):
        forces[:, g * size : (g + 1) * size] = -moved[4 * g : 4 * g + 3]


vmem = pl.BlockSpec(memory_space=pltpu.VMEM)
smem = pl.BlockSpec(memory_space=pltpu.SMEM)
hbm = pl.BlockSpec(memory_space=pltpu.MemorySpace.HBM)
shape = jax.ShapeDtypeStruct
params = pltpu.CompilerParams(vmem_limit_bytes=48 * 1024 * 1024)


def in_hbm(array):
    return pltpu.with_memory_space_constraint(array, pltpu.MemorySpace.HBM)


def like(*arrays):
    return [pltpu.VMEM(item.shape, item.dtype) for item in arrays]


def scratch_of(total, depth):
    tall, size = total.shape
    lanes = BLOCK // STREAMS
    return (
        [pltpu.VMEM((size, 2 * BLOCK), BF16), pltpu.VMEM((tall, 2 * BLOCK), BF16)]
        + [pltpu.VMEM((depth, lanes), BF16)] * STREAMS
        + [pltpu.VMEM((1, lanes), F32)]
    )


def prep_call(features, positions, halo_lists, local_pairs, counts, *weights):
    width, atoms = features.shape
    size = atoms // GROUPS
    nrbf, hid = weights[0].shape
    depth = 2 * width + nrbf + 2 * weights[3].shape[0]
    packed = shape((GROUPS * (width + 8) + LENT_ROWS, size), BF16)
    *front, w_latent, w_energy = weights
    inputs = (features, positions, halo_lists, *front, w_latent.T, w_energy)
    return pl.pallas_call(
        prep_kernel,
        out_shape=(
            packed,
            packed,
            shape((8, atoms), F32),
            shape((hid, depth), BF16),
            shape((hid, hid), BF16),
            shape((hid, hid), BF16),
            shape((depth, hid), BF16),
            shape((16, hid), BF16),
            shape(local_pairs.shape, local_pairs.dtype),
            shape(counts.shape, counts.dtype),
        ),
        in_specs=[hbm] * 13,
        out_specs=[vmem] * 9 + [smem],
        scratch_shapes=like(*inputs)
        + [pltpu.VMEM((GROUPS * 8, size), F32), pltpu.SemaphoreType.DMA((13,))],
        compiler_params=params,
        name="prep",
    )(*[in_hbm(item) for item in inputs + (local_pairs, counts)])


def local_call(dims, counts, pairs, table, places, *weights):
    depth, _ = weights[3].shape
    total_like = shape((GROUPS * (dims[0] + 4), table.shape[1]), F32)
    return pl.pallas_call(
        functools.partial(local_kernel, dims),
        out_shape=(total_like, shape((1, 128), F32)),
        in_specs=[smem] + [vmem] * 8,
        out_specs=[vmem] * 2,
        scratch_shapes=scratch_of(total_like, depth),
        compiler_params=params,
        name="local",
    )(counts, pairs, table, places, *weights)


def on_device(
    positions,
    features,
    halo_lists,
    local_pairs,
    cross_x,
    cross_y,
    pair_counts,
    w_rbf,
    w_src,
    w_dst,
    species_src,
    species_dst,
    w_hidden,
    w_latent,
    w_energy,
):
    atoms = positions.shape[1]
    width = features.shape[0]
    nrbf, hid = w_rbf.shape
    nspec = species_src.shape[0]
    size = atoms // GROUPS
    tall = GROUPS * (width + 4)
    depth = 2 * width + nrbf + 2 * nspec
    dims = (width, nrbf, nspec)
    devices = lax.axis_size("gx") * lax.axis_size("gy")
    send_x, send_y, *shared, pairs, counts = prep_call(
        features,
        positions,
        halo_lists,
        local_pairs,
        pair_counts,
        w_rbf,
        w_src,
        w_dst,
        species_src,
        species_dst,
        w_hidden,
        w_latent,
        w_energy,
    )
    got_x = shifted(send_x, "gx", -1)
    got_y = shifted(send_y, "gy", -1)
    total, energy = local_call(dims, counts, pairs, send_x, *shared)
    total_like = shape(total.shape, F32)
    back_like = shape(total.shape, BF16)
    scratch = scratch_of(total, depth)
    total, energy, back_x, back_y = pl.pallas_call(
        functools.partial(cross_kernel, dims),
        out_shape=(total_like, shape((devices, 1, 128), F32), back_like, back_like),
        in_specs=[smem] + [vmem] * 13,
        out_specs=[vmem] * 4,
        scratch_shapes=scratch
        + [
            pltpu.VMEM((tall, size), F32),
            pltpu.VMEM((8, atoms), F32),
            pltpu.VMEM((8, halo_lists.shape[1]), F32),
        ]
        + like(got_x, cross_x),
        input_output_aliases={1: 0},
        compiler_params=params,
        name="cross",
    )(counts, total, energy, cross_x, cross_y, got_x, got_y, send_x, *shared)
    back_x = shifted(back_x, "gx", 1)
    back_y = shifted(back_y, "gy", 1)
    parts = lax.all_to_all(energy, ("gx", "gy"), 0, 0)
    return pl.pallas_call(
        functools.partial(join_kernel, atoms * devices),
        out_shape=(shape((1,), F32), shape(positions.shape, F32), shape(features.shape, F32)),
        in_specs=[vmem] * 4,
        out_specs=[smem, vmem, vmem],
        compiler_params=params,
        name="join",
    )(total, back_x, back_y, parts)


def solution(mesh):
    spread = P(None, ("gx", "gy"))
    return jax.shard_map(
        on_device,
        mesh=mesh,
        in_specs=(spread,) * 6 + (P(("gx", "gy"), None),) + (P(),) * 8,
        out_specs=(P(), spread, spread),
        check_vma=False,
    )
```

```python
import functools
import math

import jax
import jax.numpy as jnp
from jax import lax
from jax.experimental import pallas as pl
from jax.experimental.pallas import tpu as pltpu
from jax.sharding import PartitionSpec as P

BLOCK = 1024
STREAMS = 4
OFFSETS = (0, 0, 0, 0)
GROUPS = 4
LENT_ROWS = 16

cutoff_radius = 6.0
block_edge = 6.0
softening = 0.1

F32 = jnp.float32
BF16 = jnp.bfloat16


def shifted(array, axis, by):
    length = lax.axis_size(axis)
    return lax.ppermute(array, axis, [(i, (i + by) % length) for i in range(length)])


def sin_cos_pi(x):
    near = jnp.floor(x + 0.5)
    y = (x - near) * math.pi
    odd = near - 2.0 * jnp.floor(near * 0.5)
    sign = 1.0 - 2.0 * odd
    z = y * y
    s = z * (-1.0 / 39916800) + 1.0 / 362880
    s = s * z - 1.0 / 5040
    s = s * z + 1.0 / 120
    s = s * z - 1.0 / 6
    s = s * z + 1.0
    c = z * (1.0 / 479001600) - 1.0 / 3628800
    c = c * z + 1.0 / 40320
    c = c * z - 1.0 / 720
    c = c * z + 1.0 / 24
    c = c * z - 0.5
    c = c * z + 1.0
    return sign * (s * y), sign * c


def group_of(index, size, groups):
    group = jnp.zeros_like(index)
    for g in range(1, groups):
        group = group + (index >= g * size).astype(jnp.int32)
    return group, index - group * size


def pick_group(stack, group, height, groups, base=0):
    out = stack[base + (groups - 1) * height : base + groups * height]
    for g in range(groups - 2, -1, -1):
        out = jnp.where(group == g, stack[base + g * height : base + (g + 1) * height], out)
    return out


def pick_rows(table, spots):
    chunk = spots >> 7
    lane = spots & 127
    best = jnp.zeros((8, 128), F32)
    for j in range(table.shape[1] // 128):
        found = jnp.take_along_axis(
            table[:, j * 128 : (j + 1) * 128], lane, axis=1, mode="promise_in_bounds"
        )
        best = jnp.where(chunk == j, found, best)
    return best


def pick_lanes(table, index, other):
    upper = lax.broadcasted_iota(jnp.int32, (8, 128), 0) >= 4
    return jnp.concatenate(
        [
            pick_rows(table, jnp.where(upper, other[:, c : c + 128], index[:, c : c + 128]))
            for c in range(0, index.shape[1], 128)
        ],
        axis=1,
    )


def one_hot(row, size):
    spots = lax.broadcasted_iota(jnp.int16, (size, row.shape[1]), 0)
    hit = spots == row.astype(jnp.int16)
    return jnp.where(hit, jnp.ones((), BF16), jnp.zeros((), BF16))


def prep_kernel(*refs):
    sources, refs = refs[:13], refs[13:]
    (send_x, send_y, places, fwd_in, fwd_hid, bwd_hid, bwd_in, readout, pairs, counts), refs = (
        refs[:10],
        refs[10:],
    )
    targets, (wide, sems) = refs[:11], refs[11:]
    copies = [
        pltpu.make_async_copy(src, dst, sems.at[k])
        for k, (src, dst) in enumerate(zip(sources, targets + (pairs, counts)))
    ]
    for copy in copies:
        copy.start()
    for copy in copies[:3]:
        copy.wait()
    feat, pos, lists, w_rbf, w_src, w_dst, sp_src, sp_dst, w_hid, w_lat, w_en = targets
    width = feat.shape[0]
    size = send_x.shape[1]
    base = GROUPS * width
    tall = base + 8 * GROUPS
    p = pos[...]
    high = p.astype(BF16).astype(F32)
    low = p - high
    places[...] = jnp.zeros_like(places)
    places[0:3, :] = p
    places[4:7, :] = p
    wide[...] = jnp.zeros_like(wide)
    for g in range(GROUPS):
        span = slice(g * size, (g + 1) * size)
        rows = slice(g * width, (g + 1) * width)
        part = feat[:, span]
        send_x[rows, :] = part
        send_y[rows, :] = part
        wide[8 * g : 8 * g + 3, :] = high[:, span]
        wide[8 * g + 3 : 8 * g + 6, :] = low[:, span]
    part = wide[...].astype(BF16)
    send_x[base:tall, :] = part
    send_y[base:tall, :] = part
    for axis, send in enumerate((send_x, send_y)):
        wide[...] = jnp.zeros_like(wide)
        for g in range(lists.shape[1] // size):
            ids = lists[axis : axis + 1, g * size : (g + 1) * size]
            wide[2 * g : 2 * g + 1, :] = (ids >> 6).astype(F32)
            wide[2 * g + 1 : 2 * g + 2, :] = (ids & 63).astype(F32)
        send[tall:, :] = wide[0:LENT_ROWS, :].astype(BF16)
    for copy in copies[3:]:
        copy.wait()
    full = jnp.concatenate(
        [ref[...].astype(F32) for ref in (w_src, w_dst, w_rbf)]
        + [jnp.concatenate([sp_src[...].astype(F32), sp_dst[...].astype(F32)], axis=0)],
        axis=0,
    )
    bwd_in[...] = full.astype(BF16)
    fwd_in[...] = (0.5 * full.T).astype(BF16)
    hid = w_hid[...].astype(F32)
    fwd_hid[...] = (0.5 * hid.T).astype(BF16)
    column = jnp.sum(w_lat[...].astype(F32).T * w_en[...].reshape(1, -1), axis=1, keepdims=True)
    line = jnp.broadcast_to(column, (column.shape[0], 128)).T[0:8, :]
    high = line.astype(BF16).astype(F32)
    first_row = lax.broadcasted_iota(jnp.int32, line.shape, 0) == 0
    both = jnp.where(first_row, high, line - high)
    readout[...] = jnp.concatenate([both, jnp.zeros_like(both)], axis=0).astype(BF16)
    bwd_hid[...] = (hid * line[0:1, :]).astype(BF16)


def half_block(
    indices, begin, count, offset, tables, weights, scratch, energy, dims
):
    width, nrbf, nspec = dims
    fwd_in, fwd_hid, bwd_hid, bwd_in, readout = weights
    hots, grads, inputs, place = scratch
    src, dst, kind_src, kind_dst = indices
    tab_src, tab_dst, places = tables
    size = tab_src.shape[1]
    lanes = src.shape[1]
    here = slice(place * lanes, (place + 1) * lanes)
    there = slice(BLOCK + place * lanes, BLOCK + (place + 1) * lanes)
    base = GROUPS * width
    grp_src, row_src = group_of(src, size, GROUPS)
    grp_dst, row_dst = group_of(dst, size, GROUPS)
    hots[:, here] = one_hot(row_src, size)
    hots[:, there] = one_hot(row_dst, size)
    yield
    got_src = jnp.dot(tab_src[0:base, :], hots[:, here], preferred_element_type=F32)
    got_dst = jnp.dot(tab_dst[0:base, :], hots[:, there], preferred_element_type=F32)
    inputs[0:width, :] = pick_group(got_src, grp_src, width, GROUPS).astype(BF16)
    inputs[width : 2 * width, :] = pick_group(got_dst, grp_dst, width, GROUPS).astype(BF16)
    sub = lax.broadcasted_iota(jnp.int32, (8, lanes), 0)
    gap = pick_lanes(places, src, dst)
    gap = pltpu.roll(gap, 4, 0) - gap
    if offset is not None:
        gap = gap + jnp.where(sub == offset, block_edge, 0.0)
    gap = jnp.where(sub < 3, gap, 0.0)
    radius = jnp.sqrt(jnp.sum(gap * gap, axis=0, keepdims=True) + softening)
    inverse = 1.0 / radius
    ratio = jnp.minimum(radius * (1.0 / cutoff_radius), 1.0)
    inside = 1.0 - ratio * ratio
    slots = begin + lax.broadcasted_iota(jnp.int32, (1, lanes), 1)
    live = jnp.where(slots < count, 1.0, 0.0)
    weight = inside * inside * live
    orders = (sub + 1).astype(F32)
    sines, cosines = sin_cos_pi(orders * ratio)
    basis = sines * inverse
    slope = (orders * (math.pi / cutoff_radius) * cosines - basis) * inverse
    kinds = jnp.where(sub < nspec, kind_src, kind_dst + nspec)
    inputs[2 * width :, :] = jnp.concatenate(
        [basis, jnp.where(sub == kinds, 1.0, 0.0)], axis=0
    ).astype(BF16)
    yield
    half = jnp.dot(fwd_in[...], inputs[...], preferred_element_type=F32)
    tan = jnp.tanh(half)
    up = 1.0 + tan
    hidden = half * up
    slope_one = up + hidden * (1.0 - tan)
    hidden = hidden.astype(BF16)
    yield
    half = jnp.dot(fwd_hid[...], hidden, preferred_element_type=F32)
    up = (1.0 + jnp.tanh(half)).astype(BF16)
    second = half.astype(BF16) * up
    slope_two = up + second * (2.0 - up)
    yield
    score = jnp.dot(readout[...], second, preferred_element_type=F32)
    score = score[0:1] + score[1:2]
    energy[...] += weight * score
    back = jnp.dot(bwd_hid[...], slope_two, preferred_element_type=F32)
    back = (back * slope_one).astype(BF16)
    yield
    back = jnp.dot(bwd_in[...], back, preferred_element_type=F32)
    scale = 0.25 * weight
    radial = scale * jnp.sum(back[2 * width : 2 * width + nrbf] * slope, axis=0, keepdims=True)
    radial = radial - (4.0 / cutoff_radius) * (inside * ratio * live) * score
    push = gap * (radial * inverse)
    for span, group, part, move in (
        (here, grp_src, back[0:width] * scale, -push),
        (there, grp_dst, back[width : 2 * width] * scale, push),
    ):
        part = part.astype(BF16)
        masks = [jnp.where(group == g, 1.0, 0.0) for g in range(GROUPS)]
        for g, mask in enumerate(masks):
            grads[g * width : (g + 1) * width, span] = part * mask.astype(BF16)
        other = pltpu.roll(move, 4, 0)
        grads[base:, span] = jnp.concatenate(
            [move * masks[g] + other * masks[g + 1] for g in range(0, GROUPS, 2)], axis=0
        ).astype(BF16)
    yield


def scatter(totals, scratch):
    hots, grads = scratch
    total_src, total_dst = totals
    spans = [(total_src, slice(0, 2 * BLOCK))]
    if total_dst is not total_src:
        spans = [(total_src, slice(0, BLOCK)), (total_dst, slice(BLOCK, 2 * BLOCK))]
    for total, span in spans:
        total[...] += lax.dot_general(
            grads[:, span], hots[:, span], (((1,), (1,)), ((), ())), preferred_element_type=F32
        )


def pair_loop(filled, pairs, count, offset, tables, weights, scratch, energy, dims, totals):
    hots, grads, *inputs = scratch
    lanes = BLOCK // STREAMS

    def visit(index, carry):
        halves = []
        for k in range(STREAMS):
            begin = index * BLOCK + k * lanes
            halves.append(
                half_block(
                    rows_of(pairs, begin, lanes),
                    begin,
                    count,
                    offset,
                    tables,
                    weights,
                    (hots, grads, inputs[k], k),
                    energy,
                    dims,
                )
            )
        for tick in range(6 + max(OFFSETS)):
            for half, late in zip(halves, OFFSETS):
                if 0 <= tick - late < 6:
                    next(half)
        scatter(totals, (hots, grads))
        return carry

    lax.fori_loop(0, filled, visit, 0)


def rows_of(pairs, begin, lanes):
    span = pl.ds(pl.multiple_of(begin, lanes), lanes)
    return [pairs[k : k + 1, span] for k in range(4)]


def units(count):
    return (count + BLOCK - 1) // BLOCK


def local_kernel(dims, counts, pairs, table, places, *refs):
    weights = refs[:5]
    total, energy, *scratch, runs = refs[5:]
    total[...] = jnp.zeros_like(total)
    runs[...] = jnp.zeros_like(runs)
    count = counts[0, 0]
    pair_loop(
        units(count),
        pairs,
        count,
        None,
        (table, table, places),
        weights,
        scratch,
        runs,
        dims,
        (total, total),
    )
    fold_energy(energy, runs, None)


def fold_energy(energy, runs, energy_in):
    part = jnp.sum(runs[...], axis=1, keepdims=True)
    part = jnp.broadcast_to(part, energy.shape[-2:])
    if energy_in is not None:
        part = part + energy_in[...]
    energy[...] = jnp.broadcast_to(part, energy.shape)


def cross_kernel(
    dims, counts, _, energy_in, pairs_x, pairs_y, got_x, got_y, table, places, *refs
):
    weights = refs[:5]
    total, energy, back_x, back_y = refs[5:9]
    *scratch, runs, away, far, lent, other, pairs = refs[9:]
    base = GROUPS * dims[0]
    size = table.shape[1]
    runs[...] = jnp.zeros_like(runs)
    far[...] = places[...]

    def visit(axis, carry):
        for k, (got, listed) in enumerate(((got_x, pairs_x), (got_y, pairs_y))):

            @pl.when(axis == k)
            def _():
                other[...] = got[...]
                pairs[...] = listed[...]

        away[...] = jnp.zeros_like(away)
        extra = other[base:, :].astype(F32)
        for g in range(GROUPS):
            span = slice(g * size, (g + 1) * size)
            far[4:7, span] = extra[8 * g : 8 * g + 3] + extra[8 * g + 3 : 8 * g + 6]
        extra = extra[8 * GROUPS :]
        for g in range(lent.shape[1] // size):
            ids = extra[2 * g : 2 * g + 1] * 64.0 + extra[2 * g + 1 : 2 * g + 2]
            lent[:, g * size : (g + 1) * size] = jnp.broadcast_to(ids, (8, size))
        for start in range(0, pairs.shape[1], 1024):
            spans = [slice(start + 128 * k, start + 128 * (k + 1)) for k in range(8)]
            slots = jnp.concatenate([pairs[1:2, span] for span in spans], axis=0)
            ids = pick_rows(lent, slots).astype(jnp.int32)
            for k, span in enumerate(spans):
                pairs[1:2, span] = ids[k : k + 1]
        count = counts[0, 1 + axis]
        pair_loop(
            units(count),
            pairs,
            count,
            axis,
            (table, other, far),
            weights,
            scratch,
            runs,
            dims,
            (total, away),
        )
        for k, back in enumerate((back_x, back_y)):

            @pl.when(axis == k)
            def _():
                back[...] = away[...].astype(BF16)

        return carry

    lax.fori_loop(0, 2, visit, 0)
    fold_energy(energy, runs, energy_in)


def join_kernel(atoms, total, back_x, back_y, parts, energy, forces, feature_grads):
    energy[0] = jnp.sum(parts[:, 0:1, 0:1]) / atoms
    width = feature_grads.shape[0]
    size = total.shape[1]
    base = GROUPS * width
    for g in range(GROUPS):
        span = slice(g * size, (g + 1) * size)
        rows = slice(g * width, (g + 1) * width)
        feature_grads[:, span] = total[rows] + (
            back_x[rows].astype(F32) + back_y[rows].astype(F32)
        )
    moved = total[base:] + (back_x[base:].astype(F32) + back_y[base:].astype(F32))
    for g in range(GROUPS):
        forces[:, g * size : (g + 1) * size] = -moved[4 * g : 4 * g + 3]


vmem = pl.BlockSpec(memory_space=pltpu.VMEM)
smem = pl.BlockSpec(memory_space=pltpu.SMEM)
hbm = pl.BlockSpec(memory_space=pltpu.MemorySpace.HBM)
shape = jax.ShapeDtypeStruct
params = pltpu.CompilerParams(vmem_limit_bytes=48 * 1024 * 1024)


def in_hbm(array):
    return pltpu.with_memory_space_constraint(array, pltpu.MemorySpace.HBM)


def like(*arrays):
    return [pltpu.VMEM(item.shape, item.dtype) for item in arrays]


def scratch_of(total, depth):
    tall, size = total.shape
    lanes = BLOCK // STREAMS
    return (
        [pltpu.VMEM((size, 2 * BLOCK), BF16), pltpu.VMEM((tall, 2 * BLOCK), BF16)]
        + [pltpu.VMEM((depth, lanes), BF16)] * STREAMS
        + [pltpu.VMEM((1, lanes), F32)]
    )


def prep_call(features, positions, halo_lists, local_pairs, counts, *weights):
    width, atoms = features.shape
    size = atoms // GROUPS
    nrbf, hid = weights[0].shape
    depth = 2 * width + nrbf + 2 * weights[3].shape[0]
    packed = shape((GROUPS * (width + 8) + LENT_ROWS, size), BF16)
    *front, w_latent, w_energy = weights
    inputs = (features, positions, halo_lists, *front, w_latent.T, w_energy)
    return pl.pallas_call(
        prep_kernel,
        out_shape=(
            packed,
            packed,
            shape((8, atoms), F32),
            shape((hid, depth), BF16),
            shape((hid, hid), BF16),
            shape((hid, hid), BF16),
            shape((depth, hid), BF16),
            shape((16, hid), BF16),
            shape(local_pairs.shape, local_pairs.dtype),
            shape(counts.shape, counts.dtype),
        ),
        in_specs=[hbm] * 13,
        out_specs=[vmem] * 9 + [smem],
        scratch_shapes=like(*inputs)
        + [pltpu.VMEM((GROUPS * 8, size), F32), pltpu.SemaphoreType.DMA((13,))],
        compiler_params=params,
        name="prep",
    )(*[in_hbm(item) for item in inputs + (local_pairs, counts)])


def local_call(dims, counts, pairs, table, places, *weights):
    depth, _ = weights[3].shape
    total_like = shape((GROUPS * (dims[0] + 4), table.shape[1]), F32)
    return pl.pallas_call(
        functools.partial(local_kernel, dims),
        out_shape=(total_like, shape((1, 128), F32)),
        in_specs=[smem] + [vmem] * 8,
        out_specs=[vmem] * 2,
        scratch_shapes=scratch_of(total_like, depth),
        compiler_params=params,
        name="local",
    )(counts, pairs, table, places, *weights)


def on_device(
    positions,
    features,
    halo_lists,
    local_pairs,
    cross_x,
    cross_y,
    pair_counts,
    w_rbf,
    w_src,
    w_dst,
    species_src,
    species_dst,
    w_hidden,
    w_latent,
    w_energy,
):
    atoms = positions.shape[1]
    width = features.shape[0]
    nrbf, hid = w_rbf.shape
    nspec = species_src.shape[0]
    size = atoms // GROUPS
    tall = GROUPS * (width + 4)
    depth = 2 * width + nrbf + 2 * nspec
    dims = (width, nrbf, nspec)
    devices = lax.axis_size("gx") * lax.axis_size("gy")
    send_x, send_y, *shared, pairs, counts = prep_call(
        features,
        positions,
        halo_lists,
        local_pairs,
        pair_counts,
        w_rbf,
        w_src,
        w_dst,
        species_src,
        species_dst,
        w_hidden,
        w_latent,
        w_energy,
    )
    got_x = shifted(send_x, "gx", -1)
    got_y = shifted(send_y, "gy", -1)
    total, energy = local_call(dims, counts, pairs, send_x, *shared)
    total_like = shape(total.shape, F32)
    back_like = shape(total.shape, BF16)
    scratch = scratch_of(total, depth)
    total, energy, back_x, back_y = pl.pallas_call(
        functools.partial(cross_kernel, dims),
        out_shape=(total_like, shape((devices, 1, 128), F32), back_like, back_like),
        in_specs=[smem] + [vmem] * 13,
        out_specs=[vmem] * 4,
        scratch_shapes=scratch
        + [
            pltpu.VMEM((tall, size), F32),
            pltpu.VMEM((8, atoms), F32),
            pltpu.VMEM((8, halo_lists.shape[1]), F32),
        ]
        + like(got_x, cross_x),
        input_output_aliases={1: 0},
        compiler_params=params,
        name="cross",
    )(counts, total, energy, cross_x, cross_y, got_x, got_y, send_x, *shared)
    back_x = shifted(back_x, "gx", 1)
    back_y = shifted(back_y, "gy", 1)
    parts = lax.all_to_all(energy, ("gx", "gy"), 0, 0)
    return pl.pallas_call(
        functools.partial(join_kernel, atoms * devices),
        out_shape=(shape((1,), F32), shape(positions.shape, F32), shape(features.shape, F32)),
        in_specs=[vmem] * 4,
        out_specs=[smem, vmem, vmem],
        compiler_params=params,
        name="join",
    )(total, back_x, back_y, parts)


def solution(mesh):
    spread = P(None, ("gx", "gy"))
    return jax.shard_map(
        on_device,
        mesh=mesh,
        in_specs=(spread,) * 6 + (P(("gx", "gy"), None),) + (P(),) * 8,
        out_specs=(P(), spread, spread),
        check_vma=False,
    )
```

```python
import functools
import math

import jax
import jax.numpy as jnp
from jax import lax
from jax.experimental import pallas as pl
from jax.experimental.pallas import tpu as pltpu
from jax.sharding import PartitionSpec as P

BLOCK = 1024
STREAMS = 4
OFFSETS = (0, 0, 0, 0)
GROUPS = 4
LENT_ROWS = 16
JOIN_PARTS = 4

cutoff_radius = 6.0
block_edge = 6.0
softening = 0.1

F32 = jnp.float32
BF16 = jnp.bfloat16


def shifted(array, axis, by):
    length = lax.axis_size(axis)
    return lax.ppermute(array, axis, [(i, (i + by) % length) for i in range(length)])


def sin_cos_pi(x):
    near = jnp.floor(x + 0.5)
    y = (x - near) * math.pi
    odd = near - 2.0 * jnp.floor(near * 0.5)
    sign = 1.0 - 2.0 * odd
    z = y * y
    s = z * (-1.0 / 39916800) + 1.0 / 362880
    s = s * z - 1.0 / 5040
    s = s * z + 1.0 / 120
    s = s * z - 1.0 / 6
    s = s * z + 1.0
    c = z * (1.0 / 479001600) - 1.0 / 3628800
    c = c * z + 1.0 / 40320
    c = c * z - 1.0 / 720
    c = c * z + 1.0 / 24
    c = c * z - 0.5
    c = c * z + 1.0
    return sign * (s * y), sign * c


def group_of(index, size, groups):
    group = jnp.zeros_like(index)
    for g in range(1, groups):
        group = group + (index >= g * size).astype(jnp.int32)
    return group, index - group * size


def pick_group(stack, group, height, groups, base=0):
    out = stack[base + (groups - 1) * height : base + groups * height]
    for g in range(groups - 2, -1, -1):
        out = jnp.where(group == g, stack[base + g * height : base + (g + 1) * height], out)
    return out


def pick_rows(table, spots):
    chunk = spots >> 7
    lane = spots & 127
    best = jnp.zeros((8, 128), F32)
    for j in range(table.shape[1] // 128):
        found = jnp.take_along_axis(
            table[:, j * 128 : (j + 1) * 128], lane, axis=1, mode="promise_in_bounds"
        )
        best = jnp.where(chunk == j, found, best)
    return best


def pick_lanes(table, index, other):
    upper = lax.broadcasted_iota(jnp.int32, (8, 128), 0) >= 4
    return jnp.concatenate(
        [
            pick_rows(table, jnp.where(upper, other[:, c : c + 128], index[:, c : c + 128]))
            for c in range(0, index.shape[1], 128)
        ],
        axis=1,
    )


def one_hot(row, size):
    spots = lax.broadcasted_iota(jnp.int16, (size, row.shape[1]), 0)
    hit = spots == row.astype(jnp.int16)
    return jnp.where(hit, jnp.ones((), BF16), jnp.zeros((), BF16))


def prep_kernel(*refs):
    sources, refs = refs[:13], refs[13:]
    (send_x, send_y, places, fwd_in, fwd_hid, bwd_hid, bwd_in, readout, pairs, counts), refs = (
        refs[:10],
        refs[10:],
    )
    targets, (wide, sems) = refs[:11], refs[11:]
    copies = [
        pltpu.make_async_copy(src, dst, sems.at[k])
        for k, (src, dst) in enumerate(zip(sources, targets + (pairs, counts)))
    ]
    for copy in copies:
        copy.start()
    for copy in copies[:3]:
        copy.wait()
    feat, pos, lists, w_rbf, w_src, w_dst, sp_src, sp_dst, w_hid, w_lat, w_en = targets
    width = feat.shape[0]
    size = send_x.shape[1]
    base = GROUPS * width
    tall = base + 8 * GROUPS
    p = pos[...]
    high = p.astype(BF16).astype(F32)
    low = p - high
    places[...] = jnp.zeros_like(places)
    places[0:3, :] = p
    places[4:7, :] = p
    wide[...] = jnp.zeros_like(wide)
    for g in range(GROUPS):
        span = slice(g * size, (g + 1) * size)
        rows = slice(g * width, (g + 1) * width)
        part = feat[:, span]
        send_x[rows, :] = part
        send_y[rows, :] = part
        wide[8 * g : 8 * g + 3, :] = high[:, span]
        wide[8 * g + 3 : 8 * g + 6, :] = low[:, span]
    part = wide[...].astype(BF16)
    send_x[base:tall, :] = part
    send_y[base:tall, :] = part
    for axis, send in enumerate((send_x, send_y)):
        wide[...] = jnp.zeros_like(wide)
        for g in range(lists.shape[1] // size):
            ids = lists[axis : axis + 1, g * size : (g + 1) * size]
            wide[2 * g : 2 * g + 1, :] = (ids >> 6).astype(F32)
            wide[2 * g + 1 : 2 * g + 2, :] = (ids & 63).astype(F32)
        send[tall:, :] = wide[0:LENT_ROWS, :].astype(BF16)
    for copy in copies[3:]:
        copy.wait()
    full = jnp.concatenate(
        [ref[...].astype(F32) for ref in (w_src, w_dst, w_rbf)]
        + [jnp.concatenate([sp_src[...].astype(F32), sp_dst[...].astype(F32)], axis=0)],
        axis=0,
    )
    bwd_in[...] = full.astype(BF16)
    fwd_in[...] = (0.5 * full.T).astype(BF16)
    hid = w_hid[...].astype(F32)
    fwd_hid[...] = (0.5 * hid.T).astype(BF16)
    column = jnp.sum(w_lat[...].astype(F32).T * w_en[...].reshape(1, -1), axis=1, keepdims=True)
    line = jnp.broadcast_to(column, (column.shape[0], 128)).T[0:8, :]
    high = line.astype(BF16).astype(F32)
    first_row = lax.broadcasted_iota(jnp.int32, line.shape, 0) == 0
    both = jnp.where(first_row, high, line - high)
    readout[...] = jnp.concatenate([both, jnp.zeros_like(both)], axis=0).astype(BF16)
    bwd_hid[...] = (hid * line[0:1, :]).astype(BF16)


def half_block(
    indices, begin, count, offset, tables, weights, scratch, energy, dims
):
    width, nrbf, nspec = dims
    fwd_in, fwd_hid, bwd_hid, bwd_in, readout = weights
    hots, grads, inputs, place = scratch
    src, dst, kind_src, kind_dst = indices
    tab_src, tab_dst, places = tables
    size = tab_src.shape[1]
    lanes = src.shape[1]
    here = slice(place * lanes, (place + 1) * lanes)
    there = slice(BLOCK + place * lanes, BLOCK + (place + 1) * lanes)
    base = GROUPS * width
    grp_src, row_src = group_of(src, size, GROUPS)
    grp_dst, row_dst = group_of(dst, size, GROUPS)
    hots[:, here] = one_hot(row_src, size)
    hots[:, there] = one_hot(row_dst, size)
    yield
    got_src = jnp.dot(tab_src[0:base, :], hots[:, here], preferred_element_type=F32)
    got_dst = jnp.dot(tab_dst[0:base, :], hots[:, there], preferred_element_type=F32)
    inputs[0:width, :] = pick_group(got_src, grp_src, width, GROUPS).astype(BF16)
    inputs[width : 2 * width, :] = pick_group(got_dst, grp_dst, width, GROUPS).astype(BF16)
    sub = lax.broadcasted_iota(jnp.int32, (8, lanes), 0)
    gap = pick_lanes(places, src, dst)
    gap = pltpu.roll(gap, 4, 0) - gap
    if offset is not None:
        gap = gap + jnp.where(sub == offset, block_edge, 0.0)
    gap = jnp.where(sub < 3, gap, 0.0)
    radius = jnp.sqrt(jnp.sum(gap * gap, axis=0, keepdims=True) + softening)
    inverse = 1.0 / radius
    ratio = jnp.minimum(radius * (1.0 / cutoff_radius), 1.0)
    inside = 1.0 - ratio * ratio
    slots = begin + lax.broadcasted_iota(jnp.int32, (1, lanes), 1)
    live = jnp.where(slots < count, 1.0, 0.0)
    weight = inside * inside * live
    orders = (sub + 1).astype(F32)
    sines, cosines = sin_cos_pi(orders * ratio)
    basis = sines * inverse
    slope = (orders * (math.pi / cutoff_radius) * cosines - basis) * inverse
    kinds = jnp.where(sub < nspec, kind_src, kind_dst + nspec)
    inputs[2 * width :, :] = jnp.concatenate(
        [basis, jnp.where(sub == kinds, 1.0, 0.0)], axis=0
    ).astype(BF16)
    yield
    half = jnp.dot(fwd_in[...], inputs[...], preferred_element_type=F32)
    tan = jnp.tanh(half)
    up = 1.0 + tan
    hidden = half * up
    slope_one = up + hidden * (1.0 - tan)
    hidden = hidden.astype(BF16)
    yield
    half = jnp.dot(fwd_hid[...], hidden, preferred_element_type=F32)
    up = (1.0 + jnp.tanh(half)).astype(BF16)
    second = half.astype(BF16) * up
    slope_two = up + second * (2.0 - up)
    yield
    score = jnp.dot(readout[...], second, preferred_element_type=F32)
    score = score[0:1] + score[1:2]
    energy[...] += weight * score
    back = jnp.dot(bwd_hid[...], slope_two, preferred_element_type=F32)
    back = (back * slope_one).astype(BF16)
    yield
    back = jnp.dot(bwd_in[...], back, preferred_element_type=F32)
    scale = 0.25 * weight
    radial = scale * jnp.sum(back[2 * width : 2 * width + nrbf] * slope, axis=0, keepdims=True)
    radial = radial - (4.0 / cutoff_radius) * (inside * ratio * live) * score
    push = gap * (radial * inverse)
    for span, group, part, move in (
        (here, grp_src, back[0:width] * scale, -push),
        (there, grp_dst, back[width : 2 * width] * scale, push),
    ):
        part = part.astype(BF16)
        masks = [jnp.where(group == g, 1.0, 0.0) for g in range(GROUPS)]
        for g, mask in enumerate(masks):
            grads[g * width : (g + 1) * width, span] = part * mask.astype(BF16)
        other = pltpu.roll(move, 4, 0)
        grads[base:, span] = jnp.concatenate(
            [move * masks[g] + other * masks[g + 1] for g in range(0, GROUPS, 2)], axis=0
        ).astype(BF16)
    yield


def scatter(totals, scratch):
    hots, grads = scratch
    total_src, total_dst = totals
    spans = [(total_src, slice(0, 2 * BLOCK))]
    if total_dst is not total_src:
        spans = [(total_src, slice(0, BLOCK)), (total_dst, slice(BLOCK, 2 * BLOCK))]
    for total, span in spans:
        total[...] += lax.dot_general(
            grads[:, span], hots[:, span], (((1,), (1,)), ((), ())), preferred_element_type=F32
        )


def pair_loop(filled, pairs, count, offset, tables, weights, scratch, energy, dims, totals):
    hots, grads, *inputs = scratch
    lanes = BLOCK // STREAMS

    def visit(index, carry):
        halves = []
        for k in range(STREAMS):
            begin = index * BLOCK + k * lanes
            halves.append(
                half_block(
                    rows_of(pairs, begin, lanes),
                    begin,
                    count,
                    offset,
                    tables,
                    weights,
                    (hots, grads, inputs[k], k),
                    energy,
                    dims,
                )
            )
        for tick in range(6 + max(OFFSETS)):
            for half, late in zip(halves, OFFSETS):
                if 0 <= tick - late < 6:
                    next(half)
        scatter(totals, (hots, grads))
        return carry

    lax.fori_loop(0, filled, visit, 0)


def rows_of(pairs, begin, lanes):
    span = pl.ds(pl.multiple_of(begin, lanes), lanes)
    return [pairs[k : k + 1, span] for k in range(4)]


def units(count):
    return (count + BLOCK - 1) // BLOCK


def local_kernel(dims, counts, pairs, table, places, *refs):
    weights = refs[:5]
    total, energy, *scratch, runs = refs[5:]
    total[...] = jnp.zeros_like(total)
    runs[...] = jnp.zeros_like(runs)
    count = counts[0, 0]
    pair_loop(
        units(count),
        pairs,
        count,
        None,
        (table, table, places),
        weights,
        scratch,
        runs,
        dims,
        (total, total),
    )
    fold_energy(energy, runs, None)


def fold_energy(energy, runs, energy_in):
    part = jnp.sum(runs[...], axis=1, keepdims=True)
    part = jnp.broadcast_to(part, energy.shape[-2:])
    if energy_in is not None:
        part = part + energy_in[...]
    energy[...] = jnp.broadcast_to(part, energy.shape)


def cross_kernel(
    dims, counts, _, energy_in, pairs_x, pairs_y, got_x, got_y, table, places, *refs
):
    weights = refs[:5]
    total, energy, back_x, back_y = refs[5:9]
    *scratch, runs, away, far, lent, other, pairs = refs[9:]
    base = GROUPS * dims[0]
    size = table.shape[1]
    runs[...] = jnp.zeros_like(runs)
    far[...] = places[...]

    def visit(axis, carry):
        for k, (got, listed) in enumerate(((got_x, pairs_x), (got_y, pairs_y))):

            @pl.when(axis == k)
            def _():
                other[...] = got[...]
                pairs[...] = listed[...]

        away[...] = jnp.zeros_like(away)
        extra = other[base:, :].astype(F32)
        for g in range(GROUPS):
            span = slice(g * size, (g + 1) * size)
            far[4:7, span] = extra[8 * g : 8 * g + 3] + extra[8 * g + 3 : 8 * g + 6]
        extra = extra[8 * GROUPS :]
        for g in range(lent.shape[1] // size):
            ids = extra[2 * g : 2 * g + 1] * 64.0 + extra[2 * g + 1 : 2 * g + 2]
            lent[:, g * size : (g + 1) * size] = jnp.broadcast_to(ids, (8, size))
        for start in range(0, pairs.shape[1], 1024):
            spans = [slice(start + 128 * k, start + 128 * (k + 1)) for k in range(8)]
            slots = jnp.concatenate([pairs[1:2, span] for span in spans], axis=0)
            ids = pick_rows(lent, slots).astype(jnp.int32)
            for k, span in enumerate(spans):
                pairs[1:2, span] = ids[k : k + 1]
        count = counts[0, 1 + axis]
        pair_loop(
            units(count),
            pairs,
            count,
            axis,
            (table, other, far),
            weights,
            scratch,
            runs,
            dims,
            (total, away),
        )
        for k, back in enumerate((back_x, back_y)):

            @pl.when(axis == k)
            def _():
                back[...] = away[...].astype(BF16)

        return carry

    lax.fori_loop(0, 2, visit, 0)
    fold_energy(energy, runs, energy_in)


def join_kernel(
    atoms, total, back_x, back_y, parts, energy, forces_out, grads_out, forces, grads, sems
):
    width = grads.shape[0]
    size = total.shape[1]
    base = GROUPS * width
    step = width // JOIN_PARTS
    copies = []
    for part in range(JOIN_PARTS):
        for g in range(GROUPS):
            rows = slice(g * width + part * step, g * width + (part + 1) * step)
            grads[part * step : (part + 1) * step, g * size : (g + 1) * size] = total[rows] + (
                back_x[rows].astype(F32) + back_y[rows].astype(F32)
            )
        here = pl.ds(part * step, step)
        copies.append(
            pltpu.make_async_copy(grads.at[here, :], grads_out.at[here, :], sems.at[part])
        )
        copies[-1].start()
    moved = total[base:] + (back_x[base:].astype(F32) + back_y[base:].astype(F32))
    for g in range(GROUPS):
        forces[:, g * size : (g + 1) * size] = -moved[4 * g : 4 * g + 3]
    copies.append(pltpu.make_async_copy(forces, forces_out, sems.at[JOIN_PARTS]))
    copies[-1].start()
    energy[0] = jnp.sum(parts[:, 0:1, 0:1]) / atoms
    for copy in copies:
        copy.wait()


vmem = pl.BlockSpec(memory_space=pltpu.VMEM)
smem = pl.BlockSpec(memory_space=pltpu.SMEM)
hbm = pl.BlockSpec(memory_space=pltpu.MemorySpace.HBM)
shape = jax.ShapeDtypeStruct
params = pltpu.CompilerParams(vmem_limit_bytes=48 * 1024 * 1024)


def in_hbm(array):
    return pltpu.with_memory_space_constraint(array, pltpu.MemorySpace.HBM)


def like(*arrays):
    return [pltpu.VMEM(item.shape, item.dtype) for item in arrays]


def scratch_of(total, depth):
    tall, size = total.shape
    lanes = BLOCK // STREAMS
    return (
        [pltpu.VMEM((size, 2 * BLOCK), BF16), pltpu.VMEM((tall, 2 * BLOCK), BF16)]
        + [pltpu.VMEM((depth, lanes), BF16)] * STREAMS
        + [pltpu.VMEM((1, lanes), F32)]
    )


def prep_call(features, positions, halo_lists, local_pairs, counts, *weights):
    width, atoms = features.shape
    size = atoms // GROUPS
    nrbf, hid = weights[0].shape
    depth = 2 * width + nrbf + 2 * weights[3].shape[0]
    packed = shape((GROUPS * (width + 8) + LENT_ROWS, size), BF16)
    *front, w_latent, w_energy = weights
    inputs = (features, positions, halo_lists, *front, w_latent.T, w_energy)
    return pl.pallas_call(
        prep_kernel,
        out_shape=(
            packed,
            packed,
            shape((8, atoms), F32),
            shape((hid, depth), BF16),
            shape((hid, hid), BF16),
            shape((hid, hid), BF16),
            shape((depth, hid), BF16),
            shape((16, hid), BF16),
            shape(local_pairs.shape, local_pairs.dtype),
            shape(counts.shape, counts.dtype),
        ),
        in_specs=[hbm] * 13,
        out_specs=[vmem] * 9 + [smem],
        scratch_shapes=like(*inputs)
        + [pltpu.VMEM((GROUPS * 8, size), F32), pltpu.SemaphoreType.DMA((13,))],
        compiler_params=params,
        name="prep",
    )(*[in_hbm(item) for item in inputs + (local_pairs, counts)])


def local_call(dims, counts, pairs, table, places, *weights):
    depth, _ = weights[3].shape
    total_like = shape((GROUPS * (dims[0] + 4), table.shape[1]), F32)
    return pl.pallas_call(
        functools.partial(local_kernel, dims),
        out_shape=(total_like, shape((1, 128), F32)),
        in_specs=[smem] + [vmem] * 8,
        out_specs=[vmem] * 2,
        scratch_shapes=scratch_of(total_like, depth),
        compiler_params=params,
        name="local",
    )(counts, pairs, table, places, *weights)


def on_device(
    positions,
    features,
    halo_lists,
    local_pairs,
    cross_x,
    cross_y,
    pair_counts,
    w_rbf,
    w_src,
    w_dst,
    species_src,
    species_dst,
    w_hidden,
    w_latent,
    w_energy,
):
    atoms = positions.shape[1]
    width = features.shape[0]
    nrbf, hid = w_rbf.shape
    nspec = species_src.shape[0]
    size = atoms // GROUPS
    tall = GROUPS * (width + 4)
    depth = 2 * width + nrbf + 2 * nspec
    dims = (width, nrbf, nspec)
    devices = lax.axis_size("gx") * lax.axis_size("gy")
    send_x, send_y, *shared, pairs, counts = prep_call(
        features,
        positions,
        halo_lists,
        local_pairs,
        pair_counts,
        w_rbf,
        w_src,
        w_dst,
        species_src,
        species_dst,
        w_hidden,
        w_latent,
        w_energy,
    )
    got_x = shifted(send_x, "gx", -1)
    got_y = shifted(send_y, "gy", -1)
    total, energy = local_call(dims, counts, pairs, send_x, *shared)
    total_like = shape(total.shape, F32)
    back_like = shape(total.shape, BF16)
    scratch = scratch_of(total, depth)
    total, energy, back_x, back_y = pl.pallas_call(
        functools.partial(cross_kernel, dims),
        out_shape=(total_like, shape((devices, 1, 128), F32), back_like, back_like),
        in_specs=[smem] + [vmem] * 13,
        out_specs=[vmem] * 4,
        scratch_shapes=scratch
        + [
            pltpu.VMEM((tall, size), F32),
            pltpu.VMEM((8, atoms), F32),
            pltpu.VMEM((8, halo_lists.shape[1]), F32),
        ]
        + like(got_x, cross_x),
        input_output_aliases={1: 0},
        compiler_params=params,
        name="cross",
    )(counts, total, energy, cross_x, cross_y, got_x, got_y, send_x, *shared)
    back_x = shifted(back_x, "gx", 1)
    back_y = shifted(back_y, "gy", 1)
    parts = lax.all_to_all(energy, ("gx", "gy"), 0, 0)
    return pl.pallas_call(
        functools.partial(join_kernel, atoms * devices),
        out_shape=(shape((1,), F32), shape(positions.shape, F32), shape(features.shape, F32)),
        in_specs=[vmem] * 4,
        out_specs=[smem, hbm, hbm],
        scratch_shapes=[
            pltpu.VMEM(positions.shape, F32),
            pltpu.VMEM(features.shape, F32),
            pltpu.SemaphoreType.DMA((JOIN_PARTS + 1,)),
        ],
        compiler_params=params,
        name="join",
    )(total, back_x, back_y, parts)


def solution(mesh):
    spread = P(None, ("gx", "gy"))
    return jax.shard_map(
        on_device,
        mesh=mesh,
        in_specs=(spread,) * 6 + (P(("gx", "gy"), None),) + (P(),) * 8,
        out_specs=(P(), spread, spread),
        check_vma=False,
    )
```

```python
import functools
import math

import jax
import jax.numpy as jnp
from jax import lax
from jax.experimental import pallas as pl
from jax.experimental.pallas import tpu as pltpu
from jax.sharding import PartitionSpec as P

BLOCK = 1024
STREAMS = 4
OFFSETS = (0, 0, 0, 0)
GROUPS = 4
LENT_ROWS = 16

cutoff_radius = 6.0
block_edge = 6.0
softening = 0.1

F32 = jnp.float32
BF16 = jnp.bfloat16


def shifted(array, axis, by):
    length = lax.axis_size(axis)
    return lax.ppermute(array, axis, [(i, (i + by) % length) for i in range(length)])


def sin_cos_pi(x):
    near = jnp.floor(x + 0.5)
    y = (x - near) * math.pi
    odd = near - 2.0 * jnp.floor(near * 0.5)
    sign = 1.0 - 2.0 * odd
    z = y * y
    s = z * (-1.0 / 39916800) + 1.0 / 362880
    s = s * z - 1.0 / 5040
    s = s * z + 1.0 / 120
    s = s * z - 1.0 / 6
    s = s * z + 1.0
    c = z * (1.0 / 479001600) - 1.0 / 3628800
    c = c * z + 1.0 / 40320
    c = c * z - 1.0 / 720
    c = c * z + 1.0 / 24
    c = c * z - 0.5
    c = c * z + 1.0
    return sign * (s * y), sign * c


def group_of(index, size, groups):
    group = jnp.zeros_like(index)
    for g in range(1, groups):
        group = group + (index >= g * size).astype(jnp.int32)
    return group, index - group * size


def pick_group(stack, group, height, groups, base=0):
    out = stack[base + (groups - 1) * height : base + groups * height]
    for g in range(groups - 2, -1, -1):
        out = jnp.where(group == g, stack[base + g * height : base + (g + 1) * height], out)
    return out


def pick_lanes(table, index, other):
    out = []
    upper = lax.broadcasted_iota(jnp.int32, (8, 128), 0) >= 4
    for c in range(0, index.shape[1], 128):
        spots = jnp.where(upper, other[:, c : c + 128], index[:, c : c + 128])
        chunk = spots >> 7
        lane = spots & 127
        best = jnp.zeros((8, 128), F32)
        for j in range(table.shape[1] // 128):
            found = jnp.take_along_axis(
                table[:, j * 128 : (j + 1) * 128], lane, axis=1, mode="promise_in_bounds"
            )
            best = jnp.where(chunk == j, found, best)
        out.append(best)
    return jnp.concatenate(out, axis=1)


def one_hot(row, size):
    spots = lax.broadcasted_iota(jnp.int16, (size, row.shape[1]), 0)
    hit = spots == row.astype(jnp.int16)
    return jnp.where(hit, jnp.ones((), BF16), jnp.zeros((), BF16))


def prep_kernel(*refs):
    sources, refs = refs[:13], refs[13:]
    (send_x, send_y, places, fwd_in, fwd_hid, bwd_hid, bwd_in, readout, pairs, counts), refs = (
        refs[:10],
        refs[10:],
    )
    targets, (wide, sems) = refs[:11], refs[11:]
    copies = [
        pltpu.make_async_copy(src, dst, sems.at[k])
        for k, (src, dst) in enumerate(zip(sources, targets + (pairs, counts)))
    ]
    for copy in copies:
        copy.start()
    for copy in copies[:3]:
        copy.wait()
    feat, pos, lists, w_rbf, w_src, w_dst, sp_src, sp_dst, w_hid, w_lat, w_en = targets
    width = feat.shape[0]
    size = send_x.shape[1]
    base = GROUPS * width
    tall = base + 8 * GROUPS
    p = pos[...]
    high = p.astype(BF16).astype(F32)
    low = p - high
    places[...] = jnp.zeros_like(places)
    places[0:3, :] = p
    places[4:7, :] = p
    wide[...] = jnp.zeros_like(wide)
    for g in range(GROUPS):
        span = slice(g * size, (g + 1) * size)
        rows = slice(g * width, (g + 1) * width)
        part = feat[:, span]
        send_x[rows, :] = part
        send_y[rows, :] = part
        wide[8 * g : 8 * g + 3, :] = high[:, span]
        wide[8 * g + 3 : 8 * g + 6, :] = low[:, span]
    part = wide[...].astype(BF16)
    send_x[base:tall, :] = part
    send_y[base:tall, :] = part
    for axis, send in enumerate((send_x, send_y)):
        wide[...] = jnp.zeros_like(wide)
        for g in range(lists.shape[1] // size):
            ids = lists[axis : axis + 1, g * size : (g + 1) * size]
            wide[2 * g : 2 * g + 1, :] = (ids >> 6).astype(F32)
            wide[2 * g + 1 : 2 * g + 2, :] = (ids & 63).astype(F32)
        send[tall:, :] = wide[0:LENT_ROWS, :].astype(BF16)
    for copy in copies[3:]:
        copy.wait()
    full = jnp.concatenate(
        [ref[...].astype(F32) for ref in (w_src, w_dst, w_rbf)]
        + [jnp.concatenate([sp_src[...].astype(F32), sp_dst[...].astype(F32)], axis=0)],
        axis=0,
    )
    bwd_in[...] = full.astype(BF16)
    fwd_in[...] = (0.5 * full.T).astype(BF16)
    hid = w_hid[...].astype(F32)
    fwd_hid[...] = (0.5 * hid.T).astype(BF16)
    column = jnp.sum(w_lat[...].astype(F32).T * w_en[...].reshape(1, -1), axis=1, keepdims=True)
    line = jnp.broadcast_to(column, (column.shape[0], 128)).T[0:8, :]
    high = line.astype(BF16).astype(F32)
    first_row = lax.broadcasted_iota(jnp.int32, line.shape, 0) == 0
    both = jnp.where(first_row, high, line - high)
    readout[...] = jnp.concatenate([both, jnp.zeros_like(both)], axis=0).astype(BF16)
    bwd_hid[...] = (hid * line[0:1, :]).astype(BF16)


def half_block(
    indices, begin, count, offset, tables, weights, scratch, energy, dims, lookup
):
    width, nrbf, nspec = dims
    fwd_in, fwd_hid, bwd_hid, bwd_in, readout = weights
    hots, grads, inputs, place = scratch
    src, dst, kind_src, kind_dst = indices
    tab_src, tab_dst, places = tables
    size = tab_src.shape[1]
    lanes = src.shape[1]
    here = slice(place * lanes, (place + 1) * lanes)
    there = slice(BLOCK + place * lanes, BLOCK + (place + 1) * lanes)
    base = GROUPS * width
    if lookup is not None:
        dst = pick_lanes(lookup, dst, dst)[0:1].astype(jnp.int32)
    grp_src, row_src = group_of(src, size, GROUPS)
    grp_dst, row_dst = group_of(dst, size, GROUPS)
    hots[:, here] = one_hot(row_src, size)
    hots[:, there] = one_hot(row_dst, size)
    yield
    got_src = jnp.dot(tab_src[0:base, :], hots[:, here], preferred_element_type=F32)
    got_dst = jnp.dot(tab_dst[0:base, :], hots[:, there], preferred_element_type=F32)
    inputs[0:width, :] = pick_group(got_src, grp_src, width, GROUPS).astype(BF16)
    inputs[width : 2 * width, :] = pick_group(got_dst, grp_dst, width, GROUPS).astype(BF16)
    sub = lax.broadcasted_iota(jnp.int32, (8, lanes), 0)
    gap = pick_lanes(places, src, dst)
    gap = pltpu.roll(gap, 4, 0) - gap
    if offset is not None:
        gap = gap + jnp.where(sub == offset, block_edge, 0.0)
    gap = jnp.where(sub < 3, gap, 0.0)
    radius = jnp.sqrt(jnp.sum(gap * gap, axis=0, keepdims=True) + softening)
    inverse = 1.0 / radius
    ratio = jnp.minimum(radius * (1.0 / cutoff_radius), 1.0)
    inside = 1.0 - ratio * ratio
    slots = begin + lax.broadcasted_iota(jnp.int32, (1, lanes), 1)
    live = jnp.where(slots < count, 1.0, 0.0)
    weight = inside * inside * live
    orders = (sub + 1).astype(F32)
    sines, cosines = sin_cos_pi(orders * ratio)
    basis = sines * inverse
    slope = (orders * (math.pi / cutoff_radius) * cosines - basis) * inverse
    kinds = jnp.where(sub < nspec, kind_src, kind_dst + nspec)
    inputs[2 * width :, :] = jnp.concatenate(
        [basis, jnp.where(sub == kinds, 1.0, 0.0)], axis=0
    ).astype(BF16)
    yield
    half = jnp.dot(fwd_in[...], inputs[...], preferred_element_type=F32)
    up = (1.0 + jnp.tanh(half)).astype(BF16)
    hidden = half.astype(BF16) * up
    slope_one = up + hidden * (2.0 - up)
    yield
    half = jnp.dot(fwd_hid[...], hidden, preferred_element_type=F32)
    up = (1.0 + jnp.tanh(half)).astype(BF16)
    second = half.astype(BF16) * up
    slope_two = up + second * (2.0 - up)
    yield
    score = jnp.dot(readout[...], second, preferred_element_type=F32)
    score = score[0:1] + score[1:2]
    energy[...] += weight * score
    back = jnp.dot(bwd_hid[...], slope_two, preferred_element_type=F32)
    back = back.astype(BF16) * slope_one
    yield
    back = jnp.dot(bwd_in[...], back, preferred_element_type=F32)
    scale = 0.25 * weight
    radial = scale * jnp.sum(back[2 * width : 2 * width + nrbf] * slope, axis=0, keepdims=True)
    radial = radial - (4.0 / cutoff_radius) * (inside * ratio * live) * score
    push = gap * (radial * inverse)
    for span, group, part, move in (
        (here, grp_src, back[0:width] * scale, -push),
        (there, grp_dst, back[width : 2 * width] * scale, push),
    ):
        part = part.astype(BF16)
        masks = [jnp.where(group == g, 1.0, 0.0) for g in range(GROUPS)]
        for g, mask in enumerate(masks):
            grads[g * width : (g + 1) * width, span] = part * mask.astype(BF16)
        other = pltpu.roll(move, 4, 0)
        grads[base:, span] = jnp.concatenate(
            [move * masks[g] + other * masks[g + 1] for g in range(0, GROUPS, 2)], axis=0
        ).astype(BF16)
    yield


def scatter(totals, scratch):
    hots, grads = scratch
    total_src, total_dst = totals
    spans = [(total_src, slice(0, 2 * BLOCK))]
    if total_dst is not total_src:
        spans = [(total_src, slice(0, BLOCK)), (total_dst, slice(BLOCK, 2 * BLOCK))]
    for total, span in spans:
        total[...] += lax.dot_general(
            grads[:, span], hots[:, span], (((1,), (1,)), ((), ())), preferred_element_type=F32
        )


def pair_loop(filled, pairs, count, offset, tables, weights, scratch, energy, dims, totals, lookup):
    hots, grads, *inputs = scratch
    lanes = BLOCK // STREAMS

    def visit(index, carry):
        halves = []
        for k in range(STREAMS):
            begin = index * BLOCK + k * lanes
            halves.append(
                half_block(
                    rows_of(pairs, begin, lanes),
                    begin,
                    count,
                    offset,
                    tables,
                    weights,
                    (hots, grads, inputs[k], k),
                    energy,
                    dims,
                    lookup,
                )
            )
        for tick in range(6 + max(OFFSETS)):
            for half, late in zip(halves, OFFSETS):
                if 0 <= tick - late < 6:
                    next(half)
        scatter(totals, (hots, grads))
        return carry

    lax.fori_loop(0, filled, visit, 0)


def rows_of(pairs, begin, lanes):
    span = pl.ds(pl.multiple_of(begin, lanes), lanes)
    return [pairs[k : k + 1, span] for k in range(4)]


def units(count):
    return (count + BLOCK - 1) // BLOCK


def local_kernel(dims, counts, pairs, table, places, *refs):
    weights = refs[:5]
    total, energy, *scratch, runs = refs[5:]
    total[...] = jnp.zeros_like(total)
    runs[...] = jnp.zeros_like(runs)
    count = counts[0, 0]
    pair_loop(
        units(count),
        pairs,
        count,
        None,
        (table, table, places),
        weights,
        scratch,
        runs,
        dims,
        (total, total),
        None,
    )
    fold_energy(energy, runs, None)


def fold_energy(energy, runs, energy_in):
    part = jnp.sum(runs[...], axis=1, keepdims=True)
    part = jnp.broadcast_to(part, energy.shape[-2:])
    if energy_in is not None:
        part = part + energy_in[...]
    energy[...] = jnp.broadcast_to(part, energy.shape)


def cross_kernel(
    dims, counts, _, energy_in, pairs_x, pairs_y, got_x, got_y, table, places, *refs
):
    weights = refs[:5]
    total, energy, back_x, back_y = refs[5:9]
    *scratch, runs, away, far, lent, other, pairs = refs[9:]
    base = GROUPS * dims[0]
    size = table.shape[1]
    runs[...] = jnp.zeros_like(runs)
    far[...] = places[...]

    def visit(axis, carry):
        for k, (got, listed) in enumerate(((got_x, pairs_x), (got_y, pairs_y))):

            @pl.when(axis == k)
            def _():
                other[...] = got[...]
                pairs[...] = listed[...]

        away[...] = jnp.zeros_like(away)
        extra = other[base:, :].astype(F32)
        for g in range(GROUPS):
            span = slice(g * size, (g + 1) * size)
            far[4:7, span] = extra[8 * g : 8 * g + 3] + extra[8 * g + 3 : 8 * g + 6]
        extra = extra[8 * GROUPS :]
        for g in range(lent.shape[1] // size):
            ids = extra[2 * g : 2 * g + 1] * 64.0 + extra[2 * g + 1 : 2 * g + 2]
            lent[:, g * size : (g + 1) * size] = jnp.broadcast_to(ids, (8, size))
        count = counts[0, 1 + axis]
        pair_loop(
            units(count),
            pairs,
            count,
            axis,
            (table, other, far),
            weights,
            scratch,
            runs,
            dims,
            (total, away),
            lent,
        )
        for k, back in enumerate((back_x, back_y)):

            @pl.when(axis == k)
            def _():
                back[...] = away[...].astype(BF16)

        return carry

    lax.fori_loop(0, 2, visit, 0)
    fold_energy(energy, runs, energy_in)


def join_kernel(atoms, total, back_x, back_y, parts, energy, forces, feature_grads):
    energy[0] = jnp.sum(parts[:, 0:1, 0:1]) / atoms
    width = feature_grads.shape[0]
    size = total.shape[1]
    base = GROUPS * width
    for g in range(GROUPS):
        span = slice(g * size, (g + 1) * size)
        rows = slice(g * width, (g + 1) * width)
        feature_grads[:, span] = total[rows] + (
            back_x[rows].astype(F32) + back_y[rows].astype(F32)
        )
    moved = total[base:] + (back_x[base:].astype(F32) + back_y[base:].astype(F32))
    for g in range(GROUPS):
        forces[:, g * size : (g + 1) * size] = -moved[4 * g : 4 * g + 3]


vmem = pl.BlockSpec(memory_space=pltpu.VMEM)
smem = pl.BlockSpec(memory_space=pltpu.SMEM)
hbm = pl.BlockSpec(memory_space=pltpu.MemorySpace.HBM)
shape = jax.ShapeDtypeStruct
params = pltpu.CompilerParams(vmem_limit_bytes=48 * 1024 * 1024)


def in_hbm(array):
    return pltpu.with_memory_space_constraint(array, pltpu.MemorySpace.HBM)


def like(*arrays):
    return [pltpu.VMEM(item.shape, item.dtype) for item in arrays]


def scratch_of(total, depth):
    tall, size = total.shape
    lanes = BLOCK // STREAMS
    return (
        [pltpu.VMEM((size, 2 * BLOCK), BF16), pltpu.VMEM((tall, 2 * BLOCK), BF16)]
        + [pltpu.VMEM((depth, lanes), BF16)] * STREAMS
        + [pltpu.VMEM((1, lanes), F32)]
    )


def prep_call(features, positions, halo_lists, local_pairs, counts, *weights):
    width, atoms = features.shape
    size = atoms // GROUPS
    nrbf, hid = weights[0].shape
    depth = 2 * width + nrbf + 2 * weights[3].shape[0]
    packed = shape((GROUPS * (width + 8) + LENT_ROWS, size), BF16)
    *front, w_latent, w_energy = weights
    inputs = (features, positions, halo_lists, *front, w_latent.T, w_energy)
    return pl.pallas_call(
        prep_kernel,
        out_shape=(
            packed,
            packed,
            shape((8, atoms), F32),
            shape((hid, depth), BF16),
            shape((hid, hid), BF16),
            shape((hid, hid), BF16),
            shape((depth, hid), BF16),
            shape((16, hid), BF16),
            shape(local_pairs.shape, local_pairs.dtype),
            shape(counts.shape, counts.dtype),
        ),
        in_specs=[hbm] * 13,
        out_specs=[vmem] * 9 + [smem],
        scratch_shapes=like(*inputs)
        + [pltpu.VMEM((GROUPS * 8, size), F32), pltpu.SemaphoreType.DMA((13,))],
        compiler_params=params,
        name="prep",
    )(*[in_hbm(item) for item in inputs + (local_pairs, counts)])


def local_call(dims, counts, pairs, table, places, *weights):
    depth, _ = weights[3].shape
    total_like = shape((GROUPS * (dims[0] + 4), table.shape[1]), F32)
    return pl.pallas_call(
        functools.partial(local_kernel, dims),
        out_shape=(total_like, shape((1, 128), F32)),
        in_specs=[smem] + [vmem] * 8,
        out_specs=[vmem] * 2,
        scratch_shapes=scratch_of(total_like, depth),
        compiler_params=params,
        name="local",
    )(counts, pairs, table, places, *weights)


def on_device(
    positions,
    features,
    halo_lists,
    local_pairs,
    cross_x,
    cross_y,
    pair_counts,
    w_rbf,
    w_src,
    w_dst,
    species_src,
    species_dst,
    w_hidden,
    w_latent,
    w_energy,
):
    atoms = positions.shape[1]
    width = features.shape[0]
    nrbf, hid = w_rbf.shape
    nspec = species_src.shape[0]
    size = atoms // GROUPS
    tall = GROUPS * (width + 4)
    depth = 2 * width + nrbf + 2 * nspec
    dims = (width, nrbf, nspec)
    devices = lax.axis_size("gx") * lax.axis_size("gy")
    send_x, send_y, *shared, pairs, counts = prep_call(
        features,
        positions,
        halo_lists,
        local_pairs,
        pair_counts,
        w_rbf,
        w_src,
        w_dst,
        species_src,
        species_dst,
        w_hidden,
        w_latent,
        w_energy,
    )
    got_x = shifted(send_x, "gx", -1)
    got_y = shifted(send_y, "gy", -1)
    total, energy = local_call(dims, counts, pairs, send_x, *shared)
    total_like = shape(total.shape, F32)
    back_like = shape(total.shape, BF16)
    scratch = scratch_of(total, depth)
    total, energy, back_x, back_y = pl.pallas_call(
        functools.partial(cross_kernel, dims),
        out_shape=(total_like, shape((devices, 1, 128), F32), back_like, back_like),
        in_specs=[smem] + [vmem] * 13,
        out_specs=[vmem] * 4,
        scratch_shapes=scratch
        + [
            pltpu.VMEM((tall, size), F32),
            pltpu.VMEM((8, atoms), F32),
            pltpu.VMEM((8, halo_lists.shape[1]), F32),
        ]
        + like(got_x, cross_x),
        input_output_aliases={1: 0},
        compiler_params=params,
        name="cross",
    )(counts, total, energy, cross_x, cross_y, got_x, got_y, send_x, *shared)
    back_x = shifted(back_x, "gx", 1)
    back_y = shifted(back_y, "gy", 1)
    parts = lax.all_to_all(energy, ("gx", "gy"), 0, 0)
    return pl.pallas_call(
        functools.partial(join_kernel, atoms * devices),
        out_shape=(shape((1,), F32), shape(positions.shape, F32), shape(features.shape, F32)),
        in_specs=[vmem] * 4,
        out_specs=[smem, vmem, vmem],
        compiler_params=params,
        name="join",
    )(total, back_x, back_y, parts)


def solution(mesh):
    spread = P(None, ("gx", "gy"))
    return jax.shard_map(
        on_device,
        mesh=mesh,
        in_specs=(spread,) * 6 + (P(("gx", "gy"), None),) + (P(),) * 8,
        out_specs=(P(), spread, spread),
        check_vma=False,
    )
```
